32 devices in a mesh: ctx: 2 (over core), section: 4 (over y, x), dp: 4 (over z).
Axes of the slice: x: 2, y: 2, z: 4, core: 2. Of those that a mesh axis runs over, the one named last changes fastest.
Arguments:
- conv_input: bfloat16 [4, 4, 256, 5120], P('section', 'dp', 'ctx'), may hold values from -6 to 6
- gate_input: bfloat16 [4, 4, 256, 1024], P('section', 'dp', 'ctx'), may hold values from -6 to 6
- step_input: bfloat16 [4, 4, 256, 16], P('section', 'dp', 'ctx'), may hold values from -7 to 3
- cotangent: bfloat16 [4, 4, 256, 1024], P('section', 'dp', 'ctx'), may hold values from -6 to 6
- conv_weight: float32 [4, 4, 5120], P('section'), may hold values from -3 to 3
- conv_bias: float32 [4, 5120], P('section'), may hold values from -0.5 to 0.5
- step_bias: float32 [4, 16], P('section'), may hold values from -0.5 to 0.5
- decay_log: float32 [4, 16], P('section'), may hold values from -6 to 0.3
- skip_gain: float32 [4, 16], P('section'), may hold values from 0.5 to 1.5
- norm_gain: float32 [4, 1024], P('section'), may hold values from 0.5 to 1.5
Outputs:
- next_input: bfloat16 [4, 4, 256, 1024], P('section', 'dp', 'ctx')
- grad_conv_input: bfloat16 [4, 4, 256, 5120], P('section', 'dp', 'ctx')
- grad_gate_input: bfloat16 [4, 4, 256, 1024], P('section', 'dp', 'ctx')
- grad_step_input: bfloat16 [4, 4, 256, 16], P('section', 'dp', 'ctx')
- kernel_filter_derivative: float32 [4, 4, 5120], P('section')
- grad_conv_bias: float32 [4, 5120], P('section')
- grad_step_bias: float32 [4, 16], P('section')
- grad_decay_log: float32 [4, 16], P('section')
- grad_skip_gain: float32 [4, 16], P('section')
- grad_norm_gain: float32 [4, 1024], P('section')
The draws below stay inside these ranges and needn't reach their ends.
All inputs are finite; a program needn't handle non-finite values.
Results may differ from the reference program's by a relative error of at most 0.0026.
Values may be sent and summed in bfloat16 or wider, within the bound.
A program may use at most 128 MiB of HBM per device.

```python
import math
import jax
import jax.numpy as jnp
from jax import lax

HEADS = 16
HEAD_DIM = 64
STATE = 256
GROUPS = 8
CONV = 4
TOK_DEV = 128
DI = 1024
CH = 5120
SEQ = 256
SECTIONS = 4
REPLICAS = 4


def draw_step_input(key, part):
    keys = jax.random.split(key, 3)
    shape = (SECTIONS, REPLICAS, SEQ, HEADS)
    rough_guess = jnp.clip(0.5 * jax.random.normal(keys[0], shape, jnp.float32), -2.0, 2.0)
    shards = SEQ // TOK_DEV
    initial_offset = jax.random.uniform(keys[1], (SECTIONS, REPLICAS, shards, 1, 1), jnp.float32, -0.7, 0.7)
    initial_offset = jnp.broadcast_to(initial_offset, (SECTIONS, REPLICAS, shards, TOK_DEV, HEADS)).reshape(shape)
    places = jax.random.randint(keys[2], (SECTIONS, REPLICAS, 4), 0, SEQ)
    offset_sequence = jnp.arange(SEQ)[None, None, :, None] == places[:, :, None, :]
    packet_clusters = jnp.any(offset_sequence, axis=-1).astype(jnp.float32)[..., None]
    payload_lines = -4.0 + rough_guess + initial_offset + 4.0 * packet_clusters
    return payload_lines.astype(jnp.bfloat16)


def draw_decay_log(key, part):
    keys = jax.random.split(key, 1)
    lowest = math.log(min(1.0, 50.0 / SEQ))
    highest = math.log(1.25)
    share = jax.random.uniform(keys[0], (SECTIONS, HEADS), jnp.float32)
    payload_lines = lowest + (highest - lowest) * share
    return payload_lines.astype(jnp.float32)


def block_levels(stream_key, extent, cuts, low, top_value):
    level = 1.0
    for dim, parts in cuts:
        steps = jax.random.uniform(jax.random.fold_in(jax.random.fold_in(stream_key, 6), dim), (parts,), jnp.float32, low / len(cuts), top_value / len(cuts))
        level = level * jnp.repeat(jnp.exp(steps), extent[dim] // parts).reshape((-1,) + (1,) * (len(extent) - 1 - dim))
    return level


def noise(key, shape, scale, bound, cuts=(), kind=jnp.bfloat16):
    array = scale * jax.random.normal(key, shape, jnp.float32)
    if cuts:
        array = array * block_levels(key, shape, cuts, -0.22, 0.18)
    return jnp.clip(array, -bound, bound).astype(kind)


def setup_inputs(seed: int = 0) -> dict:
    splits = jax.random.split(jax.random.key(seed), 11)
    conv_input = noise(splits[0], (SECTIONS, REPLICAS, SEQ, CH), 1.0, 6.0, ((0, 4), (1, 4), (2, 2)))
    gate_input = noise(splits[1], (SECTIONS, REPLICAS, SEQ, DI), 1.0, 6.0, ((0, 4), (1, 4), (2, 2)))
    step_input = draw_step_input(jax.random.fold_in(splits[10], 71), 0)
    cotangent = noise(splits[3], (SECTIONS, REPLICAS, SEQ, DI), 1.0, 6.0, ((0, 4), (1, 4), (2, 2)))
    conv_weight = noise(splits[4], (SECTIONS, CONV, CH), CONV ** -0.5, 3.0, ((0, 4),), jnp.float32)
    conv_bias = jnp.clip(jax.random.uniform(splits[5], (SECTIONS, CH), jnp.float32, -0.5, 0.5) * block_levels(splits[5], (SECTIONS, CH), ((0, 4),), -0.4, 0.0), -0.5, 0.5)
    step_bias = jnp.clip(jax.random.uniform(splits[6], (SECTIONS, HEADS), jnp.float32, -0.5, 0.5) * block_levels(splits[6], (SECTIONS, HEADS), ((0, 4),), -0.4, 0.0), -0.5, 0.5)
    decay_log = draw_decay_log(jax.random.fold_in(splits[10], 71), 0)
    skip_gain = jnp.clip(0.5 + 1.0 * jax.random.uniform(splits[8], (SECTIONS, HEADS), jnp.float32) ** block_levels(splits[8], (SECTIONS, HEADS), ((0, 4),), -0.2, 0.2), 0.5, 1.5)
    norm_gain = jnp.clip(1.0 + 0.1 * jax.random.normal(splits[9], (SECTIONS, DI), jnp.float32), 0.5, 1.5)
    return dict(conv_input=conv_input, gate_input=gate_input, step_input=step_input, cotangent=cotangent, conv_weight=conv_weight, conv_bias=conv_bias, step_bias=step_bias, decay_log=decay_log, skip_gain=skip_gain, norm_gain=norm_gain)


HIGH_BOUND = lax.Precision.HIGHEST

def layer(conv_rows, gates, steps, conv_weight, conv_bias, step_bias, decay_log, skip_gain, norm_gain):
    seq = conv_rows.shape[0]
    inner = HEADS * HEAD_DIM
    padded = jnp.concatenate([jnp.zeros((CONV - 1, conv_rows.shape[1]), jnp.float32), conv_rows], 0)
    conv = conv_bias[None, :]
    for tap in range(CONV):
        conv = conv + conv_weight[tap][None, :] * padded[tap:tap + seq]
    mixed = jax.nn.silu(conv)
    reps = HEADS // GROUPS
    xs = mixed[:, :inner].reshape(seq, HEADS, HEAD_DIM)
    b_heads = jnp.repeat(mixed[:, inner:inner + GROUPS * STATE].reshape(seq, GROUPS, STATE), reps, axis=1)
    c_heads = jnp.repeat(mixed[:, inner + GROUPS * STATE:].reshape(seq, GROUPS, STATE), reps, axis=1)
    delta = jax.nn.softplus(steps + step_bias[None, :])
    rate = delta * (-jnp.exp(decay_log))[None, :]
    width = math.gcd(seq, 64)
    count = seq // width
    lower = (jnp.arange(width)[:, None] >= jnp.arange(width)[None, :])[:, :, None]

    def block(state, pieces):
        x_blk, b_blk, c_blk, d_blk, r_blk = pieces
        cum = jnp.cumsum(r_blk, axis=0)
        seg = cum[:, None, :] - cum[None, :, :]
        weight = jnp.exp(jnp.where(lower, seg, -jnp.inf))
        score_matrix = jnp.einsum('thn,shn->tsh', c_blk, b_blk, precision=HIGH_BOUND) * weight
        final_output = jnp.einsum('tsh,shp->thp', score_matrix, x_blk * d_blk[:, :, None], precision=HIGH_BOUND)
        final_output = final_output + jnp.einsum('thn,hpn->thp', c_blk, state, precision=HIGH_BOUND) * jnp.exp(cum)[:, :, None]
        tail = jnp.exp(cum[-1][None, :] - cum) * d_blk
        state = jnp.exp(cum[-1])[:, None, None] * state + jnp.einsum('shp,shn->hpn', x_blk * tail[:, :, None], b_blk, precision=HIGH_BOUND)
        return (state, final_output)
    pieces = (xs.reshape(count, width, HEADS, HEAD_DIM), b_heads.reshape(count, width, HEADS, STATE), c_heads.reshape(count, width, HEADS, STATE), delta.reshape(count, width, HEADS), rate.reshape(count, width, HEADS))
    start = jnp.zeros((HEADS, HEAD_DIM, STATE), jnp.float32)
    _, blocks = lax.scan(block, start, pieces)
    y_all = blocks.reshape(seq, HEADS, HEAD_DIM) + skip_gain[None, :, None] * xs
    gated = y_all.reshape(seq, inner) * jax.nn.silu(gates)
    grouped = gated.reshape(seq, GROUPS, inner // GROUPS)
    normed = grouped * lax.rsqrt(lax.optimization_barrier(jnp.mean(grouped * grouped, axis=-1, keepdims=True)) + 1e-05)
    return normed.reshape(seq, inner) * norm_gain[None, :]

def reference(conv_input, gate_input, step_input, cotangent, conv_weight, conv_bias, step_bias, decay_log, skip_gain, norm_gain):
    pairs = SECTIONS * REPLICAS

    def flatten(arr):
        return arr.reshape((pairs,) + arr.shape[2:])

    def widen(arr):
        return jnp.repeat(arr, REPLICAS, axis=0)

    def single(items):
        rows_in, gates_in, steps_in, cot, w_one, w_two, w_three, w_four, w_five, w_six = items
        final_output, pull = jax.vjp(layer, rows_in.astype(jnp.float32), gates_in.astype(jnp.float32), steps_in.astype(jnp.float32), w_one, w_two, w_three, w_four, w_five, w_six)
        grads = pull(cot.astype(jnp.float32))
        return (final_output.astype(jnp.bfloat16), grads[0].astype(jnp.bfloat16), grads[1].astype(jnp.bfloat16), grads[2].astype(jnp.bfloat16), grads[3], grads[4], grads[5], grads[6], grads[7], grads[8])
    results = lax.map(single, (flatten(conv_input), flatten(gate_input), flatten(step_input), flatten(cotangent), widen(conv_weight), widen(conv_bias), widen(step_bias), widen(decay_log), widen(skip_gain), widen(norm_gain)))
    acts = [item.reshape((SECTIONS, REPLICAS) + item.shape[1:]) for item in results[:4]]
    params = [item.reshape((SECTIONS, REPLICAS) + item.shape[1:]).sum(axis=1) for item in results[4:]]

    def later(grad):
        return jnp.concatenate([grad[1:], jnp.zeros_like(grad[:1])], 0)
    next_input = jnp.concatenate([jnp.zeros_like(acts[0][:1]), acts[0][:-1]], 0)
    return (next_input, later(acts[1]), later(acts[2]), later(acts[3]), params[0], params[1], params[2], params[3], params[4], params[5])
```

```python
import functools
import jax
import jax.numpy as jnp
from jax import lax
from jax.experimental import pallas as pl
from jax.experimental.pallas import tpu as pltpu
from jax.sharding import PartitionSpec as P

HEADS = 16
HEAD_DIM = 64
STATE = 256
GROUPS = 8
CONV = 4


HIGH_BOUND = lax.Precision.HIGHEST


def shifted(block, axis, distance):
    devices = range(lax.axis_size(axis))
    route = [(i - distance, i) for i in devices if i - distance in devices]
    return lax.ppermute(block, axis, route)


def prefix(part, axis, combine, identity):
    count = lax.axis_size(axis)
    place = lax.axis_index(axis)
    ahead = count - 1 - place
    gathered = jax.tree.map(lambda a: lax.all_gather(a, axis), part)
    state = jax.tree.map(lambda a, e: jnp.zeros_like(a) + jnp.asarray(e, a.dtype), part, identity)

    def one(turn, state):
        source = count - 1 - turn
        return combine(
            state, jax.tree.map(lambda a: lax.dynamic_index_in_dim(a, source, 0, False), gathered)
        )

    return lax.fori_loop(0, ahead, one, state)


def conv_mix(extended, taps, initial_offset):
    rows = extended.shape[0] - (CONV - 1)
    total = initial_offset[None, :]
    for tap in range(CONV):
        total = total + taps[tap][None, :] * extended[tap : tap + rows]
    return jax.nn.silu(total)


def split_mix(mixed, steps, step_shift, damping_exponents):
    rows = mixed.shape[0]
    inner = HEADS * HEAD_DIM
    payload_lines = mixed[:, :inner].reshape(rows, GROUPS, HEADS // GROUPS, HEAD_DIM)
    in_maps = mixed[:, inner : inner + GROUPS * STATE].reshape(rows, GROUPS, STATE)
    out_maps = mixed[:, inner + GROUPS * STATE :].reshape(rows, GROUPS, STATE)
    delta = jax.nn.softplus(steps + step_shift[None, :])
    upto = jnp.tril(jnp.ones((rows, rows), jnp.float32))
    rates = delta * (-jnp.exp(damping_exponents))[None, :]
    cumulative = jnp.dot(upto, rates, precision=HIGH_BOUND)
    return (payload_lines, in_maps, out_maps, delta, cumulative)


def fragment_condition(extended, steps, taps, initial_offset, step_shift, damping_exponents):
    payload_lines, in_maps, out_maps, delta, cumulative = split_mix(
        conv_mix(extended, taps, initial_offset), steps, step_shift, damping_exponents
    )
    rows = payload_lines.shape[0]
    total = cumulative[-1]
    weight = (jnp.exp(total[None, :] - cumulative) * delta).reshape(rows, GROUPS, HEADS // GROUPS)
    state = jnp.einsum(
        "tgrp,tgn->grpn", payload_lines * weight[..., None], in_maps, precision=HIGH_BOUND
    )
    return (state.reshape(HEADS, HEAD_DIM, STATE), total)


def shard_layer(
    extended,
    gates,
    steps,
    taps,
    initial_offset,
    step_shift,
    damping_exponents,
    skip_values,
    gain_values,
    carried,
):
    payload_lines, in_maps, out_maps, delta, cumulative = split_mix(
        conv_mix(extended, taps, initial_offset), steps, step_shift, damping_exponents
    )
    rows = payload_lines.shape[0]
    reps = HEADS // GROUPS
    lower = (jnp.arange(rows)[:, None] >= jnp.arange(rows)[None, :])[None]
    seg = cumulative.T[:, :, None] - cumulative.T[:, None, :]
    weight = jnp.exp(jnp.where(lower, seg, -jnp.inf)).reshape(GROUPS, reps, rows, rows)
    intersection_maps = jnp.einsum("tgn,sgn->gts", out_maps, in_maps, precision=HIGH_BOUND)
    score_matrix = weight * intersection_maps[:, None]
    scaled_values = payload_lines * delta.reshape(rows, GROUPS, reps)[..., None]
    final_output = jnp.einsum("jzlh,hjzc->ljzc", score_matrix, scaled_values, precision=HIGH_BOUND)
    incoming = jnp.einsum(
        "tgn,grpn->tgrp",
        out_maps,
        carried.reshape(GROUPS, reps, HEAD_DIM, STATE),
        precision=HIGH_BOUND,
    )
    final_output = (
        final_output + incoming * jnp.exp(cumulative).reshape(rows, GROUPS, reps)[..., None]
    )
    final_output = (
        final_output + skip_values.reshape(GROUPS, reps)[None, :, :, None] * payload_lines
    )
    gated = final_output.reshape(rows, GROUPS, -1) * jax.nn.silu(gates).reshape(rows, GROUPS, -1)
    normed = gated * lax.rsqrt(jnp.mean(gated * gated, axis=-1, keepdims=True) + 1e-05)
    return normed.reshape(rows, -1) * gain_values[None, :]


def combine(earlier, later):
    return (earlier[0] * later[0], later[0][:, None] * earlier[1] + later[1])


def shards(
    conv_input,
    gate_input,
    step_input,
    cotangent,
    conv_weight,
    conv_bias,
    step_bias,
    decay_log,
    skip_gain,
    norm_gain,
):
    local_rows = conv_input[0, 0]
    count = local_rows.shape[0]
    taps, initial_offset = (conv_weight[0], conv_bias[0])
    step_shift, damping_exponents = (step_bias[0], decay_log[0])
    skip_values, gain_values = (skip_gain[0], norm_gain[0])
    previous = shifted(local_rows[count - (CONV - 1) :], "ctx", 1)
    extended = jnp.concatenate([previous, local_rows], 0).astype(jnp.float32)
    gates = gate_input[0, 0].astype(jnp.float32)
    steps = step_input[0, 0].astype(jnp.float32)
    (state, total), state_pull = jax.vjp(
        fragment_condition, extended, steps, taps, initial_offset, step_shift, damping_exponents
    )
    decay = jnp.exp(total)
    flat_state = state.reshape(HEADS, HEAD_DIM * STATE)
    unity = (jnp.ones((HEADS,), jnp.float32), jnp.zeros((HEADS, HEAD_DIM * STATE), jnp.float32))

    def advance(index, current):
        return shifted(decay[:, None] * current + flat_state, "ctx", 1)

    incoming = lax.fori_loop(
        0, lax.axis_size("ctx") - 1, advance, jnp.zeros((HEADS, HEAD_DIM * STATE), jnp.float32)
    )
    carried = incoming.reshape(HEADS, HEAD_DIM, STATE)
    final_output, layer_pull = jax.vjp(
        shard_layer,
        extended,
        gates,
        steps,
        taps,
        initial_offset,
        step_shift,
        damping_exponents,
        skip_values,
        gain_values,
        carried,
    )
    forward = shifted(final_output.astype(jnp.bfloat16)[None, None], "section", 1)
    grads = layer_pull(cotangent[0, 0].astype(jnp.float32))
    carry_grad = grads[9].reshape(HEADS, HEAD_DIM * STATE)
    outgoing = prefix((decay, carry_grad), "ctx", combine, unity)[1]
    outgoing_grad = outgoing.reshape(HEADS, HEAD_DIM, STATE)
    total_grad = jnp.sum(outgoing_grad * carried, axis=(1, 2)) * decay
    extra = state_pull((outgoing_grad, total_grad))
    ext_grad = grads[0] + extra[0]
    step_grad = grads[2] + extra[1]
    param_terms = (
        grads[3] + extra[2],
        grads[4] + extra[3],
        grads[5] + extra[4],
        grads[6] + extra[5],
        grads[7],
        grads[8],
    )
    returned = shifted(ext_grad[: CONV - 1], "ctx", -1)
    own_grad = ext_grad[CONV - 1 :]
    row_grad = jnp.concatenate(
        [own_grad[: count - (CONV - 1)], own_grad[count - (CONV - 1) :] + returned], 0
    )
    backward = shifted(
        (
            row_grad.astype(jnp.bfloat16)[None, None],
            grads[1].astype(jnp.bfloat16)[None, None],
            step_grad.astype(jnp.bfloat16)[None, None],
        ),
        "section",
        -1,
    )
    summed = lax.psum(
        (
            param_terms[0],
            param_terms[1],
            param_terms[2],
            param_terms[3],
            param_terms[4],
            param_terms[5],
        ),
        ("ctx", "dp"),
    )
    return (
        forward,
        backward[0],
        backward[1],
        backward[2],
        summed[0][None],
        summed[1][None],
        summed[2][None],
        summed[3][None],
        summed[4][None],
        summed[5][None],
    )


MESH = pl.DeviceIdType.MESH
F32 = jnp.float32
BF16 = jnp.bfloat16
INNER = HEADS * HEAD_DIM
REPS = HEADS // GROUPS
WIDE = REPS * HEAD_DIM
MIX = WIDE + 2 * STATE
HALF = GROUPS // 2
NN = ((1,), (0,))
NT = ((1,), (1,))
TN = ((0,), (0,))


def split(a):
    high = a.astype(BF16)
    return high, (a - high.astype(F32)).astype(BF16)


def dot(a, b, dims):
    return lax.dot_general(a, b, (dims, ((), ())), preferred_element_type=F32)


def dot3(a, b, dims):
    return dot(a[0], b[0], dims) + (dot(a[0], b[1], dims) + dot(a[1], b[0], dims))


def group_columns(g):
    return (
        pl.multiple_of(g * WIDE, 128),
        pl.multiple_of(INNER + g * STATE, 128),
        pl.multiple_of(INNER + (GROUPS + g) * STATE, 128),
    )


def pair_kernel(
    conv_in, gate_in, step_in, cot_in, w_ref, b_ref, sb_ref, dl_ref, sk_ref, ng_ref,
    nxt, gconv, ggate, gstep, gtap, gcb, gsb, gdl, gsk, gng,
    uin, steps, steprow, upad, zpad, mix, dsl, dtc, sigc, ratec, cumc, cumr, ddt, drate, small,
    stage_c, stage_o, stage_s, step_parts, partial, final, relay,
    own_sem, xs_sem, xr_sem, st_sem, conv_sem, gate_sem, next_sem, dstep_sem,
    ps_sem, pr_sem, fin_sem, via_sem, relay_sem,
):
    core = lax.axis_index("ctx")
    sec = lax.axis_index("section")
    dp = lax.axis_index("dp")
    nsec = lax.axis_size("section")
    ndp = lax.axis_size("dp")
    tok = conv_in.shape[2]
    seq = 2 * tok
    other = 1 - core

    def place(c, s, d):
        return {"ctx": c, "section": s, "dp": d}

    def remote(src, dst, send, recv, c, s, d):
        return pltpu.make_async_remote_copy(
            src_ref=src, dst_ref=dst, send_sem=send, recv_sem=recv,
            device_id=place(c, s, d), device_id_type=MESH,
        )

    after = lax.rem(sec + 1, nsec)
    before = lax.rem(sec + nsec - 1, nsec)
    barrier = pltpu.get_barrier_semaphore()

    def greet(c, s, d):
        pl.semaphore_signal(barrier, inc=1, device_id=place(c, s, d), device_id_type=MESH)

    greet(other, sec, dp)
    for c in range(2):
        greet(c, after, dp)
        greet(c, before, dp)
        greet(c, lax.rem(sec + 2, nsec), dp)
    for k in range(1, ndp):
        greet(core, sec, lax.rem(dp + k, ndp))

    def pieces(g):
        xc, bc, cc = group_columns(g)
        return (
            (conv_in.at[0, 0, :, pl.ds(xc, WIDE)], 0, WIDE),
            (conv_in.at[0, 0, :, pl.ds(bc, STATE)], WIDE, STATE),
            (conv_in.at[0, 0, :, pl.ds(cc, STATE)], WIDE + STATE, STATE),
            (gate_in.at[0, 0, :, pl.ds(xc, WIDE)], MIX, WIDE),
            (cot_in.at[0, 0, :, pl.ds(xc, WIDE)], MIX + WIDE, WIDE),
        )

    mine = pl.ds(pl.multiple_of(core * tok, tok), tok)
    theirs = pl.ds(pl.multiple_of(other * tok, tok), tok)
    own_step = pltpu.make_async_copy(step_in.at[0, 0], steps.at[core], st_sem.at[0])
    own_step.start()

    def fetch(j, _):
        for src, off, width in pieces(core * HALF + j):
            pltpu.make_async_copy(
                src, uin.at[j, mine, pl.ds(off, width)], own_sem.at[j]
            ).start()
        return 0

    lax.fori_loop(0, HALF, fetch, 0)
    partial[dp] = jnp.zeros(partial.shape[1:], F32)
    upad[0:8, :] = jnp.zeros((8, MIX), F32)
    zpad[seq : seq + 8, :] = jnp.zeros((8, MIX), F32)
    for ref in (steprow, dtc, sigc, ratec, ddt, drate, small):
        ref[...] = jnp.zeros_like(ref)
    pl.semaphore_wait(barrier, 1 + 6 + (ndp - 1))
    step_copy = remote(
        step_in.at[0, 0], steps.at[core], st_sem.at[1], st_sem.at[2], other, sec, dp
    )
    step_copy.start()

    def exchange(j, _):
        for src, off, width in pieces(other * HALF + j):
            remote(
                src, uin.at[j, mine, pl.ds(off, width)], xs_sem.at[j], xr_sem.at[j], other, sec, dp
            ).start()
        return 0

    lax.fori_loop(0, HALF, exchange, 0)

    own_step.wait()
    step_copy.wait()
    for c in range(2):
        steprow[0:HEADS, c * tok : (c + 1) * tok] = steps[c].astype(F32)
    raw = steprow[...].T[:, 0:HEADS] + sb_ref[...]
    delta = jnp.maximum(raw, 0.0) + jnp.log1p(jnp.exp(-jnp.abs(raw)))
    dtc[:, 0:HEADS] = delta
    sigc[:, 0:HEADS] = jax.nn.sigmoid(raw)
    ratec[:, 0:HEADS] = delta * (-jnp.exp(dl_ref[...]))
    rows2 = lax.broadcasted_iota(jnp.int32, (seq, seq), 0)
    cols2 = lax.broadcasted_iota(jnp.int32, (seq, seq), 1)
    ones_low = jnp.where(rows2 >= cols2, 1.0, 0.0).astype(BF16)
    rate = ratec[...]
    r_hi, r_rest = rate.astype(BF16), rate - rate.astype(BF16).astype(F32)
    r_mid, r_lo = split(r_rest)
    cumulative = dot(ones_low, r_hi, NN) + (dot(ones_low, r_mid, NN) + dot(ones_low, r_lo, NN))
    cumc[...] = cumulative
    cumr[...] = cumulative.T

    def group(j, _):
        g = core * HALF + j
        cols = group_columns(g)
        pltpu.make_async_copy(uin.at[j, mine], uin.at[j, mine], own_sem.at[j]).wait()
        remote(uin.at[j, mine], uin.at[j, theirs], xs_sem.at[j], xr_sem.at[j], other, sec, dp).wait()
        blocks = [(0, cols[0])]
        for base, col in ((WIDE, cols[1]), (WIDE + STATE, cols[2])):
            for part in range(STATE // 128):
                blocks.append((base + part * 128, pl.multiple_of(col + part * 128, 128)))

        for off, col in blocks:
            here = slice(off, off + 128)
            upad[8 : 8 + seq, here] = uin[j, :, here].astype(F32)
            z = b_ref[:, pl.ds(col, 128)]
            for k in range(CONV):
                z = z + w_ref[0, pl.ds(k, 1), pl.ds(col, 128)] * upad[5 + k : 5 + k + seq, here]
            s = jax.nn.sigmoid(z)
            mix[:, here] = z * s
            dsl[:, here] = s * (1.0 + z * (1.0 - s))

        lane = lax.broadcasted_iota(jnp.int32, (seq, 128), 1)
        lane1 = lax.broadcasted_iota(jnp.int32, (1, 128), 1)
        lane16 = lax.broadcasted_iota(jnp.int32, (1, HEADS), 1)
        row = lax.broadcasted_iota(jnp.int32, (seq, seq), 0)
        column = lax.broadcasted_iota(jnp.int32, (seq, seq), 1)
        first = lane < HEAD_DIM

        def pick(ref, h):
            return jnp.sum(jnp.where(lane == h, ref[...], 0.0), axis=1, keepdims=True)

        def pick1(ref, h):
            return jnp.sum(jnp.where(lane16 == h, ref[...], 0.0), axis=1, keepdims=True)

        x = mix[:, 0:WIDE]
        bmap = split(mix[:, WIDE : WIDE + STATE])
        cmap = split(mix[:, WIDE + STATE : MIX])
        h0 = g * REPS
        dt2 = jnp.where(first, pick(dtc, h0), pick(dtc, h0 + 1))
        skip2 = jnp.where(first[0:1], pick1(sk_ref, h0), pick1(sk_ref, h0 + 1))
        xs = x * dt2
        xs_p = split(xs)
        scores = dot3(cmap, bmap, NT)
        decay, mixed, ys = [], [], []
        for r in range(REPS):
            seg = pick(cumc, h0 + r) - cumr[pl.ds(h0 + r, 1), :]
            w = jnp.exp(jnp.where(row >= column, seg, -jnp.inf))
            a = scores * w
            a_p = split(a)
            decay.append(w)
            mixed.append((a, a_p))
            ys.append(dot3(a_p, xs_p, NN))
        y = jnp.where(first, ys[0], ys[1]) + skip2 * x
        gate = uin[j, :, MIX : MIX + WIDE].astype(F32)
        cot = uin[j, :, MIX + WIDE : MIX + 2 * WIDE].astype(F32)
        gain = ng_ref[:, pl.ds(cols[0], WIDE)]
        s = jax.nn.sigmoid(gate)
        act = gate * s
        gated = y * act
        scale = lax.rsqrt(jnp.mean(gated * gated, axis=1, keepdims=True) + 1e-05)
        normed = gated * scale
        stage_o[j, :, 0:WIDE] = (normed * gain).astype(BF16)
        dn = cot * gain
        dgated = scale * (dn - normed * jnp.mean(dn * normed, axis=1, keepdims=True))
        dy = dgated * act
        stage_o[j, :, WIDE : 2 * WIDE] = (dgated * y * (s * (1.0 + gate * (1.0 - s)))).astype(BF16)

        odd = lax.rem(j, 2) == 1

        def send_half(base, t, dst, done, landed, s):
            remote(
                stage_o.at[j, pl.ds(t * tok, tok), pl.ds(base, WIDE)], dst, done, landed, t, s, dp
            ).start()

        @pl.when(jnp.logical_and(sec < nsec - 1, jnp.logical_not(jnp.logical_and(sec == 1, odd))))
        def _():
            for t in range(2):
                send_half(
                    0, t, nxt.at[0, 0, :, pl.ds(cols[0], WIDE)],
                    next_sem.at[0], next_sem.at[1], sec + 1,
                )

        @pl.when(jnp.logical_and(sec == 1, odd))
        def _():
            slot = core * (HALF // 2) + j // 2
            for t in range(2):
                send_half(0, t, relay.at[slot], next_sem.at[0], relay_sem.at[slot], 3)

        @pl.when(jnp.logical_or(sec == 1, sec == 3))
        def _():
            for t in range(2):
                send_half(
                    WIDE, t, ggate.at[0, 0, :, pl.ds(cols[0], WIDE)],
                    gate_sem.at[0], gate_sem.at[1], sec - 1,
                )

        @pl.when(sec == 2)
        def _():
            slot = core * HALF + j
            for t in range(2):
                send_half(WIDE, t, relay.at[slot], gate_sem.at[0], relay_sem.at[slot], 0)

        partial[dp, j, 5:6, 0:WIDE] = jnp.sum(cot * normed, axis=0, keepdims=True)
        dyx = jnp.sum(dy * x, axis=0, keepdims=True)
        dscore = jnp.zeros((seq, seq), F32)
        dy_p = split(dy)
        das = []
        for r in range(REPS):
            own = first if r == 0 else jnp.logical_not(first)
            da = dot3(split(jnp.where(own, dy, 0.0)), xs_p, NT)
            das.append(da)
            dscore = dscore + da * decay[r]
        ds_p = split(dscore)

        def conv_back(off, width, start):
            for part in range(width // 128):
                here = slice(off + part * 128, off + part * 128 + 128)
                col = pl.multiple_of(start + part * 128, 128)
                dz = zpad[0:seq, here]
                du = jnp.zeros((seq, 128), F32)
                for k in range(CONV):
                    du = du + w_ref[0, pl.ds(k, 1), pl.ds(col, 128)] * zpad[3 - k : 3 - k + seq, here]
                    partial[dp, j, pl.ds(k, 1), here] = jnp.sum(
                        dz * upad[5 + k : 5 + k + seq, here], axis=0, keepdims=True
                    )
                partial[dp, j, pl.ds(4, 1), here] = jnp.sum(dz, axis=0, keepdims=True)
                stage_c[j, :, here] = du.astype(BF16)

            @pl.when(sec > 0)
            def _():
                for t in range(2):
                    remote(
                        stage_c.at[j, pl.ds(t * tok, tok), pl.ds(off, width)],
                        gconv.at[0, 0, :, pl.ds(start, width)],
                        conv_sem.at[0], conv_sem.at[1], t, sec - 1, dp,
                    ).start()

        zpad[0:seq, WIDE + STATE : MIX] = dot3(ds_p, bmap, NN) * dsl[:, WIDE + STATE : MIX]
        conv_back(WIDE + STATE, STATE, cols[2])
        zpad[0:seq, WIDE : WIDE + STATE] = dot3(ds_p, cmap, TN) * dsl[:, WIDE : WIDE + STATE]
        conv_back(WIDE, STATE, cols[1])
        dxs = jnp.where(first, dot3(mixed[0][1], dy_p, TN), dot3(mixed[1][1], dy_p, TN))
        zpad[0:seq, 0:WIDE] = (skip2 * dy + dxs * dt2) * dsl[:, 0:WIDE]
        conv_back(0, WIDE, cols[0])
        upper = jnp.where(row <= column, 1.0, 0.0).astype(BF16)
        dxx = dxs * x
        for r in range(REPS):
            own = first if r == 0 else jnp.logical_not(first)
            p = split(das[r] * mixed[r][0])
            later = dot(upper, p[0], NN) + dot(upper, p[1], NN)
            dr = jnp.sum(jnp.where(row > column, later, 0.0), axis=1, keepdims=True)
            drate[...] += jnp.where(lane == h0 + r, dr, 0.0)
            total = jnp.sum(jnp.where(own[0:1], dyx, 0.0), axis=1, keepdims=True)
            small[2:3, :] += jnp.where(lane1 == h0 + r, total, 0.0)
            dd = jnp.sum(jnp.where(own, dxx, 0.0), axis=1, keepdims=True)
            ddt[...] += jnp.where(lane == h0 + r, dd, 0.0)

        for k in range(1, ndp):
            to = lax.rem(dp + k, ndp)
            remote(
                partial.at[dp, j], partial.at[dp, j], ps_sem.at[to], pr_sem.at[dp], core, sec, to
            ).start()
        return 0

    lax.fori_loop(0, HALF, group, 0)

    def pass_on(slot, g, out, landed, s):
        part = relay.at[slot]
        remote(part, part, via_sem.at[0], relay_sem.at[slot], core, s, dp).wait_recv()
        remote(
            part, out.at[0, 0, :, pl.ds(g * WIDE, WIDE)], via_sem.at[0], landed, core, s, dp
        ).start()

    @pl.when(sec == 0)
    def _():
        for g in range(GROUPS):
            pass_on(g, g, ggate, gate_sem.at[1], 1)

    @pl.when(sec == 3)
    def _():
        for at in range(GROUPS // 2):
            pass_on(at, 2 * at + 1, nxt, next_sem.at[1], 2)

    @pl.when(sec == 0)
    def _():
        nxt[...] = jnp.zeros_like(nxt)

    @pl.when(sec == nsec - 1)
    def _():
        gconv[...] = jnp.zeros_like(gconv)
        ggate[...] = jnp.zeros_like(ggate)
        gstep[...] = jnp.zeros_like(gstep)

    damp = jnp.exp(dl_ref[...])
    dr16 = drate[:, 0:HEADS]
    dstep = (ddt[:, 0:HEADS] - dr16 * damp) * sigc[:, 0:HEADS]
    small[0:1, 0:HEADS] = jnp.sum(dstep, axis=0, keepdims=True)
    small[1:2, 0:HEADS] = jnp.sum(dr16 * ratec[:, 0:HEADS], axis=0, keepdims=True)
    drate[:, 0:HEADS] = dstep
    turned = drate[...].T
    for t in range(2):
        stage_s[t] = turned[0:HEADS, t * tok : (t + 1) * tok].astype(BF16)

    @pl.when(sec > 0)
    def _():
        for t in range(2):
            remote(
                stage_s.at[t], step_parts.at[core],
                dstep_sem.at[2], dstep_sem.at[core], t, sec - 1, dp,
            ).start()

    partial[dp, HALF, :, 0:128] = small[...]
    for k in range(1, ndp):
        to = lax.rem(dp + k, ndp)
        remote(
            partial.at[dp, HALF], partial.at[dp, HALF], ps_sem.at[to], pr_sem.at[dp], core, sec, to
        ).start()
    for k in range(1, ndp):
        to = lax.rem(dp + k, ndp)
        remote(partial.at[dp], partial.at[to], ps_sem.at[to], pr_sem.at[to], core, sec, to).wait()
    total = partial[0]
    for k in range(1, ndp):
        total = total + partial[k]
    final[core] = total
    halves = remote(final.at[core], final.at[core], fin_sem.at[0], fin_sem.at[1], other, sec, dp)
    halves.start()
    remote(final.at[core], final.at[other], fin_sem.at[0], fin_sem.at[1], other, sec, dp).wait()
    for g in range(GROUPS):
        c, j = g // HALF, g % HALF
        gng[0:1, g * WIDE : (g + 1) * WIDE] = final[c, j, 5:6, 0:WIDE]
        for off, width, col in (
            (0, WIDE, g * WIDE),
            (WIDE, STATE, INNER + g * STATE),
            (WIDE + STATE, STATE, INNER + (GROUPS + g) * STATE),
        ):
            gtap[0, :, col : col + width] = final[c, j, 0:CONV, off : off + width]
            gcb[0:1, col : col + width] = final[c, j, CONV : CONV + 1, off : off + width]
    for at, ref in enumerate((gsb, gdl, gsk)):
        ref[...] = final[0, HALF, at : at + 1, 0:HEADS] + final[1, HALF, at : at + 1, 0:HEADS]

    @pl.when(sec < nsec - 1)
    def _():
        for c in range(2):
            part = step_parts.at[c]
            remote(part, part, dstep_sem.at[2], dstep_sem.at[c], core, sec + 1, dp).wait_recv()
        gstep[0, 0] = (step_parts[0].astype(F32) + step_parts[1].astype(F32)).astype(BF16)

    @pl.when(sec == 0)
    def _():
        remote(relay, relay, via_sem.at[0], relay_sem.at[0], core, 1, dp).wait_send()

    @pl.when(sec > 0)
    def _():
        low = sec - 1
        remote(stage_c, stage_c, conv_sem.at[0], conv_sem.at[1], core, low, dp).wait_send()
        half_o = stage_o.at[:, :, pl.ds(0, WIDE)]
        remote(half_o, half_o, gate_sem.at[0], gate_sem.at[1], core, low, dp).wait_send()
        remote(stage_s, stage_s, dstep_sem.at[2], dstep_sem.at[0], core, low, dp).wait_send()
        remote(
            nxt.at[0, 0], nxt.at[0, 0], next_sem.at[0], next_sem.at[1], core, low, dp
        ).wait_recv()

    @pl.when(sec == nsec - 1)
    def _():
        used = relay.at[pl.ds(0, GROUPS // 2)]
        remote(used, used, via_sem.at[0], relay_sem.at[0], core, 2, dp).wait_send()

    @pl.when(sec < nsec - 1)
    def _():
        high = sec + 1
        half_o = stage_o.at[:, :, pl.ds(0, WIDE)]
        remote(half_o, half_o, next_sem.at[0], next_sem.at[1], core, high, dp).wait_send()
        whole = ggate.at[0, 0]
        remote(whole, whole, gate_sem.at[0], gate_sem.at[1], core, high, dp).wait_recv()
        whole = gconv.at[0, 0]
        remote(whole, whole, conv_sem.at[0], conv_sem.at[1], core, high, dp).wait_recv()


def finish_kernel(*refs):
    count = len(refs) // 2
    sem = refs[-1]
    copies = [pltpu.make_async_copy(refs[i], refs[count + i], sem.at[i]) for i in range(count)]
    for copy in copies:
        copy.start()
    for copy in copies:
        copy.wait()


def paired(
    conv_input, gate_input, step_input, cotangent, conv_weight,
    conv_bias, step_bias, decay_log, skip_gain, norm_gain,
):
    tok = conv_input.shape[2]
    seq = 2 * tok
    ndp = lax.axis_size("dp")
    hbm = pl.BlockSpec(memory_space=pl.ANY)
    vmem = pl.BlockSpec(memory_space=pltpu.VMEM)
    scratch = [
        pltpu.VMEM((HALF, seq, MIX + 2 * WIDE), BF16),
        pltpu.VMEM((2, HEADS, tok), BF16),
        pltpu.VMEM((128, seq), F32),
        pltpu.VMEM((seq + 8, MIX), F32),
        pltpu.VMEM((seq + 8, MIX), F32),
        pltpu.VMEM((seq, MIX), F32),
        pltpu.VMEM((seq, MIX), F32),
        pltpu.VMEM((seq, 128), F32),
        pltpu.VMEM((seq, 128), F32),
        pltpu.VMEM((seq, 128), F32),
        pltpu.VMEM((seq, 128), F32),
        pltpu.VMEM((128, seq), F32),
        pltpu.VMEM((seq, 128), F32),
        pltpu.VMEM((seq, 128), F32),
        pltpu.VMEM((8, 128), F32),
        pltpu.VMEM((HALF, seq, MIX), BF16),
        pltpu.VMEM((HALF, seq, 2 * WIDE), BF16),
        pltpu.VMEM((2, HEADS, tok), BF16),
        pltpu.VMEM((2, HEADS, tok), BF16),
        pltpu.VMEM((ndp, HALF + 1, 8, MIX), F32),
        pltpu.VMEM((2, HALF + 1, 8, MIX), F32),
        pltpu.VMEM((GROUPS, tok, WIDE), BF16),
        pltpu.SemaphoreType.DMA((HALF,)),
        pltpu.SemaphoreType.DMA((HALF,)),
        pltpu.SemaphoreType.DMA((HALF,)),
        pltpu.SemaphoreType.DMA((3,)),
        pltpu.SemaphoreType.DMA((2,)),
        pltpu.SemaphoreType.DMA((2,)),
        pltpu.SemaphoreType.DMA((2,)),
        pltpu.SemaphoreType.DMA((3,)),
        pltpu.SemaphoreType.DMA((ndp,)),
        pltpu.SemaphoreType.DMA((ndp,)),
        pltpu.SemaphoreType.DMA((2,)),
        pltpu.SemaphoreType.DMA((1,)),
        pltpu.SemaphoreType.DMA((GROUPS,)),
    ]
    turned = jnp.swapaxes(step_input, 2, 3)
    shapes = [
        (gate_input.shape, BF16),
        (conv_input.shape, BF16),
        (gate_input.shape, BF16),
        (turned.shape, BF16),
        (conv_weight.shape, F32),
        (conv_bias.shape, F32),
        (step_bias.shape, F32),
        (decay_log.shape, F32),
        (skip_gain.shape, F32),
        (norm_gain.shape, F32),
    ]
    inputs = [
        pltpu.with_memory_space_constraint(a, pltpu.HBM)
        for a in (
            conv_input, gate_input, turned, cotangent, conv_weight,
            conv_bias, step_bias, decay_log, skip_gain, norm_gain,
        )
    ]
    sent = pl.pallas_call(
        pair_kernel,
        name="mixer_tick",
        in_specs=[hbm] * 4 + [vmem] * 6,
        out_specs=[vmem] * 10,
        out_shape=[pltpu.VMEM(shape, kind) for shape, kind in shapes],
        scratch_shapes=scratch,
        compiler_params=pltpu.CompilerParams(
            collective_id=0, has_side_effects=True, vmem_limit_bytes=24 * 1024 * 1024
        ),
    )(*inputs)
    done = pl.pallas_call(
        finish_kernel,
        name="mixer_finish",
        in_specs=[vmem] * 10,
        out_specs=[hbm] * 10,
        out_shape=[jax.ShapeDtypeStruct(shape, kind) for shape, kind in shapes],
        scratch_shapes=[pltpu.SemaphoreType.DMA((10,))],
        compiler_params=pltpu.CompilerParams(vmem_limit_bytes=1024 * 1024),
    )(*sent)
    return tuple(done[:3]) + (jnp.swapaxes(done[3], 2, 3),) + tuple(done[4:])


def solution(mesh):
    in_specs = (
        P("section", "dp", "ctx", None),
        P("section", "dp", "ctx", None),
        P("section", "dp", "ctx", None),
        P("section", "dp", "ctx", None),
        P("section", None, None),
        P("section", None),
        P("section", None),
        P("section", None),
        P("section", None),
        P("section", None),
    )
    out_specs = (
        P("section", "dp", "ctx", None),
        P("section", "dp", "ctx", None),
        P("section", "dp", "ctx", None),
        P("section", "dp", "ctx", None),
        P("section", None, None),
        P("section", None),
        P("section", None),
        P("section", None),
        P("section", None),
        P("section", None),
    )
    body = paired if (mesh.shape["ctx"], mesh.shape["section"]) == (2, 4) else shards
    return jax.shard_map(body, mesh=mesh, in_specs=in_specs, out_specs=out_specs, check_vma=False)
```

```python
import functools
import jax
import jax.numpy as jnp
from jax import lax
from jax.experimental import pallas as pl
from jax.experimental.pallas import tpu as pltpu
from jax.sharding import PartitionSpec as P

HEADS = 16
HEAD_DIM = 64
STATE = 256
GROUPS = 8
CONV = 4


HIGH_BOUND = lax.Precision.HIGHEST


def shifted(block, axis, distance):
    devices = range(lax.axis_size(axis))
    route = [(i - distance, i) for i in devices if i - distance in devices]
    return lax.ppermute(block, axis, route)


def prefix(part, axis, combine, identity):
    count = lax.axis_size(axis)
    place = lax.axis_index(axis)
    ahead = count - 1 - place
    gathered = jax.tree.map(lambda a: lax.all_gather(a, axis), part)
    state = jax.tree.map(lambda a, e: jnp.zeros_like(a) + jnp.asarray(e, a.dtype), part, identity)

    def one(turn, state):
        source = count - 1 - turn
        return combine(
            state, jax.tree.map(lambda a: lax.dynamic_index_in_dim(a, source, 0, False), gathered)
        )

    return lax.fori_loop(0, ahead, one, state)


def conv_mix(extended, taps, initial_offset):
    rows = extended.shape[0] - (CONV - 1)
    total = initial_offset[None, :]
    for tap in range(CONV):
        total = total + taps[tap][None, :] * extended[tap : tap + rows]
    return jax.nn.silu(total)


def split_mix(mixed, steps, step_shift, damping_exponents):
    rows = mixed.shape[0]
    inner = HEADS * HEAD_DIM
    payload_lines = mixed[:, :inner].reshape(rows, GROUPS, HEADS // GROUPS, HEAD_DIM)
    in_maps = mixed[:, inner : inner + GROUPS * STATE].reshape(rows, GROUPS, STATE)
    out_maps = mixed[:, inner + GROUPS * STATE :].reshape(rows, GROUPS, STATE)
    delta = jax.nn.softplus(steps + step_shift[None, :])
    upto = jnp.tril(jnp.ones((rows, rows), jnp.float32))
    rates = delta * (-jnp.exp(damping_exponents))[None, :]
    cumulative = jnp.dot(upto, rates, precision=HIGH_BOUND)
    return (payload_lines, in_maps, out_maps, delta, cumulative)


def fragment_condition(extended, steps, taps, initial_offset, step_shift, damping_exponents):
    payload_lines, in_maps, out_maps, delta, cumulative = split_mix(
        conv_mix(extended, taps, initial_offset), steps, step_shift, damping_exponents
    )
    rows = payload_lines.shape[0]
    total = cumulative[-1]
    weight = (jnp.exp(total[None, :] - cumulative) * delta).reshape(rows, GROUPS, HEADS // GROUPS)
    state = jnp.einsum(
        "tgrp,tgn->grpn", payload_lines * weight[..., None], in_maps, precision=HIGH_BOUND
    )
    return (state.reshape(HEADS, HEAD_DIM, STATE), total)


def shard_layer(
    extended,
    gates,
    steps,
    taps,
    initial_offset,
    step_shift,
    damping_exponents,
    skip_values,
    gain_values,
    carried,
):
    payload_lines, in_maps, out_maps, delta, cumulative = split_mix(
        conv_mix(extended, taps, initial_offset), steps, step_shift, damping_exponents
    )
    rows = payload_lines.shape[0]
    reps = HEADS // GROUPS
    lower = (jnp.arange(rows)[:, None] >= jnp.arange(rows)[None, :])[None]
    seg = cumulative.T[:, :, None] - cumulative.T[:, None, :]
    weight = jnp.exp(jnp.where(lower, seg, -jnp.inf)).reshape(GROUPS, reps, rows, rows)
    intersection_maps = jnp.einsum("tgn,sgn->gts", out_maps, in_maps, precision=HIGH_BOUND)
    score_matrix = weight * intersection_maps[:, None]
    scaled_values = payload_lines * delta.reshape(rows, GROUPS, reps)[..., None]
    final_output = jnp.einsum("jzlh,hjzc->ljzc", score_matrix, scaled_values, precision=HIGH_BOUND)
    incoming = jnp.einsum(
        "tgn,grpn->tgrp",
        out_maps,
        carried.reshape(GROUPS, reps, HEAD_DIM, STATE),
        precision=HIGH_BOUND,
    )
    final_output = (
        final_output + incoming * jnp.exp(cumulative).reshape(rows, GROUPS, reps)[..., None]
    )
    final_output = (
        final_output + skip_values.reshape(GROUPS, reps)[None, :, :, None] * payload_lines
    )
    gated = final_output.reshape(rows, GROUPS, -1) * jax.nn.silu(gates).reshape(rows, GROUPS, -1)
    normed = gated * lax.rsqrt(jnp.mean(gated * gated, axis=-1, keepdims=True) + 1e-05)
    return normed.reshape(rows, -1) * gain_values[None, :]


def combine(earlier, later):
    return (earlier[0] * later[0], later[0][:, None] * earlier[1] + later[1])


def shards(
    conv_input,
    gate_input,
    step_input,
    cotangent,
    conv_weight,
    conv_bias,
    step_bias,
    decay_log,
    skip_gain,
    norm_gain,
):
    local_rows = conv_input[0, 0]
    count = local_rows.shape[0]
    taps, initial_offset = (conv_weight[0], conv_bias[0])
    step_shift, damping_exponents = (step_bias[0], decay_log[0])
    skip_values, gain_values = (skip_gain[0], norm_gain[0])
    previous = shifted(local_rows[count - (CONV - 1) :], "ctx", 1)
    extended = jnp.concatenate([previous, local_rows], 0).astype(jnp.float32)
    gates = gate_input[0, 0].astype(jnp.float32)
    steps = step_input[0, 0].astype(jnp.float32)
    (state, total), state_pull = jax.vjp(
        fragment_condition, extended, steps, taps, initial_offset, step_shift, damping_exponents
    )
    decay = jnp.exp(total)
    flat_state = state.reshape(HEADS, HEAD_DIM * STATE)
    unity = (jnp.ones((HEADS,), jnp.float32), jnp.zeros((HEADS, HEAD_DIM * STATE), jnp.float32))

    def advance(index, current):
        return shifted(decay[:, None] * current + flat_state, "ctx", 1)

    incoming = lax.fori_loop(
        0, lax.axis_size("ctx") - 1, advance, jnp.zeros((HEADS, HEAD_DIM * STATE), jnp.float32)
    )
    carried = incoming.reshape(HEADS, HEAD_DIM, STATE)
    final_output, layer_pull = jax.vjp(
        shard_layer,
        extended,
        gates,
        steps,
        taps,
        initial_offset,
        step_shift,
        damping_exponents,
        skip_values,
        gain_values,
        carried,
    )
    forward = shifted(final_output.astype(jnp.bfloat16)[None, None], "section", 1)
    grads = layer_pull(cotangent[0, 0].astype(jnp.float32))
    carry_grad = grads[9].reshape(HEADS, HEAD_DIM * STATE)
    outgoing = prefix((decay, carry_grad), "ctx", combine, unity)[1]
    outgoing_grad = outgoing.reshape(HEADS, HEAD_DIM, STATE)
    total_grad = jnp.sum(outgoing_grad * carried, axis=(1, 2)) * decay
    extra = state_pull((outgoing_grad, total_grad))
    ext_grad = grads[0] + extra[0]
    step_grad = grads[2] + extra[1]
    param_terms = (
        grads[3] + extra[2],
        grads[4] + extra[3],
        grads[5] + extra[4],
        grads[6] + extra[5],
        grads[7],
        grads[8],
    )
    returned = shifted(ext_grad[: CONV - 1], "ctx", -1)
    own_grad = ext_grad[CONV - 1 :]
    row_grad = jnp.concatenate(
        [own_grad[: count - (CONV - 1)], own_grad[count - (CONV - 1) :] + returned], 0
    )
    backward = shifted(
        (
            row_grad.astype(jnp.bfloat16)[None, None],
            grads[1].astype(jnp.bfloat16)[None, None],
            step_grad.astype(jnp.bfloat16)[None, None],
        ),
        "section",
        -1,
    )
    summed = lax.psum(
        (
            param_terms[0],
            param_terms[1],
            param_terms[2],
            param_terms[3],
            param_terms[4],
            param_terms[5],
        ),
        ("ctx", "dp"),
    )
    return (
        forward,
        backward[0],
        backward[1],
        backward[2],
        summed[0][None],
        summed[1][None],
        summed[2][None],
        summed[3][None],
        summed[4][None],
        summed[5][None],
    )


MESH = pl.DeviceIdType.MESH
F32 = jnp.float32
BF16 = jnp.bfloat16
INNER = HEADS * HEAD_DIM
REPS = HEADS // GROUPS
WIDE = REPS * HEAD_DIM
MIX = WIDE + 2 * STATE
HALF = GROUPS // 2
NN = ((1,), (0,))
NT = ((1,), (1,))
TN = ((0,), (0,))


def split(a):
    high = a.astype(BF16)
    return high, (a - high.astype(F32)).astype(BF16)


def dot(a, b, dims):
    return lax.dot_general(a, b, (dims, ((), ())), preferred_element_type=F32)


def dot3(a, b, dims):
    return dot(a[0], b[0], dims) + (dot(a[0], b[1], dims) + dot(a[1], b[0], dims))


def group_columns(g):
    return (
        pl.multiple_of(g * WIDE, 128),
        pl.multiple_of(INNER + g * STATE, 128),
        pl.multiple_of(INNER + (GROUPS + g) * STATE, 128),
    )


def pair_kernel(
    conv_in, gate_in, step_in, cot_in, w_in, b_in, sb_in, dl_in, sk_in, ng_in,
    nxt, gconv, ggate, gstep, gtap, gcb, gsb, gdl, gsk, gng,
    w_ref, b_ref, sb_ref, dl_ref, sk_ref, ng_ref,
    uin, steps, token_rows, token_cols, upad, zpad, mix, dsl, ddt, drate, small,
    stage_c, stage_o, stage_s, step_parts, partial, final, relay,
    own_sem, xs_sem, xr_sem, st_sem, conv_sem, gate_sem, next_sem, dstep_sem,
    ps_sem, pr_sem, fin_sem, via_sem, relay_sem, par_sem, plane_sem, world_sem,
):
    core = lax.axis_index("ctx")
    sec = lax.axis_index("section")
    dp = lax.axis_index("dp")
    nsec = lax.axis_size("section")
    ndp = lax.axis_size("dp")
    tok = conv_in.shape[2]
    seq = 2 * tok
    other = 1 - core

    def place(c, s, d):
        return {"ctx": c, "section": s, "dp": d}

    def remote(src, dst, send, recv, c, s, d):
        return pltpu.make_async_remote_copy(
            src_ref=src, dst_ref=dst, send_sem=send, recv_sem=recv,
            device_id=place(c, s, d), device_id_type=MESH,
        )

    after = lax.rem(sec + 1, nsec)
    before = lax.rem(sec + nsec - 1, nsec)
    barrier = pltpu.get_barrier_semaphore()

    def greet(c, s, d):
        pl.semaphore_signal(barrier, inc=1, device_id=place(c, s, d), device_id_type=MESH)

    for c in range(2):
        for s in range(1, 4):

            @pl.when(jnp.logical_or(sec != s, core != c))
            def _():
                greet(c, s, dp)

    def pieces(g):
        xc, bc, cc = group_columns(g)
        return (
            (conv_in.at[0, 0, :, pl.ds(xc, WIDE)], 0, WIDE),
            (conv_in.at[0, 0, :, pl.ds(bc, STATE)], WIDE, STATE),
            (conv_in.at[0, 0, :, pl.ds(cc, STATE)], WIDE + STATE, STATE),
            (gate_in.at[0, 0, :, pl.ds(xc, WIDE)], MIX, WIDE),
            (cot_in.at[0, 0, :, pl.ds(xc, WIDE)], MIX + WIDE, WIDE),
        )

    mine = pl.ds(pl.multiple_of(core * tok, tok), tok)
    theirs = pl.ds(pl.multiple_of(other * tok, tok), tok)
    own_step = pltpu.make_async_copy(step_in.at[0, 0], steps.at[core], st_sem.at[0])
    own_step.start()

    def fetch(j, _):
        for src, off, width in pieces(core * HALF + j):
            pltpu.make_async_copy(
                src, uin.at[j, mine, pl.ds(off, width)], own_sem.at[j]
            ).start()
        return 0

    fetch(0, 0)
    params = [
        pltpu.make_async_copy(src, dst, par_sem.at[at])
        for at, (src, dst) in enumerate((
            (sb_in, sb_ref), (dl_in, dl_ref), (w_in, w_ref),
            (b_in, b_ref), (sk_in, sk_ref), (ng_in, ng_ref),
        ))
    ]
    for copy in params:
        copy.start()
    lax.fori_loop(1, HALF, fetch, 0)
    partial[dp] = jnp.zeros(partial.shape[1:], F32)
    upad[0:8, :] = jnp.zeros((8, MIX), F32)
    zpad[seq : seq + 8, :] = jnp.zeros((8, MIX), F32)
    for ref in (token_rows, ddt, drate, small):
        ref[...] = jnp.zeros_like(ref)

    @pl.when(sec > 0)
    def _():
        pl.semaphore_wait(barrier, 7)

    @pl.when(sec == 1)
    def _():
        pl.semaphore_signal(
            plane_sem, inc=1, device_id=place(core, 0, dp), device_id_type=MESH
        )
        for k in range(1, ndp):
            greet(core, 0, lax.rem(dp + k, ndp))

    @pl.when(sec == 0)
    def _():
        pl.semaphore_wait(plane_sem, 1)

    step_copy = remote(
        step_in.at[0, 0], steps.at[core], st_sem.at[1], st_sem.at[2], other, sec, dp
    )
    step_copy.start()

    def exchange(j, _):
        for src, off, width in pieces(other * HALF + j):
            remote(
                src, uin.at[j, mine, pl.ds(off, width)], xs_sem.at[j], xr_sem.at[j], other, sec, dp
            ).start()
        return 0

    lax.fori_loop(0, HALF, exchange, 0)
    for copy in params:
        copy.wait()

    def token_terms():
        own_step.wait()
        step_copy.wait()
        diagonal = lax.broadcasted_iota(jnp.int32, (HEADS, HEADS), 0) == lax.broadcasted_iota(
            jnp.int32, (HEADS, HEADS), 1
        )

        def upright(ref):
            return jnp.sum(jnp.where(diagonal, ref[...], 0.0), axis=1, keepdims=True)

        raw = jnp.concatenate([steps[0].astype(F32), steps[1].astype(F32)], axis=1)
        raw = raw + upright(sb_ref)
        delta = jnp.maximum(raw, 0.0) + jnp.log1p(jnp.exp(-jnp.abs(raw)))
        rate = delta * (-jnp.exp(upright(dl_ref)))
        rows2 = lax.broadcasted_iota(jnp.int32, (seq, seq), 0)
        cols2 = lax.broadcasted_iota(jnp.int32, (seq, seq), 1)
        ones_up = jnp.where(rows2 <= cols2, 1.0, 0.0).astype(BF16)
        r_hi, r_rest = rate.astype(BF16), rate - rate.astype(BF16).astype(F32)
        r_mid, r_lo = split(r_rest)
        cumulative = dot(r_hi, ones_up, NN) + (dot(r_mid, ones_up, NN) + dot(r_lo, ones_up, NN))
        token_rows[0:HEADS, :] = delta
        token_rows[HEADS : 2 * HEADS, :] = cumulative
        token_rows[2 * HEADS : 3 * HEADS, :] = jax.nn.sigmoid(raw)
        token_rows[3 * HEADS : 4 * HEADS, :] = rate
        token_cols[...] = token_rows[...].T

    def group(j, _):
        g = core * HALF + j
        cols = group_columns(g)
        blocks = [(0, cols[0])]
        for base, col in ((WIDE, cols[1]), (WIDE + STATE, cols[2])):
            for part in range(STATE // 128):
                blocks.append((base + part * 128, pl.multiple_of(col + part * 128, 128)))

        def conv_rows(start, count, fresh):
            for off, col in blocks:
                here = slice(off, off + 128)
                if fresh:
                    upad[pl.ds(pl.multiple_of(start + 8, 8), count), here] = uin[
                        j, pl.ds(start, count), here
                    ].astype(F32)
                window = upad[pl.ds(start, count + 8), here]
                z = b_ref[:, pl.ds(col, 128)] + w_ref[0, 3:4, pl.ds(col, 128)] * window[8:]
                for k in range(CONV - 1):
                    z = z + w_ref[0, pl.ds(k, 1), pl.ds(col, 128)] * pltpu.roll(window, 3 - k, 0)[8:]
                s = jax.nn.sigmoid(z)
                mix[pl.ds(start, count), here] = z * s
                dsl[pl.ds(start, count), here] = s * (1.0 + z * (1.0 - s))

        pltpu.make_async_copy(uin.at[j, mine], uin.at[j, mine], own_sem.at[j]).wait()
        conv_rows(pl.multiple_of(core * tok, tok), tok, True)

        @pl.when(j == 0)
        def _():
            token_terms()

        remote(uin.at[j, mine], uin.at[j, theirs], xs_sem.at[j], xr_sem.at[j], other, sec, dp).wait()
        conv_rows(pl.multiple_of(other * tok, tok), tok, True)
        conv_rows(tok, 8, False)

        lane = lax.broadcasted_iota(jnp.int32, (seq, 128), 1)
        lane1 = lax.broadcasted_iota(jnp.int32, (1, 128), 1)
        lane16 = lax.broadcasted_iota(jnp.int32, (1, HEADS), 1)
        row = lax.broadcasted_iota(jnp.int32, (seq, seq), 0)
        column = lax.broadcasted_iota(jnp.int32, (seq, seq), 1)
        first = lane < HEAD_DIM

        def pick(at):
            return jnp.sum(jnp.where(lane == at, token_cols[...], 0.0), axis=1, keepdims=True)

        def pick1(ref, h):
            return jnp.sum(jnp.where(lane16 == h, ref[...], 0.0), axis=1, keepdims=True)

        x = mix[:, 0:WIDE]
        bmap = split(mix[:, WIDE : WIDE + STATE])
        cmap = split(mix[:, WIDE + STATE : MIX])
        h0 = g * REPS
        dt2 = jnp.where(first, pick(h0), pick(h0 + 1))
        skip2 = jnp.where(first[0:1], pick1(sk_ref, h0), pick1(sk_ref, h0 + 1))
        xs = x * dt2
        xs_p = split(xs)
        scores = dot3(cmap, bmap, NT)
        decay, mixed, ys = [], [], []
        for r in range(REPS):
            seg = pick(HEADS + h0 + r) - token_rows[pl.ds(HEADS + h0 + r, 1), :]
            w = jnp.exp(jnp.where(row >= column, seg, -jnp.inf))
            a = scores * w
            a_p = split(a)
            decay.append(w)
            mixed.append((a, a_p))
            ys.append(dot3(a_p, xs_p, NN))
        y = jnp.where(first, ys[0], ys[1]) + skip2 * x
        gate = uin[j, :, MIX : MIX + WIDE].astype(F32)
        cot = uin[j, :, MIX + WIDE : MIX + 2 * WIDE].astype(F32)
        gain = ng_ref[:, pl.ds(cols[0], WIDE)]
        s = jax.nn.sigmoid(gate)
        act = gate * s
        gated = y * act
        scale = lax.rsqrt(jnp.mean(gated * gated, axis=1, keepdims=True) + 1e-05)
        normed = gated * scale
        stage_o[j, :, 0:WIDE] = (normed * gain).astype(BF16)
        dn = cot * gain
        dgated = scale * (dn - normed * jnp.mean(dn * normed, axis=1, keepdims=True))
        dy = dgated * act
        stage_o[j, :, WIDE : 2 * WIDE] = (dgated * y * (s * (1.0 + gate * (1.0 - s)))).astype(BF16)

        odd = lax.rem(j, 2) == 1

        def send_half(base, t, dst, done, landed, s):
            remote(
                stage_o.at[j, pl.ds(t * tok, tok), pl.ds(base, WIDE)], dst, done, landed, t, s, dp
            ).start()

        @pl.when(jnp.logical_and(sec < nsec - 1, jnp.logical_not(jnp.logical_and(sec == 1, odd))))
        def _():
            for t in range(2):
                send_half(
                    0, t, nxt.at[0, 0, :, pl.ds(cols[0], WIDE)],
                    next_sem.at[0], next_sem.at[1], sec + 1,
                )

        @pl.when(jnp.logical_and(sec == 1, odd))
        def _():
            slot = core * (HALF // 2) + j // 2
            for t in range(2):
                send_half(0, t, relay.at[slot], next_sem.at[0], relay_sem.at[slot], 3)

        @pl.when(jnp.logical_or(sec == 1, sec == 3))
        def _():
            for t in range(2):
                send_half(
                    WIDE, t, ggate.at[0, 0, :, pl.ds(cols[0], WIDE)],
                    gate_sem.at[0], gate_sem.at[1], sec - 1,
                )

        @pl.when(sec == 2)
        def _():
            slot = core * HALF + j
            for t in range(2):
                send_half(WIDE, t, relay.at[slot], gate_sem.at[0], relay_sem.at[slot], 0)

        partial[dp, j, 5:6, 0:WIDE] = jnp.sum(cot * normed, axis=0, keepdims=True)
        dyx = jnp.sum(dy * x, axis=0, keepdims=True)
        dscore = jnp.zeros((seq, seq), F32)
        dy_p = split(dy)
        das = []
        for r in range(REPS):
            own = first if r == 0 else jnp.logical_not(first)
            da = dot3(split(jnp.where(own, dy, 0.0)), xs_p, NT)
            das.append(da)
            dscore = dscore + da * decay[r]
        ds_p = split(dscore)

        def conv_back(off, width, start):
            for part in range(width // 128):
                here = slice(off + part * 128, off + part * 128 + 128)
                col = pl.multiple_of(start + part * 128, 128)
                dz = zpad[0:seq, here]
                du = jnp.zeros((seq, 128), F32)
                for k in range(CONV):
                    du = du + w_ref[0, pl.ds(k, 1), pl.ds(col, 128)] * zpad[3 - k : 3 - k + seq, here]
                    partial[dp, j, pl.ds(k, 1), here] = jnp.sum(
                        dz * upad[5 + k : 5 + k + seq, here], axis=0, keepdims=True
                    )
                partial[dp, j, pl.ds(4, 1), here] = jnp.sum(dz, axis=0, keepdims=True)
                stage_c[j, :, here] = du.astype(BF16)

            @pl.when(sec > 0)
            def _():
                for t in range(2):
                    remote(
                        stage_c.at[j, pl.ds(t * tok, tok), pl.ds(off, width)],
                        gconv.at[0, 0, :, pl.ds(start, width)],
                        conv_sem.at[0], conv_sem.at[1], t, sec - 1, dp,
                    ).start()

        zpad[0:seq, WIDE + STATE : MIX] = dot3(ds_p, bmap, NN) * dsl[:, WIDE + STATE : MIX]
        conv_back(WIDE + STATE, STATE, cols[2])
        zpad[0:seq, WIDE : WIDE + STATE] = dot3(ds_p, cmap, TN) * dsl[:, WIDE : WIDE + STATE]
        conv_back(WIDE, STATE, cols[1])
        dxs = jnp.where(first, dot3(mixed[0][1], dy_p, TN), dot3(mixed[1][1], dy_p, TN))
        zpad[0:seq, 0:WIDE] = (skip2 * dy + dxs * dt2) * dsl[:, 0:WIDE]
        conv_back(0, WIDE, cols[0])
        upper = jnp.where(row <= column, 1.0, 0.0).astype(BF16)
        dxx = dxs * x
        for r in range(REPS):
            own = first if r == 0 else jnp.logical_not(first)
            p = split(das[r] * mixed[r][0])
            later = dot(upper, p[0], NN) + dot(upper, p[1], NN)
            dr = jnp.sum(jnp.where(row > column, later, 0.0), axis=1, keepdims=True)
            drate[...] += jnp.where(lane == h0 + r, dr, 0.0)
            total = jnp.sum(jnp.where(own[0:1], dyx, 0.0), axis=1, keepdims=True)
            small[2:3, :] += jnp.where(lane1 == h0 + r, total, 0.0)
            dd = jnp.sum(jnp.where(own, dxx, 0.0), axis=1, keepdims=True)
            ddt[...] += jnp.where(lane == h0 + r, dd, 0.0)

        @pl.when(jnp.logical_and(j == 0, sec == 0))
        def _():
            pl.semaphore_wait(barrier, ndp - 1)
            for s in range(1, 4):
                pl.semaphore_signal(
                    world_sem, inc=1, device_id=place(core, s, dp), device_id_type=MESH
                )

        @pl.when(jnp.logical_and(j == 0, sec > 0))
        def _():
            pl.semaphore_wait(world_sem, 1)

        for k in range(1, ndp):
            to = lax.rem(dp + k, ndp)
            remote(
                partial.at[dp, j], partial.at[dp, j], ps_sem.at[to], pr_sem.at[dp], core, sec, to
            ).start()
        return 0

    lax.fori_loop(0, HALF, group, 0)

    def pass_on(slot, g, out, landed, s):
        part = relay.at[slot]
        remote(part, part, via_sem.at[0], relay_sem.at[slot], core, s, dp).wait_recv()
        remote(
            part, out.at[0, 0, :, pl.ds(g * WIDE, WIDE)], via_sem.at[0], landed, core, s, dp
        ).start()

    @pl.when(sec == 0)
    def _():
        for g in range(GROUPS):
            pass_on(g, g, ggate, gate_sem.at[1], 1)

    @pl.when(sec == 3)
    def _():
        for at in range(GROUPS // 2):
            pass_on(at, 2 * at + 1, nxt, next_sem.at[1], 2)

    @pl.when(sec == 0)
    def _():
        nxt[...] = jnp.zeros_like(nxt)

    @pl.when(sec == nsec - 1)
    def _():
        gconv[...] = jnp.zeros_like(gconv)
        ggate[...] = jnp.zeros_like(ggate)
        gstep[...] = jnp.zeros_like(gstep)

    damp = jnp.exp(dl_ref[...])
    dr16 = drate[:, 0:HEADS]
    dstep = (ddt[:, 0:HEADS] - dr16 * damp) * token_cols[:, 2 * HEADS : 3 * HEADS]
    small[0:1, 0:HEADS] = jnp.sum(dstep, axis=0, keepdims=True)
    small[1:2, 0:HEADS] = jnp.sum(
        dr16 * token_cols[:, 3 * HEADS : 4 * HEADS], axis=0, keepdims=True
    )
    drate[:, 0:HEADS] = dstep
    turned = drate[...].T
    for t in range(2):
        stage_s[t] = turned[0:HEADS, t * tok : (t + 1) * tok].astype(BF16)

    @pl.when(sec > 0)
    def _():
        for t in range(2):
            remote(
                stage_s.at[t], step_parts.at[core],
                dstep_sem.at[2], dstep_sem.at[core], t, sec - 1, dp,
            ).start()

    partial[dp, HALF, :, 0:128] = small[...]
    for k in range(1, ndp):
        to = lax.rem(dp + k, ndp)
        remote(
            partial.at[dp, HALF], partial.at[dp, HALF], ps_sem.at[to], pr_sem.at[dp], core, sec, to
        ).start()
    for k in range(1, ndp):
        to = lax.rem(dp + k, ndp)
        remote(partial.at[dp], partial.at[to], ps_sem.at[to], pr_sem.at[to], core, sec, to).wait()
    total = partial[0]
    for k in range(1, ndp):
        total = total + partial[k]
    final[core] = total
    halves = remote(final.at[core], final.at[core], fin_sem.at[0], fin_sem.at[1], other, sec, dp)
    halves.start()
    remote(final.at[core], final.at[other], fin_sem.at[0], fin_sem.at[1], other, sec, dp).wait()
    for g in range(GROUPS):
        c, j = g // HALF, g % HALF
        gng[0:1, g * WIDE : (g + 1) * WIDE] = final[c, j, 5:6, 0:WIDE]
        for off, width, col in (
            (0, WIDE, g * WIDE),
            (WIDE, STATE, INNER + g * STATE),
            (WIDE + STATE, STATE, INNER + (GROUPS + g) * STATE),
        ):
            gtap[0, :, col : col + width] = final[c, j, 0:CONV, off : off + width]
            gcb[0:1, col : col + width] = final[c, j, CONV : CONV + 1, off : off + width]
    for at, ref in enumerate((gsb, gdl, gsk)):
        ref[...] = final[0, HALF, at : at + 1, 0:HEADS] + final[1, HALF, at : at + 1, 0:HEADS]

    @pl.when(sec < nsec - 1)
    def _():
        for c in range(2):
            part = step_parts.at[c]
            remote(part, part, dstep_sem.at[2], dstep_sem.at[c], core, sec + 1, dp).wait_recv()
        gstep[0, 0] = (step_parts[0].astype(F32) + step_parts[1].astype(F32)).astype(BF16)

    @pl.when(sec == 0)
    def _():
        remote(relay, relay, via_sem.at[0], relay_sem.at[0], core, 1, dp).wait_send()

    @pl.when(sec > 0)
    def _():
        low = sec - 1
        remote(stage_c, stage_c, conv_sem.at[0], conv_sem.at[1], core, low, dp).wait_send()
        half_o = stage_o.at[:, :, pl.ds(0, WIDE)]
        remote(half_o, half_o, gate_sem.at[0], gate_sem.at[1], core, low, dp).wait_send()
        remote(stage_s, stage_s, dstep_sem.at[2], dstep_sem.at[0], core, low, dp).wait_send()
        remote(
            nxt.at[0, 0], nxt.at[0, 0], next_sem.at[0], next_sem.at[1], core, low, dp
        ).wait_recv()

    @pl.when(sec == nsec - 1)
    def _():
        used = relay.at[pl.ds(0, GROUPS // 2)]
        remote(used, used, via_sem.at[0], relay_sem.at[0], core, 2, dp).wait_send()

    @pl.when(sec < nsec - 1)
    def _():
        high = sec + 1
        half_o = stage_o.at[:, :, pl.ds(0, WIDE)]
        remote(half_o, half_o, next_sem.at[0], next_sem.at[1], core, high, dp).wait_send()
        whole = ggate.at[0, 0]
        remote(whole, whole, gate_sem.at[0], gate_sem.at[1], core, high, dp).wait_recv()
        whole = gconv.at[0, 0]
        remote(whole, whole, conv_sem.at[0], conv_sem.at[1], core, high, dp).wait_recv()


def finish_kernel(*refs):
    count = len(refs) // 2
    sem = refs[-1]
    copies = [pltpu.make_async_copy(refs[i], refs[count + i], sem.at[i]) for i in range(count)]
    for copy in copies:
        copy.start()
    for copy in copies:
        copy.wait()


def paired(
    conv_input, gate_input, step_input, cotangent, conv_weight,
    conv_bias, step_bias, decay_log, skip_gain, norm_gain,
):
    tok = conv_input.shape[2]
    seq = 2 * tok
    ndp = lax.axis_size("dp")
    hbm = pl.BlockSpec(memory_space=pl.ANY)
    vmem = pl.BlockSpec(memory_space=pltpu.VMEM)
    scratch = [
        pltpu.VMEM(conv_weight.shape, F32),
        pltpu.VMEM(conv_bias.shape, F32),
        pltpu.VMEM(step_bias.shape, F32),
        pltpu.VMEM(decay_log.shape, F32),
        pltpu.VMEM(skip_gain.shape, F32),
        pltpu.VMEM(norm_gain.shape, F32),
        pltpu.VMEM((HALF, seq, MIX + 2 * WIDE), BF16),
        pltpu.VMEM((2, HEADS, tok), BF16),
        pltpu.VMEM((128, seq), F32),
        pltpu.VMEM((seq, 128), F32),
        pltpu.VMEM((seq + 8, MIX), F32),
        pltpu.VMEM((seq + 8, MIX), F32),
        pltpu.VMEM((seq, MIX), F32),
        pltpu.VMEM((seq, MIX), F32),
        pltpu.VMEM((seq, 128), F32),
        pltpu.VMEM((seq, 128), F32),
        pltpu.VMEM((8, 128), F32),
        pltpu.VMEM((HALF, seq, MIX), BF16),
        pltpu.VMEM((HALF, seq, 2 * WIDE), BF16),
        pltpu.VMEM((2, HEADS, tok), BF16),
        pltpu.VMEM((2, HEADS, tok), BF16),
        pltpu.VMEM((ndp, HALF + 1, 8, MIX), F32),
        pltpu.VMEM((2, HALF + 1, 8, MIX), F32),
        pltpu.VMEM((GROUPS, tok, WIDE), BF16),
        pltpu.SemaphoreType.DMA((HALF,)),
        pltpu.SemaphoreType.DMA((HALF,)),
        pltpu.SemaphoreType.DMA((HALF,)),
        pltpu.SemaphoreType.DMA((3,)),
        pltpu.SemaphoreType.DMA((2,)),
        pltpu.SemaphoreType.DMA((2,)),
        pltpu.SemaphoreType.DMA((2,)),
        pltpu.SemaphoreType.DMA((3,)),
        pltpu.SemaphoreType.DMA((ndp,)),
        pltpu.SemaphoreType.DMA((ndp,)),
        pltpu.SemaphoreType.DMA((2,)),
        pltpu.SemaphoreType.DMA((1,)),
        pltpu.SemaphoreType.DMA((GROUPS,)),
        pltpu.SemaphoreType.DMA((6,)),
        pltpu.SemaphoreType.REGULAR,
        pltpu.SemaphoreType.REGULAR,
    ]
    turned = jnp.swapaxes(step_input, 2, 3)
    shapes = [
        (gate_input.shape, BF16),
        (conv_input.shape, BF16),
        (gate_input.shape, BF16),
        (turned.shape, BF16),
        (conv_weight.shape, F32),
        (conv_bias.shape, F32),
        (step_bias.shape, F32),
        (decay_log.shape, F32),
        (skip_gain.shape, F32),
        (norm_gain.shape, F32),
    ]
    inputs = [
        pltpu.with_memory_space_constraint(a, pltpu.HBM)
        for a in (
            conv_input, gate_input, turned, cotangent, conv_weight,
            conv_bias, step_bias, decay_log, skip_gain, norm_gain,
        )
    ]
    sent = pl.pallas_call(
        pair_kernel,
        name="mixer_tick",
        in_specs=[hbm] * 10,
        out_specs=[vmem] * 10,
        out_shape=[pltpu.VMEM(shape, kind) for shape, kind in shapes],
        scratch_shapes=scratch,
        compiler_params=pltpu.CompilerParams(
            collective_id=0, has_side_effects=True, vmem_limit_bytes=24 * 1024 * 1024
        ),
    )(*inputs)
    done = pl.pallas_call(
        finish_kernel,
        name="mixer_finish",
        in_specs=[vmem] * 10,
        out_specs=[hbm] * 10,
        out_shape=[jax.ShapeDtypeStruct(shape, kind) for shape, kind in shapes],
        scratch_shapes=[pltpu.SemaphoreType.DMA((10,))],
        compiler_params=pltpu.CompilerParams(vmem_limit_bytes=1024 * 1024),
    )(*sent)
    return tuple(done[:3]) + (jnp.swapaxes(done[3], 2, 3),) + tuple(done[4:])


def solution(mesh):
    in_specs = (
        P("section", "dp", "ctx", None),
        P("section", "dp", "ctx", None),
        P("section", "dp", "ctx", None),
        P("section", "dp", "ctx", None),
        P("section", None, None),
        P("section", None),
        P("section", None),
        P("section", None),
        P("section", None),
        P("section", None),
    )
    out_specs = (
        P("section", "dp", "ctx", None),
        P("section", "dp", "ctx", None),
        P("section", "dp", "ctx", None),
        P("section", "dp", "ctx", None),
        P("section", None, None),
        P("section", None),
        P("section", None),
        P("section", None),
        P("section", None),
        P("section", None),
    )
    body = paired if (mesh.shape["ctx"], mesh.shape["section"]) == (2, 4) else shards
    return jax.shard_map(body, mesh=mesh, in_specs=in_specs, out_specs=out_specs, check_vma=False)
```

```python
import functools
import jax
import jax.numpy as jnp
from jax import lax
from jax.experimental import pallas as pl
from jax.experimental.pallas import tpu as pltpu
from jax.sharding import PartitionSpec as P

HEADS = 16
HEAD_DIM = 64
STATE = 256
GROUPS = 8
CONV = 4


HIGH_BOUND = lax.Precision.HIGHEST


def shifted(block, axis, distance):
    devices = range(lax.axis_size(axis))
    route = [(i - distance, i) for i in devices if i - distance in devices]
    return lax.ppermute(block, axis, route)


def prefix(part, axis, combine, identity):
    count = lax.axis_size(axis)
    place = lax.axis_index(axis)
    ahead = count - 1 - place
    gathered = jax.tree.map(lambda a: lax.all_gather(a, axis), part)
    state = jax.tree.map(lambda a, e: jnp.zeros_like(a) + jnp.asarray(e, a.dtype), part, identity)

    def one(turn, state):
        source = count - 1 - turn
        return combine(
            state, jax.tree.map(lambda a: lax.dynamic_index_in_dim(a, source, 0, False), gathered)
        )

    return lax.fori_loop(0, ahead, one, state)


def conv_mix(extended, taps, initial_offset):
    rows = extended.shape[0] - (CONV - 1)
    total = initial_offset[None, :]
    for tap in range(CONV):
        total = total + taps[tap][None, :] * extended[tap : tap + rows]
    return jax.nn.silu(total)


def split_mix(mixed, steps, step_shift, damping_exponents):
    rows = mixed.shape[0]
    inner = HEADS * HEAD_DIM
    payload_lines = mixed[:, :inner].reshape(rows, GROUPS, HEADS // GROUPS, HEAD_DIM)
    in_maps = mixed[:, inner : inner + GROUPS * STATE].reshape(rows, GROUPS, STATE)
    out_maps = mixed[:, inner + GROUPS * STATE :].reshape(rows, GROUPS, STATE)
    delta = jax.nn.softplus(steps + step_shift[None, :])
    upto = jnp.tril(jnp.ones((rows, rows), jnp.float32))
    rates = delta * (-jnp.exp(damping_exponents))[None, :]
    cumulative = jnp.dot(upto, rates, precision=HIGH_BOUND)
    return (payload_lines, in_maps, out_maps, delta, cumulative)


def fragment_condition(extended, steps, taps, initial_offset, step_shift, damping_exponents):
    payload_lines, in_maps, out_maps, delta, cumulative = split_mix(
        conv_mix(extended, taps, initial_offset), steps, step_shift, damping_exponents
    )
    rows = payload_lines.shape[0]
    total = cumulative[-1]
    weight = (jnp.exp(total[None, :] - cumulative) * delta).reshape(rows, GROUPS, HEADS // GROUPS)
    state = jnp.einsum(
        "tgrp,tgn->grpn", payload_lines * weight[..., None], in_maps, precision=HIGH_BOUND
    )
    return (state.reshape(HEADS, HEAD_DIM, STATE), total)


def shard_layer(
    extended,
    gates,
    steps,
    taps,
    initial_offset,
    step_shift,
    damping_exponents,
    skip_values,
    gain_values,
    carried,
):
    payload_lines, in_maps, out_maps, delta, cumulative = split_mix(
        conv_mix(extended, taps, initial_offset), steps, step_shift, damping_exponents
    )
    rows = payload_lines.shape[0]
    reps = HEADS // GROUPS
    lower = (jnp.arange(rows)[:, None] >= jnp.arange(rows)[None, :])[None]
    seg = cumulative.T[:, :, None] - cumulative.T[:, None, :]
    weight = jnp.exp(jnp.where(lower, seg, -jnp.inf)).reshape(GROUPS, reps, rows, rows)
    intersection_maps = jnp.einsum("tgn,sgn->gts", out_maps, in_maps, precision=HIGH_BOUND)
    score_matrix = weight * intersection_maps[:, None]
    scaled_values = payload_lines * delta.reshape(rows, GROUPS, reps)[..., None]
    final_output = jnp.einsum("jzlh,hjzc->ljzc", score_matrix, scaled_values, precision=HIGH_BOUND)
    incoming = jnp.einsum(
        "tgn,grpn->tgrp",
        out_maps,
        carried.reshape(GROUPS, reps, HEAD_DIM, STATE),
        precision=HIGH_BOUND,
    )
    final_output = (
        final_output + incoming * jnp.exp(cumulative).reshape(rows, GROUPS, reps)[..., None]
    )
    final_output = (
        final_output + skip_values.reshape(GROUPS, reps)[None, :, :, None] * payload_lines
    )
    gated = final_output.reshape(rows, GROUPS, -1) * jax.nn.silu(gates).reshape(rows, GROUPS, -1)
    normed = gated * lax.rsqrt(jnp.mean(gated * gated, axis=-1, keepdims=True) + 1e-05)
    return normed.reshape(rows, -1) * gain_values[None, :]


def combine(earlier, later):
    return (earlier[0] * later[0], later[0][:, None] * earlier[1] + later[1])


def shards(
    conv_input,
    gate_input,
    step_input,
    cotangent,
    conv_weight,
    conv_bias,
    step_bias,
    decay_log,
    skip_gain,
    norm_gain,
):
    local_rows = conv_input[0, 0]
    count = local_rows.shape[0]
    taps, initial_offset = (conv_weight[0], conv_bias[0])
    step_shift, damping_exponents = (step_bias[0], decay_log[0])
    skip_values, gain_values = (skip_gain[0], norm_gain[0])
    previous = shifted(local_rows[count - (CONV - 1) :], "ctx", 1)
    extended = jnp.concatenate([previous, local_rows], 0).astype(jnp.float32)
    gates = gate_input[0, 0].astype(jnp.float32)
    steps = step_input[0, 0].astype(jnp.float32)
    (state, total), state_pull = jax.vjp(
        fragment_condition, extended, steps, taps, initial_offset, step_shift, damping_exponents
    )
    decay = jnp.exp(total)
    flat_state = state.reshape(HEADS, HEAD_DIM * STATE)
    unity = (jnp.ones((HEADS,), jnp.float32), jnp.zeros((HEADS, HEAD_DIM * STATE), jnp.float32))

    def advance(index, current):
        return shifted(decay[:, None] * current + flat_state, "ctx", 1)

    incoming = lax.fori_loop(
        0, lax.axis_size("ctx") - 1, advance, jnp.zeros((HEADS, HEAD_DIM * STATE), jnp.float32)
    )
    carried = incoming.reshape(HEADS, HEAD_DIM, STATE)
    final_output, layer_pull = jax.vjp(
        shard_layer,
        extended,
        gates,
        steps,
        taps,
        initial_offset,
        step_shift,
        damping_exponents,
        skip_values,
        gain_values,
        carried,
    )
    forward = shifted(final_output.astype(jnp.bfloat16)[None, None], "section", 1)
    grads = layer_pull(cotangent[0, 0].astype(jnp.float32))
    carry_grad = grads[9].reshape(HEADS, HEAD_DIM * STATE)
    outgoing = prefix((decay, carry_grad), "ctx", combine, unity)[1]
    outgoing_grad = outgoing.reshape(HEADS, HEAD_DIM, STATE)
    total_grad = jnp.sum(outgoing_grad * carried, axis=(1, 2)) * decay
    extra = state_pull((outgoing_grad, total_grad))
    ext_grad = grads[0] + extra[0]
    step_grad = grads[2] + extra[1]
    param_terms = (
        grads[3] + extra[2],
        grads[4] + extra[3],
        grads[5] + extra[4],
        grads[6] + extra[5],
        grads[7],
        grads[8],
    )
    returned = shifted(ext_grad[: CONV - 1], "ctx", -1)
    own_grad = ext_grad[CONV - 1 :]
    row_grad = jnp.concatenate(
        [own_grad[: count - (CONV - 1)], own_grad[count - (CONV - 1) :] + returned], 0
    )
    backward = shifted(
        (
            row_grad.astype(jnp.bfloat16)[None, None],
            grads[1].astype(jnp.bfloat16)[None, None],
            step_grad.astype(jnp.bfloat16)[None, None],
        ),
        "section",
        -1,
    )
    summed = lax.psum(
        (
            param_terms[0],
            param_terms[1],
            param_terms[2],
            param_terms[3],
            param_terms[4],
            param_terms[5],
        ),
        ("ctx", "dp"),
    )
    return (
        forward,
        backward[0],
        backward[1],
        backward[2],
        summed[0][None],
        summed[1][None],
        summed[2][None],
        summed[3][None],
        summed[4][None],
        summed[5][None],
    )


MESH = pl.DeviceIdType.MESH
F32 = jnp.float32
BF16 = jnp.bfloat16
INNER = HEADS * HEAD_DIM
REPS = HEADS // GROUPS
WIDE = REPS * HEAD_DIM
MIX = WIDE + 2 * STATE
HALF = GROUPS // 2
NN = ((1,), (0,))
NT = ((1,), (1,))
TN = ((0,), (0,))


def split(a):
    high = a.astype(BF16)
    return high, (a - high.astype(F32)).astype(BF16)


def dot(a, b, dims):
    return lax.dot_general(a, b, (dims, ((), ())), preferred_element_type=F32)


def dot3(a, b, dims):
    return dot(a[0], b[0], dims) + (dot(a[0], b[1], dims) + dot(a[1], b[0], dims))


def group_columns(g):
    return (
        pl.multiple_of(g * WIDE, 128),
        pl.multiple_of(INNER + g * STATE, 128),
        pl.multiple_of(INNER + (GROUPS + g) * STATE, 128),
    )


def pair_kernel(
    conv_in, gate_in, step_in, cot_in, w_in, b_in, sb_in, dl_in, sk_in, ng_in,
    nxt, gconv, ggate, gstep, gtap, gcb, gsb, gdl, gsk, gng,
    w_ref, b_ref, sb_ref, dl_ref, sk_ref, ng_ref,
    uin, steps, token_rows, token_cols, upad, zpad, mix, dsl, ddt, drate, small,
    stage_c, stage_o, stage_s, step_parts, partial, final, relay, small_out, small_in,
    own_sem, xs_sem, xr_sem, st_sem, conv_sem, gate_sem, next_sem, dstep_sem,
    ps_sem, pr_sem, fin_sem, via_sem, relay_sem, par_sem, plane_sem, world_sem,
    ship_sem, ship_recv, hand_sem,
):
    core = lax.axis_index("ctx")
    sec = lax.axis_index("section")
    dp = lax.axis_index("dp")
    nsec = lax.axis_size("section")
    ndp = lax.axis_size("dp")
    tok = conv_in.shape[2]
    seq = 2 * tok
    other = 1 - core
    gives = (sec + nsec - 1) // nsec
    takes = 1 - sec // (nsec - 1)
    donor = core * gives
    helper = core * takes
    own_groups = HALF - donor
    last = GROUPS - 1
    halves_of = 4 * HEADS

    def place(c, s, d):
        return {"ctx": c, "section": s, "dp": d}

    def remote(src, dst, send, recv, c, s, d):
        return pltpu.make_async_remote_copy(
            src_ref=src, dst_ref=dst, send_sem=send, recv_sem=recv,
            device_id=place(c, s, d), device_id_type=MESH,
        )

    after = lax.rem(sec + 1, nsec)
    before = lax.rem(sec + nsec - 1, nsec)
    barrier = pltpu.get_barrier_semaphore()

    def greet(c, s, d):
        pl.semaphore_signal(barrier, inc=1, device_id=place(c, s, d), device_id_type=MESH)

    for c in range(2):
        for s in range(1, 4):

            @pl.when(jnp.logical_or(sec != s, core != c))
            def _():
                greet(c, s, dp)

    def pieces(g):
        xc, bc, cc = group_columns(g)
        return (
            (conv_in.at[0, 0, :, pl.ds(xc, WIDE)], 0, WIDE),
            (conv_in.at[0, 0, :, pl.ds(bc, STATE)], WIDE, STATE),
            (conv_in.at[0, 0, :, pl.ds(cc, STATE)], WIDE + STATE, STATE),
            (gate_in.at[0, 0, :, pl.ds(xc, WIDE)], MIX, WIDE),
            (cot_in.at[0, 0, :, pl.ds(xc, WIDE)], MIX + WIDE, WIDE),
        )

    mine = pl.ds(pl.multiple_of(core * tok, tok), tok)
    theirs = pl.ds(pl.multiple_of(other * tok, tok), tok)
    own_step = pltpu.make_async_copy(step_in.at[0, 0], steps.at[0, core], st_sem.at[0])
    own_step.start()

    def fetch(j, _):
        for src, off, width in pieces(core * HALF + j):
            pltpu.make_async_copy(
                src, uin.at[j, mine, pl.ds(off, width)], own_sem.at[j]
            ).start()
        return 0

    fetch(0, 0)
    params = [
        pltpu.make_async_copy(src, dst, par_sem.at[at])
        for at, (src, dst) in enumerate((
            (sb_in, sb_ref.at[0]), (dl_in, dl_ref.at[0]), (w_in, w_ref.at[pl.ds(0, 1)]),
            (b_in, b_ref.at[0]), (sk_in, sk_ref.at[0]), (ng_in, ng_ref.at[0]),
        ))
    ]
    for copy in params:
        copy.start()
    lax.fori_loop(1, own_groups, fetch, 0)
    partial[dp] = jnp.zeros(partial.shape[1:], F32)
    upad[0:8, :] = jnp.zeros((8, MIX), F32)
    zpad[seq : seq + 8, :] = jnp.zeros((8, MIX), F32)
    for ref in (token_rows, ddt, drate, small, small_out):
        ref[...] = jnp.zeros_like(ref)

    @pl.when(sec > 0)
    def _():
        pl.semaphore_wait(barrier, 7)

    @pl.when(sec == 1)
    def _():
        pl.semaphore_signal(
            plane_sem, inc=1, device_id=place(core, 0, dp), device_id_type=MESH
        )
        for k in range(1, ndp):
            greet(core, 0, lax.rem(dp + k, ndp))

    @pl.when(sec == 0)
    def _():
        pl.semaphore_wait(plane_sem, 1)

    step_copy = remote(
        step_in.at[0, 0], steps.at[0, core], st_sem.at[1], st_sem.at[2], other, sec, dp
    )
    step_copy.start()

    def exchange(j, _):
        for src, off, width in pieces(other * HALF + j):
            remote(
                src, uin.at[j, mine, pl.ds(off, width)], xs_sem.at[j], xr_sem.at[j], other, sec, dp
            ).start()
        return 0

    exchange(0, 0)

    def hand(src, dst, at):
        return remote(src, dst, ship_sem.at[at], ship_recv.at[at], 1, sec - 1, dp)

    @pl.when(sec > 0)
    def _():
        for src, off, width in pieces(last):
            hand(src, uin.at[HALF, mine, pl.ds(off, width)], 0).start()
        hand(step_in.at[0, 0], steps.at[1, core], 1).start()

    @pl.when(jnp.logical_and(sec > 0, core == 0))
    def _():
        xc, bc, cc = group_columns(last)
        for col, width in ((xc, WIDE), (bc, STATE), (cc, STATE)):
            cut = pl.ds(col, width)
            hand(w_in.at[:, :, cut], w_ref.at[pl.ds(1, 1), :, cut], 2).start()
            hand(b_in.at[:, cut], b_ref.at[1, :, cut], 3).start()
        cut = pl.ds(xc, WIDE)
        hand(ng_in.at[:, cut], ng_ref.at[1, :, cut], 4).start()
        hand(sb_in, sb_ref.at[1], 5).start()
        hand(dl_in, dl_ref.at[1], 6).start()
        hand(sk_in, sk_ref.at[1], 7).start()

    lax.fori_loop(1, HALF - other * gives, exchange, 0)
    for copy in params:
        copy.wait()

    def token_terms(which):
        diagonal = lax.broadcasted_iota(jnp.int32, (HEADS, HEADS), 0) == lax.broadcasted_iota(
            jnp.int32, (HEADS, HEADS), 1
        )

        def upright(ref):
            return jnp.sum(jnp.where(diagonal, ref[which], 0.0), axis=1, keepdims=True)

        raw = jnp.concatenate(
            [steps[which, 0].astype(F32), steps[which, 1].astype(F32)], axis=1
        )
        raw = raw + upright(sb_ref)
        delta = jnp.maximum(raw, 0.0) + jnp.log1p(jnp.exp(-jnp.abs(raw)))
        rate = delta * (-jnp.exp(upright(dl_ref)))
        rows2 = lax.broadcasted_iota(jnp.int32, (seq, seq), 0)
        cols2 = lax.broadcasted_iota(jnp.int32, (seq, seq), 1)
        ones_up = jnp.where(rows2 <= cols2, 1.0, 0.0).astype(BF16)
        r_hi, r_rest = rate.astype(BF16), rate - rate.astype(BF16).astype(F32)
        r_mid, r_lo = split(r_rest)
        cumulative = dot(r_hi, ones_up, NN) + (dot(r_mid, ones_up, NN) + dot(r_lo, ones_up, NN))
        for at, value in enumerate((delta, cumulative, jax.nn.sigmoid(raw), rate)):
            top = pl.multiple_of(which * halves_of + at * HEADS, HEADS)
            token_rows[pl.ds(top, HEADS), :] = value
        token_cols[...] = token_rows[...].T

    def group(turn, _):
        j = turn + (turn // (HALF - 1)) * donor
        helping = j // HALF
        g = core * HALF + j - helping
        ours = helping == 0
        slot_p = j + helping
        lane0 = helping * halves_of
        cols = group_columns(g)
        blocks = [(0, cols[0])]
        for base, col in ((WIDE, cols[1]), (WIDE + STATE, cols[2])):
            for part in range(STATE // 128):
                blocks.append((base + part * 128, pl.multiple_of(col + part * 128, 128)))

        def conv_rows(start, count, fresh):
            for off, col in blocks:
                here = slice(off, off + 128)
                if fresh:
                    upad[pl.ds(pl.multiple_of(start + 8, 8), count), here] = uin[
                        j, pl.ds(start, count), here
                    ].astype(F32)
                window = upad[pl.ds(start, count + 8), here]
                z = b_ref[helping, :, pl.ds(col, 128)]
                z = z + w_ref[helping, 3:4, pl.ds(col, 128)] * window[8:]
                for k in range(CONV - 1):
                    tap = w_ref[helping, pl.ds(k, 1), pl.ds(col, 128)]
                    z = z + tap * pltpu.roll(window, 3 - k, 0)[8:]
                s = jax.nn.sigmoid(z)
                mix[pl.ds(start, count), here] = z * s
                dsl[pl.ds(start, count), here] = s * (1.0 + z * (1.0 - s))

        @pl.when(ours)
        def _():
            pltpu.make_async_copy(uin.at[j, mine], uin.at[j, mine], own_sem.at[j]).wait()

        @pl.when(helping == 1)
        def _():
            some = pl.ds(0, WIDE + 2 * STATE)
            for at, ref in enumerate((
                uin.at[HALF], steps.at[1], w_ref.at[pl.ds(1, 1), :, some], b_ref.at[1, :, some],
                ng_ref.at[1, :, pl.ds(0, WIDE)], sb_ref.at[1], dl_ref.at[1], sk_ref.at[1],
            )):
                remote(
                    ref, ref, ship_sem.at[at], ship_recv.at[at], core, sec + 1, dp
                ).wait_recv()

        conv_rows(pl.multiple_of(core * tok, tok), tok, True)

        @pl.when(j == 0)
        def _():
            own_step.wait()
            step_copy.wait()

        @pl.when(lax.rem(j, HALF) == 0)
        def _():
            token_terms(helping)

        @pl.when(ours)
        def _():
            remote(
                uin.at[j, theirs], uin.at[j, theirs], xs_sem.at[j], xr_sem.at[j], other, sec, dp
            ).wait_recv()

        conv_rows(pl.multiple_of(other * tok, tok), tok, True)
        conv_rows(tok, 8, False)

        lane = lax.broadcasted_iota(jnp.int32, (seq, 128), 1)
        lane1 = lax.broadcasted_iota(jnp.int32, (1, 128), 1)
        lane16 = lax.broadcasted_iota(jnp.int32, (1, HEADS), 1)
        row = lax.broadcasted_iota(jnp.int32, (seq, seq), 0)
        column = lax.broadcasted_iota(jnp.int32, (seq, seq), 1)
        first = lane < HEAD_DIM

        def pick(at):
            return jnp.sum(
                jnp.where(lane == lane0 + at, token_cols[...], 0.0), axis=1, keepdims=True
            )

        def pick1(ref, h):
            return jnp.sum(jnp.where(lane16 == h, ref[helping], 0.0), axis=1, keepdims=True)

        x = mix[:, 0:WIDE]
        bmap = split(mix[:, WIDE : WIDE + STATE])
        cmap = split(mix[:, WIDE + STATE : MIX])
        h0 = g * REPS
        dt2 = jnp.where(first, pick(h0), pick(h0 + 1))
        skip2 = jnp.where(first[0:1], pick1(sk_ref, h0), pick1(sk_ref, h0 + 1))
        xs = x * dt2
        xs_p = split(xs)
        scores = dot3(cmap, bmap, NT)
        decay, mixed, ys = [], [], []
        for r in range(REPS):
            seg = pick(HEADS + h0 + r) - token_rows[pl.ds(lane0 + HEADS + h0 + r, 1), :]
            w = jnp.exp(jnp.where(row >= column, seg, -jnp.inf))
            a = scores * w
            a_p = split(a)
            decay.append(w)
            mixed.append((a, a_p))
            ys.append(dot3(a_p, xs_p, NN))
        y = jnp.where(first, ys[0], ys[1]) + skip2 * x
        gate = uin[j, :, MIX : MIX + WIDE].astype(F32)
        cot = uin[j, :, MIX + WIDE : MIX + 2 * WIDE].astype(F32)
        gain = ng_ref[helping, :, pl.ds(cols[0], WIDE)]
        s = jax.nn.sigmoid(gate)
        act = gate * s
        gated = y * act
        scale = lax.rsqrt(jnp.mean(gated * gated, axis=1, keepdims=True) + 1e-05)
        normed = gated * scale
        stage_o[j, :, 0:WIDE] = (normed * gain).astype(BF16)
        dn = cot * gain
        dgated = scale * (dn - normed * jnp.mean(dn * normed, axis=1, keepdims=True))
        dy = dgated * act
        stage_o[j, :, WIDE : 2 * WIDE] = (dgated * y * (s * (1.0 + gate * (1.0 - s)))).astype(BF16)

        even = lax.rem(j, 2) == 0
        out_cut = pl.ds(cols[0], WIDE)

        def send_half(base, t, dst, done, landed, s):
            remote(
                stage_o.at[j, pl.ds(t * tok, tok), pl.ds(base, WIDE)], dst, done, landed, t, s, dp
            ).start()

        direct = jnp.logical_and(
            ours, jnp.logical_and(sec < nsec - 1, jnp.logical_not(jnp.logical_and(sec == 1, even)))
        )

        @pl.when(direct)
        def _():
            for t in range(2):
                send_half(0, t, nxt.at[0, 0, :, out_cut], next_sem.at[0], next_sem.at[1], sec + 1)

        @pl.when(jnp.logical_and(ours, jnp.logical_and(sec == 1, even)))
        def _():
            slot = core * (HALF // 2) + j // 2
            for t in range(2):
                send_half(0, t, relay.at[slot], next_sem.at[0], relay_sem.at[slot], 3)

        @pl.when(jnp.logical_and(ours, jnp.logical_or(sec == 1, sec == 3)))
        def _():
            for t in range(2):
                send_half(
                    WIDE, t, ggate.at[0, 0, :, out_cut], gate_sem.at[0], gate_sem.at[1], sec - 1
                )

        @pl.when(jnp.logical_and(ours, sec == 2))
        def _():
            slot = core * HALF + j
            for t in range(2):
                send_half(WIDE, t, relay.at[slot], gate_sem.at[0], relay_sem.at[slot], 0)

        @pl.when(helping == 1)
        def _():
            ggate[0, 0, :, out_cut] = stage_o[j, tok : 2 * tok, WIDE : 2 * WIDE]
            send_half(WIDE, 0, ggate.at[0, 0, :, out_cut], gate_sem.at[0], gate_sem.at[1], sec)

        @pl.when(jnp.logical_and(helping == 1, sec < nsec - 2))
        def _():
            for t in range(2):
                send_half(0, t, nxt.at[0, 0, :, out_cut], next_sem.at[0], next_sem.at[1], sec + 2)

        partial[dp, slot_p, 5:6, 0:WIDE] = jnp.sum(cot * normed, axis=0, keepdims=True)
        dyx = jnp.sum(dy * x, axis=0, keepdims=True)
        dscore = jnp.zeros((seq, seq), F32)
        dy_p = split(dy)
        das = []
        for r in range(REPS):
            own = first if r == 0 else jnp.logical_not(first)
            da = dot3(split(jnp.where(own, dy, 0.0)), xs_p, NT)
            das.append(da)
            dscore = dscore + da * decay[r]
        ds_p = split(dscore)

        def conv_back(off, width, start):
            for part in range(width // 128):
                here = slice(off + part * 128, off + part * 128 + 128)
                col = pl.multiple_of(start + part * 128, 128)
                dz = zpad[0:seq, here]
                du = jnp.zeros((seq, 128), F32)
                for k in range(CONV):
                    du = du + (
                        w_ref[helping, pl.ds(k, 1), pl.ds(col, 128)]
                        * zpad[3 - k : 3 - k + seq, here]
                    )
                    partial[dp, slot_p, pl.ds(k, 1), here] = jnp.sum(
                        dz * upad[5 + k : 5 + k + seq, here], axis=0, keepdims=True
                    )
                partial[dp, slot_p, pl.ds(4, 1), here] = jnp.sum(dz, axis=0, keepdims=True)
                stage_c[j, :, here] = du.astype(BF16)

            @pl.when(helping == 1)
            def _():
                gconv[0, 0, :, pl.ds(start, width)] = stage_c[j, tok : 2 * tok, off : off + width]
                remote(
                    stage_c.at[j, pl.ds(0, tok), pl.ds(off, width)],
                    gconv.at[0, 0, :, pl.ds(start, width)],
                    conv_sem.at[0], conv_sem.at[1], 0, sec, dp,
                ).start()

            @pl.when(jnp.logical_and(ours, sec > 0))
            def _():
                for t in range(2):
                    remote(
                        stage_c.at[j, pl.ds(t * tok, tok), pl.ds(off, width)],
                        gconv.at[0, 0, :, pl.ds(start, width)],
                        conv_sem.at[0], conv_sem.at[1], t, sec - 1, dp,
                    ).start()

        zpad[0:seq, WIDE + STATE : MIX] = dot3(ds_p, bmap, NN) * dsl[:, WIDE + STATE : MIX]
        conv_back(WIDE + STATE, STATE, cols[2])
        zpad[0:seq, WIDE : WIDE + STATE] = dot3(ds_p, cmap, TN) * dsl[:, WIDE : WIDE + STATE]
        conv_back(WIDE, STATE, cols[1])
        dxs = jnp.where(first, dot3(mixed[0][1], dy_p, TN), dot3(mixed[1][1], dy_p, TN))
        zpad[0:seq, 0:WIDE] = (skip2 * dy + dxs * dt2) * dsl[:, 0:WIDE]
        conv_back(0, WIDE, cols[0])
        upper = jnp.where(row <= column, 1.0, 0.0).astype(BF16)
        dxx = dxs * x
        for r in range(REPS):
            own = first if r == 0 else jnp.logical_not(first)
            p = split(das[r] * mixed[r][0])
            later = dot(upper, p[0], NN) + dot(upper, p[1], NN)
            dr = jnp.sum(jnp.where(row > column, later, 0.0), axis=1, keepdims=True)
            drate[...] += jnp.where(lane == lane0 + h0 + r, dr, 0.0)
            total = jnp.sum(jnp.where(own[0:1], dyx, 0.0), axis=1, keepdims=True)
            small[2:3, :] += jnp.where(lane1 == lane0 + h0 + r, total, 0.0)
            dd = jnp.sum(jnp.where(own, dxx, 0.0), axis=1, keepdims=True)
            ddt[...] += jnp.where(lane == lane0 + h0 + r, dd, 0.0)

        @pl.when(jnp.logical_and(j == 0, sec == 0))
        def _():
            pl.semaphore_wait(barrier, ndp - 1)
            for s in range(1, 4):
                pl.semaphore_signal(
                    world_sem, inc=1, device_id=place(core, s, dp), device_id_type=MESH
                )

        @pl.when(jnp.logical_and(j == 0, sec > 0))
        def _():
            pl.semaphore_wait(world_sem, 1)

        @pl.when(ours)
        def _():
            spread(j)

        @pl.when(helping == 1)
        def _():
            remote(
                partial.at[dp, HALF + 1], partial.at[dp, HALF - 1],
                hand_sem.at[0], hand_sem.at[1], core, sec + 1, dp,
            ).start()

        return 0

    def spread(slot):
        for k in range(1, ndp):
            to = lax.rem(dp + k, ndp)
            remote(
                partial.at[dp, slot], partial.at[dp, slot], ps_sem.at[to], pr_sem.at[dp],
                core, sec, to,
            ).start()

    lax.fori_loop(0, own_groups + helper, group, 0)

    def pass_on(slot, g, out, landed, s):
        part = relay.at[slot]
        remote(part, part, via_sem.at[0], relay_sem.at[slot], core, s, dp).wait_recv()
        remote(
            part, out.at[0, 0, :, pl.ds(g * WIDE, WIDE)], via_sem.at[0], landed, core, s, dp
        ).start()

    @pl.when(sec == 0)
    def _():
        for g in range(GROUPS - 1):
            pass_on(g, g, ggate, gate_sem.at[1], 1)

    @pl.when(sec == 3)
    def _():
        for at in range(GROUPS // 2):
            pass_on(at, 2 * at, nxt, next_sem.at[1], 2)

    @pl.when(sec == 0)
    def _():
        nxt[...] = jnp.zeros_like(nxt)

    @pl.when(sec == nsec - 1)
    def _():
        gconv[...] = jnp.zeros_like(gconv)
        ggate[...] = jnp.zeros_like(ggate)
        gstep[...] = jnp.zeros_like(gstep)

    def step_terms(which, into):
        lane0 = which * halves_of
        heads = slice(lane0, lane0 + HEADS)
        dr16 = drate[:, heads]
        gate = token_cols[:, lane0 + 2 * HEADS : lane0 + 3 * HEADS]
        rate = token_cols[:, lane0 + 3 * HEADS : lane0 + 4 * HEADS]
        dstep = (ddt[:, heads] - dr16 * jnp.exp(dl_ref[which])) * gate
        into[0:1, 0:HEADS] = jnp.sum(dstep, axis=0, keepdims=True)
        into[1:2, 0:HEADS] = jnp.sum(dr16 * rate, axis=0, keepdims=True)
        drate[:, heads] = dstep

    step_terms(0, small)

    @pl.when(helper == 1)
    def _():
        step_terms(1, small_out)
        small_out[2:3, 0:HEADS] = small[2:3, halves_of : halves_of + HEADS]
        remote(
            small_out, small_in, hand_sem.at[2], hand_sem.at[3], core, sec + 1, dp
        ).start()

    turned = drate[...].T
    for t in range(2):
        stage_s[t] = turned[0:HEADS, t * tok : (t + 1) * tok].astype(BF16)

    @pl.when(sec > 0)
    def _():
        for t in range(2):
            remote(
                stage_s.at[t], step_parts.at[core],
                dstep_sem.at[2], dstep_sem.at[core], t, sec - 1, dp,
            ).start()

    @pl.when(helper == 1)
    def _():
        stage_s[2] = turned[halves_of : halves_of + HEADS, 0:tok].astype(BF16)
        step_parts[2] = turned[halves_of : halves_of + HEADS, tok : 2 * tok].astype(BF16)
        remote(
            stage_s.at[2], step_parts.at[2], dstep_sem.at[4], dstep_sem.at[3], other, sec, dp
        ).start()

    @pl.when(donor == 1)
    def _():
        landed = partial.at[dp, HALF - 1]
        remote(landed, landed, hand_sem.at[0], hand_sem.at[1], core, sec - 1, dp).wait_recv()
        spread(HALF - 1)
        remote(small_in, small_in, hand_sem.at[2], hand_sem.at[3], core, sec - 1, dp).wait_recv()
        small[...] += small_in[...]

    partial[dp, HALF, :, 0:128] = small[...]
    spread(HALF)
    for k in range(1, ndp):
        to = lax.rem(dp + k, ndp)
        remote(
            partial.at[dp, pl.ds(0, HALF + 1)], partial.at[to, pl.ds(0, HALF + 1)],
            ps_sem.at[to], pr_sem.at[to], core, sec, to,
        ).wait()
    total = partial[0, 0 : HALF + 1]
    for k in range(1, ndp):
        total = total + partial[k, 0 : HALF + 1]
    final[core] = total
    halves = remote(final.at[core], final.at[core], fin_sem.at[0], fin_sem.at[1], other, sec, dp)
    halves.start()
    remote(final.at[core], final.at[other], fin_sem.at[0], fin_sem.at[1], other, sec, dp).wait()
    for g in range(GROUPS):
        c, j = g // HALF, g % HALF
        gng[0:1, g * WIDE : (g + 1) * WIDE] = final[c, j, 5:6, 0:WIDE]
        for off, width, col in (
            (0, WIDE, g * WIDE),
            (WIDE, STATE, INNER + g * STATE),
            (WIDE + STATE, STATE, INNER + (GROUPS + g) * STATE),
        ):
            gtap[0, :, col : col + width] = final[c, j, 0:CONV, off : off + width]
            gcb[0:1, col : col + width] = final[c, j, CONV : CONV + 1, off : off + width]
    for at, ref in enumerate((gsb, gdl, gsk)):
        ref[...] = final[0, HALF, at : at + 1, 0:HEADS] + final[1, HALF, at : at + 1, 0:HEADS]

    @pl.when(sec < nsec - 1)
    def _():
        for c in range(2):
            part = step_parts.at[c]
            remote(part, part, dstep_sem.at[2], dstep_sem.at[c], core, sec + 1, dp).wait_recv()

        @pl.when(core == 0)
        def _():
            part = step_parts.at[2]
            remote(part, part, dstep_sem.at[4], dstep_sem.at[3], other, sec, dp).wait_recv()

        both = step_parts[0].astype(F32) + step_parts[1].astype(F32)
        gstep[0, 0] = (both + step_parts[2].astype(F32)).astype(BF16)

    def sent(ref, sem):
        remote(ref, ref, sem, sem, other, sec, dp).wait_send()

    def landed(ref, sem):
        remote(ref, ref, sem, sem, other, sec, dp).wait_recv()

    def exchanged(j, _):
        sent(uin.at[j, mine], xs_sem.at[j])
        return 0

    lax.fori_loop(0, HALF - other * gives, exchanged, 0)
    first = pl.ds(0, HALF - 1)
    half = pl.ds(0, WIDE)

    @pl.when(sec == 0)
    def _():
        sent(relay.at[pl.ds(0, GROUPS - 1)], via_sem.at[0])

    @pl.when(sec == nsec - 1)
    def _():
        sent(relay.at[pl.ds(0, GROUPS // 2)], via_sem.at[0])

    @pl.when(sec > 0)
    def _():
        sent(uin.at[HALF, pl.ds(0, tok)], ship_sem.at[0])
        sent(steps.at[1, 0], ship_sem.at[1])
        sent(stage_c.at[first], conv_sem.at[0])
        sent(stage_o.at[first, :, half], gate_sem.at[0])
        sent(stage_s.at[pl.ds(0, 2)], dstep_sem.at[2])
        landed(nxt.at[0, 0], next_sem.at[1])

    @pl.when(jnp.logical_and(sec > 0, core == 0))
    def _():
        some = pl.ds(0, WIDE + 2 * STATE)
        sent(w_ref.at[pl.ds(1, 1), :, some], ship_sem.at[2])
        sent(b_ref.at[1, :, some], ship_sem.at[3])
        sent(ng_ref.at[1, :, half], ship_sem.at[4])
        sent(sb_ref.at[1], ship_sem.at[5])
        sent(dl_ref.at[1], ship_sem.at[6])
        sent(sk_ref.at[1], ship_sem.at[7])
        sent(stage_c.at[HALF - 1], conv_sem.at[0])
        sent(stage_o.at[HALF - 1, :, half], gate_sem.at[0])

    @pl.when(sec < nsec - 1)
    def _():
        sent(stage_o.at[first, :, half], next_sem.at[0])

    @pl.when(jnp.logical_and(sec < nsec - 1, donor == 0))
    def _():
        sent(stage_o.at[HALF - 1, :, half], next_sem.at[0])

    @pl.when(helper == 1)
    def _():
        sent(stage_c.at[HALF, pl.ds(0, tok)], conv_sem.at[0])
        sent(stage_o.at[HALF, pl.ds(0, tok), half], gate_sem.at[0])
        sent(stage_s.at[2], dstep_sem.at[4])
        sent(partial.at[dp, HALF + 1], hand_sem.at[0])
        sent(small_out, hand_sem.at[2])
        landed(ggate.at[0, 0, :, pl.ds(0, INNER - WIDE)], gate_sem.at[1])
        landed(gconv.at[0, 0, :, pl.ds(0, (GROUPS - 1) * MIX)], conv_sem.at[1])

    @pl.when(jnp.logical_and(helper == 1, sec < nsec - 2))
    def _():
        sent(stage_o.at[HALF, :, half], next_sem.at[0])

    @pl.when(jnp.logical_and(sec < nsec - 1, core == 0))
    def _():
        landed(ggate.at[0, 0], gate_sem.at[1])
        landed(gconv.at[0, 0], conv_sem.at[1])


def finish_kernel(*refs):
    count = len(refs) // 2
    sem = refs[-1]
    copies = [pltpu.make_async_copy(refs[i], refs[count + i], sem.at[i]) for i in range(count)]
    for copy in copies:
        copy.start()
    for copy in copies:
        copy.wait()


def paired(
    conv_input, gate_input, step_input, cotangent, conv_weight,
    conv_bias, step_bias, decay_log, skip_gain, norm_gain,
):
    tok = conv_input.shape[2]
    seq = 2 * tok
    ndp = lax.axis_size("dp")
    hbm = pl.BlockSpec(memory_space=pl.ANY)
    vmem = pl.BlockSpec(memory_space=pltpu.VMEM)
    scratch = [
        pltpu.VMEM((2,) + conv_weight.shape[1:], F32),
        pltpu.VMEM((2,) + conv_bias.shape, F32),
        pltpu.VMEM((2,) + step_bias.shape, F32),
        pltpu.VMEM((2,) + decay_log.shape, F32),
        pltpu.VMEM((2,) + skip_gain.shape, F32),
        pltpu.VMEM((2,) + norm_gain.shape, F32),
        pltpu.VMEM((HALF + 1, seq, MIX + 2 * WIDE), BF16),
        pltpu.VMEM((2, 2, HEADS, tok), BF16),
        pltpu.VMEM((128, seq), F32),
        pltpu.VMEM((seq, 128), F32),
        pltpu.VMEM((seq + 8, MIX), F32),
        pltpu.VMEM((seq + 8, MIX), F32),
        pltpu.VMEM((seq, MIX), F32),
        pltpu.VMEM((seq, MIX), F32),
        pltpu.VMEM((seq, 128), F32),
        pltpu.VMEM((seq, 128), F32),
        pltpu.VMEM((8, 128), F32),
        pltpu.VMEM((HALF + 1, seq, MIX), BF16),
        pltpu.VMEM((HALF + 1, seq, 2 * WIDE), BF16),
        pltpu.VMEM((3, HEADS, tok), BF16),
        pltpu.VMEM((3, HEADS, tok), BF16),
        pltpu.VMEM((ndp, HALF + 2, 8, MIX), F32),
        pltpu.VMEM((2, HALF + 1, 8, MIX), F32),
        pltpu.VMEM((GROUPS, tok, WIDE), BF16),
        pltpu.VMEM((8, 128), F32),
        pltpu.VMEM((8, 128), F32),
        pltpu.SemaphoreType.DMA((HALF,)),
        pltpu.SemaphoreType.DMA((HALF,)),
        pltpu.SemaphoreType.DMA((HALF,)),
        pltpu.SemaphoreType.DMA((3,)),
        pltpu.SemaphoreType.DMA((2,)),
        pltpu.SemaphoreType.DMA((2,)),
        pltpu.SemaphoreType.DMA((2,)),
        pltpu.SemaphoreType.DMA((5,)),
        pltpu.SemaphoreType.DMA((ndp,)),
        pltpu.SemaphoreType.DMA((ndp,)),
        pltpu.SemaphoreType.DMA((2,)),
        pltpu.SemaphoreType.DMA((1,)),
        pltpu.SemaphoreType.DMA((GROUPS,)),
        pltpu.SemaphoreType.DMA((6,)),
        pltpu.SemaphoreType.REGULAR,
        pltpu.SemaphoreType.REGULAR,
        pltpu.SemaphoreType.DMA((8,)),
        pltpu.SemaphoreType.DMA((8,)),
        pltpu.SemaphoreType.DMA((4,)),
    ]
    turned = jnp.swapaxes(step_input, 2, 3)
    shapes = [
        (gate_input.shape, BF16),
        (conv_input.shape, BF16),
        (gate_input.shape, BF16),
        (turned.shape, BF16),
        (conv_weight.shape, F32),
        (conv_bias.shape, F32),
        (step_bias.shape, F32),
        (decay_log.shape, F32),
        (skip_gain.shape, F32),
        (norm_gain.shape, F32),
    ]
    inputs = [
        pltpu.with_memory_space_constraint(a, pltpu.HBM)
        for a in (
            conv_input, gate_input, turned, cotangent, conv_weight,
            conv_bias, step_bias, decay_log, skip_gain, norm_gain,
        )
    ]
    sent = pl.pallas_call(
        pair_kernel,
        name="mixer_tick",
        in_specs=[hbm] * 10,
        out_specs=[vmem] * 10,
        out_shape=[pltpu.VMEM(shape, kind) for shape, kind in shapes],
        scratch_shapes=scratch,
        compiler_params=pltpu.CompilerParams(
            collective_id=0, has_side_effects=True, vmem_limit_bytes=24 * 1024 * 1024
        ),
    )(*inputs)
    done = pl.pallas_call(
        finish_kernel,
        name="mixer_finish",
        in_specs=[vmem] * 10,
        out_specs=[hbm] * 10,
        out_shape=[jax.ShapeDtypeStruct(shape, kind) for shape, kind in shapes],
        scratch_shapes=[pltpu.SemaphoreType.DMA((10,))],
        compiler_params=pltpu.CompilerParams(vmem_limit_bytes=1024 * 1024),
    )(*sent)
    return tuple(done[:3]) + (jnp.swapaxes(done[3], 2, 3),) + tuple(done[4:])


def solution(mesh):
    in_specs = (
        P("section", "dp", "ctx", None),
        P("section", "dp", "ctx", None),
        P("section", "dp", "ctx", None),
        P("section", "dp", "ctx", None),
        P("section", None, None),
        P("section", None),
        P("section", None),
        P("section", None),
        P("section", None),
        P("section", None),
    )
    out_specs = (
        P("section", "dp", "ctx", None),
        P("section", "dp", "ctx", None),
        P("section", "dp", "ctx", None),
        P("section", "dp", "ctx", None),
        P("section", None, None),
        P("section", None),
        P("section", None),
        P("section", None),
        P("section", None),
        P("section", None),
    )
    body = paired if (mesh.shape["ctx"], mesh.shape["section"]) == (2, 4) else shards
    return jax.shard_map(body, mesh=mesh, in_specs=in_specs, out_specs=out_specs, check_vma=False)
```

```python
import functools
import jax
import jax.numpy as jnp
from jax import lax
from jax.experimental import pallas as pl
from jax.experimental.pallas import tpu as pltpu
from jax.sharding import PartitionSpec as P

HEADS = 16
HEAD_DIM = 64
STATE = 256
GROUPS = 8
CONV = 4


HIGH_BOUND = lax.Precision.HIGHEST


def shifted(block, axis, distance):
    devices = range(lax.axis_size(axis))
    route = [(i - distance, i) for i in devices if i - distance in devices]
    return lax.ppermute(block, axis, route)


def prefix(part, axis, combine, identity):
    count = lax.axis_size(axis)
    place = lax.axis_index(axis)
    ahead = count - 1 - place
    gathered = jax.tree.map(lambda a: lax.all_gather(a, axis), part)
    state = jax.tree.map(lambda a, e: jnp.zeros_like(a) + jnp.asarray(e, a.dtype), part, identity)

    def one(turn, state):
        source = count - 1 - turn
        return combine(
            state, jax.tree.map(lambda a: lax.dynamic_index_in_dim(a, source, 0, False), gathered)
        )

    return lax.fori_loop(0, ahead, one, state)


def conv_mix(extended, taps, initial_offset):
    rows = extended.shape[0] - (CONV - 1)
    total = initial_offset[None, :]
    for tap in range(CONV):
        total = total + taps[tap][None, :] * extended[tap : tap + rows]
    return jax.nn.silu(total)


def split_mix(mixed, steps, step_shift, damping_exponents):
    rows = mixed.shape[0]
    inner = HEADS * HEAD_DIM
    payload_lines = mixed[:, :inner].reshape(rows, GROUPS, HEADS // GROUPS, HEAD_DIM)
    in_maps = mixed[:, inner : inner + GROUPS * STATE].reshape(rows, GROUPS, STATE)
    out_maps = mixed[:, inner + GROUPS * STATE :].reshape(rows, GROUPS, STATE)
    delta = jax.nn.softplus(steps + step_shift[None, :])
    upto = jnp.tril(jnp.ones((rows, rows), jnp.float32))
    rates = delta * (-jnp.exp(damping_exponents))[None, :]
    cumulative = jnp.dot(upto, rates, precision=HIGH_BOUND)
    return (payload_lines, in_maps, out_maps, delta, cumulative)


def fragment_condition(extended, steps, taps, initial_offset, step_shift, damping_exponents):
    payload_lines, in_maps, out_maps, delta, cumulative = split_mix(
        conv_mix(extended, taps, initial_offset), steps, step_shift, damping_exponents
    )
    rows = payload_lines.shape[0]
    total = cumulative[-1]
    weight = (jnp.exp(total[None, :] - cumulative) * delta).reshape(rows, GROUPS, HEADS // GROUPS)
    state = jnp.einsum(
        "tgrp,tgn->grpn", payload_lines * weight[..., None], in_maps, precision=HIGH_BOUND
    )
    return (state.reshape(HEADS, HEAD_DIM, STATE), total)


def shard_layer(
    extended,
    gates,
    steps,
    taps,
    initial_offset,
    step_shift,
    damping_exponents,
    skip_values,
    gain_values,
    carried,
):
    payload_lines, in_maps, out_maps, delta, cumulative = split_mix(
        conv_mix(extended, taps, initial_offset), steps, step_shift, damping_exponents
    )
    rows = payload_lines.shape[0]
    reps = HEADS // GROUPS
    lower = (jnp.arange(rows)[:, None] >= jnp.arange(rows)[None, :])[None]
    seg = cumulative.T[:, :, None] - cumulative.T[:, None, :]
    weight = jnp.exp(jnp.where(lower, seg, -jnp.inf)).reshape(GROUPS, reps, rows, rows)
    intersection_maps = jnp.einsum("tgn,sgn->gts", out_maps, in_maps, precision=HIGH_BOUND)
    score_matrix = weight * intersection_maps[:, None]
    scaled_values = payload_lines * delta.reshape(rows, GROUPS, reps)[..., None]
    final_output = jnp.einsum("jzlh,hjzc->ljzc", score_matrix, scaled_values, precision=HIGH_BOUND)
    incoming = jnp.einsum(
        "tgn,grpn->tgrp",
        out_maps,
        carried.reshape(GROUPS, reps, HEAD_DIM, STATE),
        precision=HIGH_BOUND,
    )
    final_output = (
        final_output + incoming * jnp.exp(cumulative).reshape(rows, GROUPS, reps)[..., None]
    )
    final_output = (
        final_output + skip_values.reshape(GROUPS, reps)[None, :, :, None] * payload_lines
    )
    gated = final_output.reshape(rows, GROUPS, -1) * jax.nn.silu(gates).reshape(rows, GROUPS, -1)
    normed = gated * lax.rsqrt(jnp.mean(gated * gated, axis=-1, keepdims=True) + 1e-05)
    return normed.reshape(rows, -1) * gain_values[None, :]


def combine(earlier, later):
    return (earlier[0] * later[0], later[0][:, None] * earlier[1] + later[1])


def shards(
    conv_input,
    gate_input,
    step_input,
    cotangent,
    conv_weight,
    conv_bias,
    step_bias,
    decay_log,
    skip_gain,
    norm_gain,
):
    local_rows = conv_input[0, 0]
    count = local_rows.shape[0]
    taps, initial_offset = (conv_weight[0], conv_bias[0])
    step_shift, damping_exponents = (step_bias[0], decay_log[0])
    skip_values, gain_values = (skip_gain[0], norm_gain[0])
    previous = shifted(local_rows[count - (CONV - 1) :], "ctx", 1)
    extended = jnp.concatenate([previous, local_rows], 0).astype(jnp.float32)
    gates = gate_input[0, 0].astype(jnp.float32)
    steps = step_input[0, 0].astype(jnp.float32)
    (state, total), state_pull = jax.vjp(
        fragment_condition, extended, steps, taps, initial_offset, step_shift, damping_exponents
    )
    decay = jnp.exp(total)
    flat_state = state.reshape(HEADS, HEAD_DIM * STATE)
    unity = (jnp.ones((HEADS,), jnp.float32), jnp.zeros((HEADS, HEAD_DIM * STATE), jnp.float32))

    def advance(index, current):
        return shifted(decay[:, None] * current + flat_state, "ctx", 1)

    incoming = lax.fori_loop(
        0, lax.axis_size("ctx") - 1, advance, jnp.zeros((HEADS, HEAD_DIM * STATE), jnp.float32)
    )
    carried = incoming.reshape(HEADS, HEAD_DIM, STATE)
    final_output, layer_pull = jax.vjp(
        shard_layer,
        extended,
        gates,
        steps,
        taps,
        initial_offset,
        step_shift,
        damping_exponents,
        skip_values,
        gain_values,
        carried,
    )
    forward = shifted(final_output.astype(jnp.bfloat16)[None, None], "section", 1)
    grads = layer_pull(cotangent[0, 0].astype(jnp.float32))
    carry_grad = grads[9].reshape(HEADS, HEAD_DIM * STATE)
    outgoing = prefix((decay, carry_grad), "ctx", combine, unity)[1]
    outgoing_grad = outgoing.reshape(HEADS, HEAD_DIM, STATE)
    total_grad = jnp.sum(outgoing_grad * carried, axis=(1, 2)) * decay
    extra = state_pull((outgoing_grad, total_grad))
    ext_grad = grads[0] + extra[0]
    step_grad = grads[2] + extra[1]
    param_terms = (
        grads[3] + extra[2],
        grads[4] + extra[3],
        grads[5] + extra[4],
        grads[6] + extra[5],
        grads[7],
        grads[8],
    )
    returned = shifted(ext_grad[: CONV - 1], "ctx", -1)
    own_grad = ext_grad[CONV - 1 :]
    row_grad = jnp.concatenate(
        [own_grad[: count - (CONV - 1)], own_grad[count - (CONV - 1) :] + returned], 0
    )
    backward = shifted(
        (
            row_grad.astype(jnp.bfloat16)[None, None],
            grads[1].astype(jnp.bfloat16)[None, None],
            step_grad.astype(jnp.bfloat16)[None, None],
        ),
        "section",
        -1,
    )
    summed = lax.psum(
        (
            param_terms[0],
            param_terms[1],
            param_terms[2],
            param_terms[3],
            param_terms[4],
            param_terms[5],
        ),
        ("ctx", "dp"),
    )
    return (
        forward,
        backward[0],
        backward[1],
        backward[2],
        summed[0][None],
        summed[1][None],
        summed[2][None],
        summed[3][None],
        summed[4][None],
        summed[5][None],
    )


MESH = pl.DeviceIdType.MESH
F32 = jnp.float32
BF16 = jnp.bfloat16
INNER = HEADS * HEAD_DIM
REPS = HEADS // GROUPS
WIDE = REPS * HEAD_DIM
MIX = WIDE + 2 * STATE
HALF = GROUPS // 2
NN = ((1,), (0,))
NT = ((1,), (1,))
TN = ((0,), (0,))


def split(a):
    high = a.astype(BF16)
    return high, (a - high.astype(F32)).astype(BF16)


def dot(a, b, dims):
    return lax.dot_general(a, b, (dims, ((), ())), preferred_element_type=F32)


def dot3(a, b, dims):
    return dot(a[0], b[0], dims) + (dot(a[0], b[1], dims) + dot(a[1], b[0], dims))


def group_columns(g):
    return (
        pl.multiple_of(g * WIDE, 128),
        pl.multiple_of(INNER + g * STATE, 128),
        pl.multiple_of(INNER + (GROUPS + g) * STATE, 128),
    )


def pair_kernel(
    conv_in, gate_in, step_in, cot_in, w_in, b_in, sb_in, dl_in, sk_in, ng_in,
    nxt, gconv, ggate, gstep, gtap, gcb, gsb, gdl, gsk, gng,
    w_ref, b_ref, sb_ref, dl_ref, sk_ref, ng_ref,
    uin, steps, token_rows, token_cols, upad, zpad, mix, dsl, ddt, drate, small,
    stage_c, stage_o, stage_s, step_parts, partial, final, relay, small_out, small_in,
    own_sem, xs_sem, xr_sem, st_sem, conv_sem, gate_sem, next_sem, dstep_sem,
    ps_sem, pr_sem, fin_sem, via_sem, relay_sem, par_sem, pair_sem, plane_sem, world_sem,
    ship_sem, ship_recv, hand_sem,
):
    core = lax.axis_index("ctx")
    sec = lax.axis_index("section")
    dp = lax.axis_index("dp")
    nsec = lax.axis_size("section")
    ndp = lax.axis_size("dp")
    tok = conv_in.shape[2]
    seq = 2 * tok
    other = 1 - core
    gives = (sec + nsec - 1) // nsec
    takes = 1 - sec // (nsec - 1)
    donor = core * gives
    helper = core * takes
    own_groups = HALF - donor
    last = GROUPS - 1
    halves_of = 4 * HEADS

    def place(c, s, d):
        return {"ctx": c, "section": s, "dp": d}

    def remote(src, dst, send, recv, c, s, d):
        return pltpu.make_async_remote_copy(
            src_ref=src, dst_ref=dst, send_sem=send, recv_sem=recv,
            device_id=place(c, s, d), device_id_type=MESH,
        )

    after = lax.rem(sec + 1, nsec)
    before = lax.rem(sec + nsec - 1, nsec)
    barrier = pltpu.get_barrier_semaphore()

    def greet(c, s, d):
        pl.semaphore_signal(barrier, inc=1, device_id=place(c, s, d), device_id_type=MESH)

    for c in range(2):
        for s in (1, 3):

            @pl.when(jnp.logical_and(sec // 2 == s // 2, jnp.logical_or(sec != s, core != c)))
            def _():
                greet(c, s, dp)

    def pieces(g):
        xc, bc, cc = group_columns(g)
        return (
            (conv_in.at[0, 0, :, pl.ds(xc, WIDE)], 0, WIDE),
            (conv_in.at[0, 0, :, pl.ds(bc, STATE)], WIDE, STATE),
            (conv_in.at[0, 0, :, pl.ds(cc, STATE)], WIDE + STATE, STATE),
            (gate_in.at[0, 0, :, pl.ds(xc, WIDE)], MIX, WIDE),
            (cot_in.at[0, 0, :, pl.ds(xc, WIDE)], MIX + WIDE, WIDE),
        )

    mine = pl.ds(pl.multiple_of(core * tok, tok), tok)
    theirs = pl.ds(pl.multiple_of(other * tok, tok), tok)
    own_step = pltpu.make_async_copy(step_in.at[0, 0], steps.at[0, core], st_sem.at[0])
    own_step.start()

    def fetch(j, _):
        for src, off, width in pieces(core * HALF + j):
            pltpu.make_async_copy(
                src, uin.at[j, mine, pl.ds(off, width)], own_sem.at[j]
            ).start()
        return 0

    fetch(0, 0)
    params = [
        pltpu.make_async_copy(src, dst, par_sem.at[at])
        for at, (src, dst) in enumerate((
            (sb_in, sb_ref.at[0]), (dl_in, dl_ref.at[0]), (w_in, w_ref.at[pl.ds(0, 1)]),
            (b_in, b_ref.at[0]), (sk_in, sk_ref.at[0]), (ng_in, ng_ref.at[0]),
        ))
    ]
    for copy in params:
        copy.start()
    lax.fori_loop(1, own_groups, fetch, 0)
    partial[dp] = jnp.zeros(partial.shape[1:], F32)
    upad[0:8, :] = jnp.zeros((8, MIX), F32)
    zpad[seq : seq + 8, :] = jnp.zeros((8, MIX), F32)
    for ref in (token_rows, ddt, drate, small, small_out):
        ref[...] = jnp.zeros_like(ref)

    upper = lax.rem(sec, 2) == 1

    def tell(sem, s):
        pl.semaphore_signal(sem, inc=1, device_id=place(core, s, dp), device_id_type=MESH)

    @pl.when(upper)
    def _():
        pl.semaphore_wait(barrier, 3)

    def hand(src, dst, at):
        return remote(src, dst, ship_sem.at[at], ship_recv.at[at], 1, sec - 1, dp)

    def hand_over():
        for src, off, width in pieces(last):
            hand(src, uin.at[HALF, mine, pl.ds(off, width)], 0).start()
        hand(step_in.at[0, 0], steps.at[1, core], 1).start()

    def hand_params():
        xc, bc, cc = group_columns(last)
        for col, width in ((xc, WIDE), (bc, STATE), (cc, STATE)):
            cut = pl.ds(col, width)
            hand(w_in.at[:, :, cut], w_ref.at[pl.ds(1, 1), :, cut], 2).start()
            hand(b_in.at[:, cut], b_ref.at[1, :, cut], 3).start()
        cut = pl.ds(xc, WIDE)
        hand(ng_in.at[:, cut], ng_ref.at[1, :, cut], 4).start()
        hand(sb_in, sb_ref.at[1], 5).start()
        hand(dl_in, dl_ref.at[1], 6).start()
        hand(sk_in, sk_ref.at[1], 7).start()

    @pl.when(upper)
    def _():
        tell(pair_sem, sec - 1)
        hand_over()

    @pl.when(sec == 1)
    def _():
        greet(core, 2, dp)

    @pl.when(jnp.logical_not(upper))
    def _():
        pl.semaphore_wait(pair_sem, 1)

    step_copy = remote(
        step_in.at[0, 0], steps.at[0, core], st_sem.at[1], st_sem.at[2], other, sec, dp
    )
    step_copy.start()

    def exchange(j, _):
        for src, off, width in pieces(other * HALF + j):
            remote(
                src, uin.at[j, mine, pl.ds(off, width)], xs_sem.at[j], xr_sem.at[j], other, sec, dp
            ).start()
        return 0

    exchange(0, 0)

    @pl.when(sec == 2)
    def _():
        pl.semaphore_wait(barrier, 1)
        tell(plane_sem, 0)
        tell(plane_sem, 1)
        hand_over()

    @pl.when(jnp.logical_and(sec > 0, core == 0))
    def _():
        hand_params()

    lax.fori_loop(1, HALF - other * gives, exchange, 0)
    for copy in params:
        copy.wait()

    def token_terms(which):
        diagonal = lax.broadcasted_iota(jnp.int32, (HEADS, HEADS), 0) == lax.broadcasted_iota(
            jnp.int32, (HEADS, HEADS), 1
        )

        def upright(ref):
            return jnp.sum(jnp.where(diagonal, ref[which], 0.0), axis=1, keepdims=True)

        raw = jnp.concatenate(
            [steps[which, 0].astype(F32), steps[which, 1].astype(F32)], axis=1
        )
        raw = raw + upright(sb_ref)
        delta = jnp.maximum(raw, 0.0) + jnp.log1p(jnp.exp(-jnp.abs(raw)))
        rate = delta * (-jnp.exp(upright(dl_ref)))
        rows2 = lax.broadcasted_iota(jnp.int32, (seq, seq), 0)
        cols2 = lax.broadcasted_iota(jnp.int32, (seq, seq), 1)
        ones_up = jnp.where(rows2 <= cols2, 1.0, 0.0).astype(BF16)
        r_hi, r_rest = rate.astype(BF16), rate - rate.astype(BF16).astype(F32)
        r_mid, r_lo = split(r_rest)
        cumulative = dot(r_hi, ones_up, NN) + (dot(r_mid, ones_up, NN) + dot(r_lo, ones_up, NN))
        for at, value in enumerate((delta, cumulative, jax.nn.sigmoid(raw), rate)):
            top = pl.multiple_of(which * halves_of + at * HEADS, HEADS)
            token_rows[pl.ds(top, HEADS), :] = value
        token_cols[...] = token_rows[...].T

    def group(turn, _):
        j = turn + (turn // (HALF - 1)) * donor
        helping = j // HALF
        g = core * HALF + j - helping
        ours = helping == 0
        slot_p = j + helping
        lane0 = helping * halves_of
        cols = group_columns(g)
        blocks = [(0, cols[0])]
        for base, col in ((WIDE, cols[1]), (WIDE + STATE, cols[2])):
            for part in range(STATE // 128):
                blocks.append((base + part * 128, pl.multiple_of(col + part * 128, 128)))

        def conv_rows(start, count, fresh):
            for off, col in blocks:
                here = slice(off, off + 128)
                if fresh:
                    upad[pl.ds(pl.multiple_of(start + 8, 8), count), here] = uin[
                        j, pl.ds(start, count), here
                    ].astype(F32)
                window = upad[pl.ds(start, count + 8), here]
                z = b_ref[helping, :, pl.ds(col, 128)]
                z = z + w_ref[helping, 3:4, pl.ds(col, 128)] * window[8:]
                for k in range(CONV - 1):
                    tap = w_ref[helping, pl.ds(k, 1), pl.ds(col, 128)]
                    z = z + tap * pltpu.roll(window, 3 - k, 0)[8:]
                s = jax.nn.sigmoid(z)
                mix[pl.ds(start, count), here] = z * s
                dsl[pl.ds(start, count), here] = s * (1.0 + z * (1.0 - s))

        @pl.when(ours)
        def _():
            pltpu.make_async_copy(uin.at[j, mine], uin.at[j, mine], own_sem.at[j]).wait()

        @pl.when(helping == 1)
        def _():
            some = pl.ds(0, WIDE + 2 * STATE)
            for at, ref in enumerate((
                uin.at[HALF], steps.at[1], w_ref.at[pl.ds(1, 1), :, some], b_ref.at[1, :, some],
                ng_ref.at[1, :, pl.ds(0, WIDE)], sb_ref.at[1], dl_ref.at[1], sk_ref.at[1],
            )):
                remote(
                    ref, ref, ship_sem.at[at], ship_recv.at[at], core, sec + 1, dp
                ).wait_recv()

        conv_rows(pl.multiple_of(core * tok, tok), tok, True)

        @pl.when(j == 0)
        def _():
            own_step.wait()
            step_copy.wait()

        @pl.when(jnp.logical_and(j == 0, sec == 1))
        def _():
            pl.semaphore_wait(plane_sem, 1)
            for k in range(1, ndp):
                greet(core, 0, lax.rem(dp + k, ndp))

        @pl.when(lax.rem(j, HALF) == 0)
        def _():
            token_terms(helping)

        @pl.when(ours)
        def _():
            remote(
                uin.at[j, theirs], uin.at[j, theirs], xs_sem.at[j], xr_sem.at[j], other, sec, dp
            ).wait_recv()

        conv_rows(pl.multiple_of(other * tok, tok), tok, True)
        conv_rows(tok, 8, False)

        lane = lax.broadcasted_iota(jnp.int32, (seq, 128), 1)
        lane1 = lax.broadcasted_iota(jnp.int32, (1, 128), 1)
        lane16 = lax.broadcasted_iota(jnp.int32, (1, HEADS), 1)
        row = lax.broadcasted_iota(jnp.int32, (seq, seq), 0)
        column = lax.broadcasted_iota(jnp.int32, (seq, seq), 1)
        first = lane < HEAD_DIM

        def pick(at):
            return jnp.sum(
                jnp.where(lane == lane0 + at, token_cols[...], 0.0), axis=1, keepdims=True
            )

        def pick1(ref, h):
            return jnp.sum(jnp.where(lane16 == h, ref[helping], 0.0), axis=1, keepdims=True)

        x = mix[:, 0:WIDE]
        bmap = split(mix[:, WIDE : WIDE + STATE])
        cmap = split(mix[:, WIDE + STATE : MIX])
        h0 = g * REPS
        dt2 = jnp.where(first, pick(h0), pick(h0 + 1))
        skip2 = jnp.where(first[0:1], pick1(sk_ref, h0), pick1(sk_ref, h0 + 1))
        xs = x * dt2
        xs_p = split(xs)
        scores = dot3(cmap, bmap, NT)
        decay, mixed, ys = [], [], []
        for r in range(REPS):
            seg = pick(HEADS + h0 + r) - token_rows[pl.ds(lane0 + HEADS + h0 + r, 1), :]
            w = jnp.exp(jnp.where(row >= column, seg, -jnp.inf))
            a = scores * w
            a_p = split(a)
            decay.append(w)
            mixed.append((a, a_p))
            ys.append(dot3(a_p, xs_p, NN))
        y = jnp.where(first, ys[0], ys[1]) + skip2 * x
        gate = uin[j, :, MIX : MIX + WIDE].astype(F32)
        cot = uin[j, :, MIX + WIDE : MIX + 2 * WIDE].astype(F32)
        gain = ng_ref[helping, :, pl.ds(cols[0], WIDE)]
        s = jax.nn.sigmoid(gate)
        act = gate * s
        gated = y * act
        scale = lax.rsqrt(jnp.mean(gated * gated, axis=1, keepdims=True) + 1e-05)
        normed = gated * scale
        stage_o[j, :, 0:WIDE] = (normed * gain).astype(BF16)
        dn = cot * gain
        dgated = scale * (dn - normed * jnp.mean(dn * normed, axis=1, keepdims=True))
        dy = dgated * act
        stage_o[j, :, WIDE : 2 * WIDE] = (dgated * y * (s * (1.0 + gate * (1.0 - s)))).astype(BF16)

        even = lax.rem(j, 2) == 0
        out_cut = pl.ds(cols[0], WIDE)

        def send_half(base, t, dst, done, landed, s):
            remote(
                stage_o.at[j, pl.ds(t * tok, tok), pl.ds(base, WIDE)], dst, done, landed, t, s, dp
            ).start()

        direct = jnp.logical_and(
            ours, jnp.logical_and(sec < nsec - 1, jnp.logical_not(jnp.logical_and(sec == 1, even)))
        )

        @pl.when(direct)
        def _():
            for t in range(2):
                send_half(0, t, nxt.at[0, 0, :, out_cut], next_sem.at[0], next_sem.at[1], sec + 1)

        @pl.when(jnp.logical_and(ours, jnp.logical_and(sec == 1, even)))
        def _():
            slot = core * (HALF // 2) + j // 2
            for t in range(2):
                send_half(0, t, relay.at[slot], next_sem.at[0], relay_sem.at[slot], 3)

        @pl.when(jnp.logical_and(ours, jnp.logical_or(sec == 1, sec == 3)))
        def _():
            for t in range(2):
                send_half(
                    WIDE, t, ggate.at[0, 0, :, out_cut], gate_sem.at[0], gate_sem.at[1], sec - 1
                )

        @pl.when(jnp.logical_and(ours, sec == 2))
        def _():
            slot = core * HALF + j
            for t in range(2):
                send_half(WIDE, t, relay.at[slot], gate_sem.at[0], relay_sem.at[slot], 0)

        @pl.when(helping == 1)
        def _():
            ggate[0, 0, :, out_cut] = stage_o[j, tok : 2 * tok, WIDE : 2 * WIDE]
            send_half(WIDE, 0, ggate.at[0, 0, :, out_cut], gate_sem.at[0], gate_sem.at[1], sec)

        @pl.when(jnp.logical_and(helping == 1, sec < nsec - 2))
        def _():
            for t in range(2):
                send_half(0, t, nxt.at[0, 0, :, out_cut], next_sem.at[0], next_sem.at[1], sec + 2)

        partial[dp, slot_p, 5:6, 0:WIDE] = jnp.sum(cot * normed, axis=0, keepdims=True)
        dyx = jnp.sum(dy * x, axis=0, keepdims=True)
        dscore = jnp.zeros((seq, seq), F32)
        dy_p = split(dy)
        das = []
        for r in range(REPS):
            own = first if r == 0 else jnp.logical_not(first)
            da = dot3(split(jnp.where(own, dy, 0.0)), xs_p, NT)
            das.append(da)
            dscore = dscore + da * decay[r]
        ds_p = split(dscore)

        def conv_back(off, width, start):
            for part in range(width // 128):
                here = slice(off + part * 128, off + part * 128 + 128)
                col = pl.multiple_of(start + part * 128, 128)
                dz = zpad[0:seq, here]
                du = jnp.zeros((seq, 128), F32)
                for k in range(CONV):
                    du = du + (
                        w_ref[helping, pl.ds(k, 1), pl.ds(col, 128)]
                        * zpad[3 - k : 3 - k + seq, here]
                    )
                    partial[dp, slot_p, pl.ds(k, 1), here] = jnp.sum(
                        dz * upad[5 + k : 5 + k + seq, here], axis=0, keepdims=True
                    )
                partial[dp, slot_p, pl.ds(4, 1), here] = jnp.sum(dz, axis=0, keepdims=True)
                stage_c[j, :, here] = du.astype(BF16)

            @pl.when(helping == 1)
            def _():
                gconv[0, 0, :, pl.ds(start, width)] = stage_c[j, tok : 2 * tok, off : off + width]
                remote(
                    stage_c.at[j, pl.ds(0, tok), pl.ds(off, width)],
                    gconv.at[0, 0, :, pl.ds(start, width)],
                    conv_sem.at[0], conv_sem.at[1], 0, sec, dp,
                ).start()

            @pl.when(jnp.logical_and(ours, sec > 0))
            def _():
                for t in range(2):
                    remote(
                        stage_c.at[j, pl.ds(t * tok, tok), pl.ds(off, width)],
                        gconv.at[0, 0, :, pl.ds(start, width)],
                        conv_sem.at[0], conv_sem.at[1], t, sec - 1, dp,
                    ).start()

        zpad[0:seq, WIDE + STATE : MIX] = dot3(ds_p, bmap, NN) * dsl[:, WIDE + STATE : MIX]
        conv_back(WIDE + STATE, STATE, cols[2])
        zpad[0:seq, WIDE : WIDE + STATE] = dot3(ds_p, cmap, TN) * dsl[:, WIDE : WIDE + STATE]
        conv_back(WIDE, STATE, cols[1])
        dxs = jnp.where(first, dot3(mixed[0][1], dy_p, TN), dot3(mixed[1][1], dy_p, TN))
        zpad[0:seq, 0:WIDE] = (skip2 * dy + dxs * dt2) * dsl[:, 0:WIDE]
        conv_back(0, WIDE, cols[0])
        upper = jnp.where(row <= column, 1.0, 0.0).astype(BF16)
        dxx = dxs * x
        for r in range(REPS):
            own = first if r == 0 else jnp.logical_not(first)
            p = split(das[r] * mixed[r][0])
            later = dot(upper, p[0], NN) + dot(upper, p[1], NN)
            dr = jnp.sum(jnp.where(row > column, later, 0.0), axis=1, keepdims=True)
            drate[...] += jnp.where(lane == lane0 + h0 + r, dr, 0.0)
            total = jnp.sum(jnp.where(own[0:1], dyx, 0.0), axis=1, keepdims=True)
            small[2:3, :] += jnp.where(lane1 == lane0 + h0 + r, total, 0.0)
            dd = jnp.sum(jnp.where(own, dxx, 0.0), axis=1, keepdims=True)
            ddt[...] += jnp.where(lane == lane0 + h0 + r, dd, 0.0)

        @pl.when(jnp.logical_and(j == 0, sec == 0))
        def _():
            pl.semaphore_wait(plane_sem, 1)
            pl.semaphore_wait(barrier, ndp - 1)
            for s in range(1, 4):
                pl.semaphore_signal(
                    world_sem, inc=1, device_id=place(core, s, dp), device_id_type=MESH
                )

        @pl.when(jnp.logical_and(j == 0, sec > 0))
        def _():
            pl.semaphore_wait(world_sem, 1)

        @pl.when(ours)
        def _():
            spread(j)

        @pl.when(helping == 1)
        def _():
            remote(
                partial.at[dp, HALF + 1], partial.at[dp, HALF - 1],
                hand_sem.at[0], hand_sem.at[1], core, sec + 1, dp,
            ).start()

        return 0

    def spread(slot):
        for k in range(1, ndp):
            to = lax.rem(dp + k, ndp)
            remote(
                partial.at[dp, slot], partial.at[dp, slot], ps_sem.at[to], pr_sem.at[dp],
                core, sec, to,
            ).start()

    lax.fori_loop(0, own_groups + helper, group, 0)

    def pass_on(slot, g, out, landed, s):
        part = relay.at[slot]
        remote(part, part, via_sem.at[0], relay_sem.at[slot], core, s, dp).wait_recv()
        remote(
            part, out.at[0, 0, :, pl.ds(g * WIDE, WIDE)], via_sem.at[0], landed, core, s, dp
        ).start()

    @pl.when(sec == 0)
    def _():
        for g in range(GROUPS - 1):
            pass_on(g, g, ggate, gate_sem.at[1], 1)

    @pl.when(sec == 3)
    def _():
        for at in range(GROUPS // 2):
            pass_on(at, 2 * at, nxt, next_sem.at[1], 2)

    @pl.when(sec == 0)
    def _():
        nxt[...] = jnp.zeros_like(nxt)

    @pl.when(sec == nsec - 1)
    def _():
        gconv[...] = jnp.zeros_like(gconv)
        ggate[...] = jnp.zeros_like(ggate)
        gstep[...] = jnp.zeros_like(gstep)

    def step_terms(which, into):
        lane0 = which * halves_of
        heads = slice(lane0, lane0 + HEADS)
        dr16 = drate[:, heads]
        gate = token_cols[:, lane0 + 2 * HEADS : lane0 + 3 * HEADS]
        rate = token_cols[:, lane0 + 3 * HEADS : lane0 + 4 * HEADS]
        dstep = (ddt[:, heads] - dr16 * jnp.exp(dl_ref[which])) * gate
        into[0:1, 0:HEADS] = jnp.sum(dstep, axis=0, keepdims=True)
        into[1:2, 0:HEADS] = jnp.sum(dr16 * rate, axis=0, keepdims=True)
        drate[:, heads] = dstep

    step_terms(0, small)

    @pl.when(helper == 1)
    def _():
        step_terms(1, small_out)
        small_out[2:3, 0:HEADS] = small[2:3, halves_of : halves_of + HEADS]
        remote(
            small_out, small_in, hand_sem.at[2], hand_sem.at[3], core, sec + 1, dp
        ).start()

    turned = drate[...].T
    for t in range(2):
        stage_s[t] = turned[0:HEADS, t * tok : (t + 1) * tok].astype(BF16)

    @pl.when(sec > 0)
    def _():
        for t in range(2):
            remote(
                stage_s.at[t], step_parts.at[core],
                dstep_sem.at[2], dstep_sem.at[core], t, sec - 1, dp,
            ).start()

    @pl.when(helper == 1)
    def _():
        stage_s[2] = turned[halves_of : halves_of + HEADS, 0:tok].astype(BF16)
        step_parts[2] = turned[halves_of : halves_of + HEADS, tok : 2 * tok].astype(BF16)
        remote(
            stage_s.at[2], step_parts.at[2], dstep_sem.at[4], dstep_sem.at[3], other, sec, dp
        ).start()

    @pl.when(donor == 1)
    def _():
        landed = partial.at[dp, HALF - 1]
        remote(landed, landed, hand_sem.at[0], hand_sem.at[1], core, sec - 1, dp).wait_recv()
        spread(HALF - 1)
        remote(small_in, small_in, hand_sem.at[2], hand_sem.at[3], core, sec - 1, dp).wait_recv()
        small[...] += small_in[...]

    partial[dp, HALF, :, 0:128] = small[...]
    spread(HALF)
    for k in range(1, ndp):
        to = lax.rem(dp + k, ndp)
        remote(
            partial.at[dp, pl.ds(0, HALF + 1)], partial.at[to, pl.ds(0, HALF + 1)],
            ps_sem.at[to], pr_sem.at[to], core, sec, to,
        ).wait()
    total = partial[0, 0 : HALF + 1]
    for k in range(1, ndp):
        total = total + partial[k, 0 : HALF + 1]
    final[core] = total
    halves = remote(final.at[core], final.at[core], fin_sem.at[0], fin_sem.at[1], other, sec, dp)
    halves.start()
    remote(final.at[core], final.at[other], fin_sem.at[0], fin_sem.at[1], other, sec, dp).wait()
    for g in range(GROUPS):
        c, j = g // HALF, g % HALF
        gng[0:1, g * WIDE : (g + 1) * WIDE] = final[c, j, 5:6, 0:WIDE]
        for off, width, col in (
            (0, WIDE, g * WIDE),
            (WIDE, STATE, INNER + g * STATE),
            (WIDE + STATE, STATE, INNER + (GROUPS + g) * STATE),
        ):
            gtap[0, :, col : col + width] = final[c, j, 0:CONV, off : off + width]
            gcb[0:1, col : col + width] = final[c, j, CONV : CONV + 1, off : off + width]
    for at, ref in enumerate((gsb, gdl, gsk)):
        ref[...] = final[0, HALF, at : at + 1, 0:HEADS] + final[1, HALF, at : at + 1, 0:HEADS]

    @pl.when(sec < nsec - 1)
    def _():
        for c in range(2):
            part = step_parts.at[c]
            remote(part, part, dstep_sem.at[2], dstep_sem.at[c], core, sec + 1, dp).wait_recv()

        @pl.when(core == 0)
        def _():
            part = step_parts.at[2]
            remote(part, part, dstep_sem.at[4], dstep_sem.at[3], other, sec, dp).wait_recv()

        both = step_parts[0].astype(F32) + step_parts[1].astype(F32)
        gstep[0, 0] = (both + step_parts[2].astype(F32)).astype(BF16)

    def sent(ref, sem):
        remote(ref, ref, sem, sem, other, sec, dp).wait_send()

    def landed(ref, sem):
        remote(ref, ref, sem, sem, other, sec, dp).wait_recv()

    def exchanged(j, _):
        sent(uin.at[j, mine], xs_sem.at[j])
        return 0

    lax.fori_loop(0, HALF - other * gives, exchanged, 0)
    first = pl.ds(0, HALF - 1)
    half = pl.ds(0, WIDE)

    @pl.when(sec == 0)
    def _():
        sent(relay.at[pl.ds(0, GROUPS - 1)], via_sem.at[0])

    @pl.when(sec == nsec - 1)
    def _():
        sent(relay.at[pl.ds(0, GROUPS // 2)], via_sem.at[0])

    @pl.when(sec > 0)
    def _():
        sent(uin.at[HALF, pl.ds(0, tok)], ship_sem.at[0])
        sent(steps.at[1, 0], ship_sem.at[1])
        sent(stage_c.at[first], conv_sem.at[0])
        sent(stage_o.at[first, :, half], gate_sem.at[0])
        sent(stage_s.at[pl.ds(0, 2)], dstep_sem.at[2])
        landed(nxt.at[0, 0], next_sem.at[1])

    @pl.when(jnp.logical_and(sec > 0, core == 0))
    def _():
        some = pl.ds(0, WIDE + 2 * STATE)
        sent(w_ref.at[pl.ds(1, 1), :, some], ship_sem.at[2])
        sent(b_ref.at[1, :, some], ship_sem.at[3])
        sent(ng_ref.at[1, :, half], ship_sem.at[4])
        sent(sb_ref.at[1], ship_sem.at[5])
        sent(dl_ref.at[1], ship_sem.at[6])
        sent(sk_ref.at[1], ship_sem.at[7])
        sent(stage_c.at[HALF - 1], conv_sem.at[0])
        sent(stage_o.at[HALF - 1, :, half], gate_sem.at[0])

    @pl.when(sec < nsec - 1)
    def _():
        sent(stage_o.at[first, :, half], next_sem.at[0])

    @pl.when(jnp.logical_and(sec < nsec - 1, donor == 0))
    def _():
        sent(stage_o.at[HALF - 1, :, half], next_sem.at[0])

    @pl.when(helper == 1)
    def _():
        sent(stage_c.at[HALF, pl.ds(0, tok)], conv_sem.at[0])
        sent(stage_o.at[HALF, pl.ds(0, tok), half], gate_sem.at[0])
        sent(stage_s.at[2], dstep_sem.at[4])
        sent(partial.at[dp, HALF + 1], hand_sem.at[0])
        sent(small_out, hand_sem.at[2])
        landed(ggate.at[0, 0, :, pl.ds(0, INNER - WIDE)], gate_sem.at[1])
        landed(gconv.at[0, 0, :, pl.ds(0, (GROUPS - 1) * MIX)], conv_sem.at[1])

    @pl.when(jnp.logical_and(helper == 1, sec < nsec - 2))
    def _():
        sent(stage_o.at[HALF, :, half], next_sem.at[0])

    @pl.when(jnp.logical_and(sec < nsec - 1, core == 0))
    def _():
        landed(ggate.at[0, 0], gate_sem.at[1])
        landed(gconv.at[0, 0], conv_sem.at[1])


def finish_kernel(*refs):
    count = len(refs) // 2
    sem = refs[-1]
    copies = [pltpu.make_async_copy(refs[i], refs[count + i], sem.at[i]) for i in range(count)]
    for copy in copies:
        copy.start()
    for copy in copies:
        copy.wait()


def paired(
    conv_input, gate_input, step_input, cotangent, conv_weight,
    conv_bias, step_bias, decay_log, skip_gain, norm_gain,
):
    tok = conv_input.shape[2]
    seq = 2 * tok
    ndp = lax.axis_size("dp")
    hbm = pl.BlockSpec(memory_space=pl.ANY)
    vmem = pl.BlockSpec(memory_space=pltpu.VMEM)
    scratch = [
        pltpu.VMEM((2,) + conv_weight.shape[1:], F32),
        pltpu.VMEM((2,) + conv_bias.shape, F32),
        pltpu.VMEM((2,) + step_bias.shape, F32),
        pltpu.VMEM((2,) + decay_log.shape, F32),
        pltpu.VMEM((2,) + skip_gain.shape, F32),
        pltpu.VMEM((2,) + norm_gain.shape, F32),
        pltpu.VMEM((HALF + 1, seq, MIX + 2 * WIDE), BF16),
        pltpu.VMEM((2, 2, HEADS, tok), BF16),
        pltpu.VMEM((128, seq), F32),
        pltpu.VMEM((seq, 128), F32),
        pltpu.VMEM((seq + 8, MIX), F32),
        pltpu.VMEM((seq + 8, MIX), F32),
        pltpu.VMEM((seq, MIX), F32),
        pltpu.VMEM((seq, MIX), F32),
        pltpu.VMEM((seq, 128), F32),
        pltpu.VMEM((seq, 128), F32),
        pltpu.VMEM((8, 128), F32),
        pltpu.VMEM((HALF + 1, seq, MIX), BF16),
        pltpu.VMEM((HALF + 1, seq, 2 * WIDE), BF16),
        pltpu.VMEM((3, HEADS, tok), BF16),
        pltpu.VMEM((3, HEADS, tok), BF16),
        pltpu.VMEM((ndp, HALF + 2, 8, MIX), F32),
        pltpu.VMEM((2, HALF + 1, 8, MIX), F32),
        pltpu.VMEM((GROUPS, tok, WIDE), BF16),
        pltpu.VMEM((8, 128), F32),
        pltpu.VMEM((8, 128), F32),
        pltpu.SemaphoreType.DMA((HALF,)),
        pltpu.SemaphoreType.DMA((HALF,)),
        pltpu.SemaphoreType.DMA((HALF,)),
        pltpu.SemaphoreType.DMA((3,)),
        pltpu.SemaphoreType.DMA((2,)),
        pltpu.SemaphoreType.DMA((2,)),
        pltpu.SemaphoreType.DMA((2,)),
        pltpu.SemaphoreType.DMA((5,)),
        pltpu.SemaphoreType.DMA((ndp,)),
        pltpu.SemaphoreType.DMA((ndp,)),
        pltpu.SemaphoreType.DMA((2,)),
        pltpu.SemaphoreType.DMA((1,)),
        pltpu.SemaphoreType.DMA((GROUPS,)),
        pltpu.SemaphoreType.DMA((6,)),
        pltpu.SemaphoreType.REGULAR,
        pltpu.SemaphoreType.REGULAR,
        pltpu.SemaphoreType.REGULAR,
        pltpu.SemaphoreType.DMA((8,)),
        pltpu.SemaphoreType.DMA((8,)),
        pltpu.SemaphoreType.DMA((4,)),
    ]
    turned = jnp.swapaxes(step_input, 2, 3)
    shapes = [
        (gate_input.shape, BF16),
        (conv_input.shape, BF16),
        (gate_input.shape, BF16),
        (turned.shape, BF16),
        (conv_weight.shape, F32),
        (conv_bias.shape, F32),
        (step_bias.shape, F32),
        (decay_log.shape, F32),
        (skip_gain.shape, F32),
        (norm_gain.shape, F32),
    ]
    inputs = [
        pltpu.with_memory_space_constraint(a, pltpu.HBM)
        for a in (
            conv_input, gate_input, turned, cotangent, conv_weight,
            conv_bias, step_bias, decay_log, skip_gain, norm_gain,
        )
    ]
    sent = pl.pallas_call(
        pair_kernel,
        name="mixer_tick",
        in_specs=[hbm] * 10,
        out_specs=[vmem] * 10,
        out_shape=[pltpu.VMEM(shape, kind) for shape, kind in shapes],
        scratch_shapes=scratch,
        compiler_params=pltpu.CompilerParams(
            collective_id=0, has_side_effects=True, vmem_limit_bytes=24 * 1024 * 1024
        ),
    )(*inputs)
    done = pl.pallas_call(
        finish_kernel,
        name="mixer_finish",
        in_specs=[vmem] * 10,
        out_specs=[hbm] * 10,
        out_shape=[jax.ShapeDtypeStruct(shape, kind) for shape, kind in shapes],
        scratch_shapes=[pltpu.SemaphoreType.DMA((10,))],
        compiler_params=pltpu.CompilerParams(vmem_limit_bytes=1024 * 1024),
    )(*sent)
    return tuple(done[:3]) + (jnp.swapaxes(done[3], 2, 3),) + tuple(done[4:])


def solution(mesh):
    in_specs = (
        P("section", "dp", "ctx", None),
        P("section", "dp", "ctx", None),
        P("section", "dp", "ctx", None),
        P("section", "dp", "ctx", None),
        P("section", None, None),
        P("section", None),
        P("section", None),
        P("section", None),
        P("section", None),
        P("section", None),
    )
    out_specs = (
        P("section", "dp", "ctx", None),
        P("section", "dp", "ctx", None),
        P("section", "dp", "ctx", None),
        P("section", "dp", "ctx", None),
        P("section", None, None),
        P("section", None),
        P("section", None),
        P("section", None),
        P("section", None),
        P("section", None),
    )
    body = paired if (mesh.shape["ctx"], mesh.shape["section"]) == (2, 4) else shards
    return jax.shard_map(body, mesh=mesh, in_specs=in_specs, out_specs=out_specs, check_vma=False)
```

```python
import functools
import jax
import jax.numpy as jnp
from jax import lax
from jax.experimental import pallas as pl
from jax.experimental.pallas import tpu as pltpu
from jax.sharding import PartitionSpec as P

HEADS = 16
HEAD_DIM = 64
STATE = 256
GROUPS = 8
CONV = 4


HIGH_BOUND = lax.Precision.HIGHEST


def shifted(block, axis, distance):
    devices = range(lax.axis_size(axis))
    route = [(i - distance, i) for i in devices if i - distance in devices]
    return lax.ppermute(block, axis, route)


def prefix(part, axis, combine, identity):
    count = lax.axis_size(axis)
    place = lax.axis_index(axis)
    ahead = count - 1 - place
    gathered = jax.tree.map(lambda a: lax.all_gather(a, axis), part)
    state = jax.tree.map(lambda a, e: jnp.zeros_like(a) + jnp.asarray(e, a.dtype), part, identity)

    def one(turn, state):
        source = count - 1 - turn
        return combine(
            state, jax.tree.map(lambda a: lax.dynamic_index_in_dim(a, source, 0, False), gathered)
        )

    return lax.fori_loop(0, ahead, one, state)


def conv_mix(extended, taps, initial_offset):
    rows = extended.shape[0] - (CONV - 1)
    total = initial_offset[None, :]
    for tap in range(CONV):
        total = total + taps[tap][None, :] * extended[tap : tap + rows]
    return jax.nn.silu(total)


def split_mix(mixed, steps, step_shift, damping_exponents):
    rows = mixed.shape[0]
    inner = HEADS * HEAD_DIM
    payload_lines = mixed[:, :inner].reshape(rows, GROUPS, HEADS // GROUPS, HEAD_DIM)
    in_maps = mixed[:, inner : inner + GROUPS * STATE].reshape(rows, GROUPS, STATE)
    out_maps = mixed[:, inner + GROUPS * STATE :].reshape(rows, GROUPS, STATE)
    delta = jax.nn.softplus(steps + step_shift[None, :])
    upto = jnp.tril(jnp.ones((rows, rows), jnp.float32))
    rates = delta * (-jnp.exp(damping_exponents))[None, :]
    cumulative = jnp.dot(upto, rates, precision=HIGH_BOUND)
    return (payload_lines, in_maps, out_maps, delta, cumulative)


def fragment_condition(extended, steps, taps, initial_offset, step_shift, damping_exponents):
    payload_lines, in_maps, out_maps, delta, cumulative = split_mix(
        conv_mix(extended, taps, initial_offset), steps, step_shift, damping_exponents
    )
    rows = payload_lines.shape[0]
    total = cumulative[-1]
    weight = (jnp.exp(total[None, :] - cumulative) * delta).reshape(rows, GROUPS, HEADS // GROUPS)
    state = jnp.einsum(
        "tgrp,tgn->grpn", payload_lines * weight[..., None], in_maps, precision=HIGH_BOUND
    )
    return (state.reshape(HEADS, HEAD_DIM, STATE), total)


def shard_layer(
    extended,
    gates,
    steps,
    taps,
    initial_offset,
    step_shift,
    damping_exponents,
    skip_values,
    gain_values,
    carried,
):
    payload_lines, in_maps, out_maps, delta, cumulative = split_mix(
        conv_mix(extended, taps, initial_offset), steps, step_shift, damping_exponents
    )
    rows = payload_lines.shape[0]
    reps = HEADS // GROUPS
    lower = (jnp.arange(rows)[:, None] >= jnp.arange(rows)[None, :])[None]
    seg = cumulative.T[:, :, None] - cumulative.T[:, None, :]
    weight = jnp.exp(jnp.where(lower, seg, -jnp.inf)).reshape(GROUPS, reps, rows, rows)
    intersection_maps = jnp.einsum("tgn,sgn->gts", out_maps, in_maps, precision=HIGH_BOUND)
    score_matrix = weight * intersection_maps[:, None]
    scaled_values = payload_lines * delta.reshape(rows, GROUPS, reps)[..., None]
    final_output = jnp.einsum("jzlh,hjzc->ljzc", score_matrix, scaled_values, precision=HIGH_BOUND)
    incoming = jnp.einsum(
        "tgn,grpn->tgrp",
        out_maps,
        carried.reshape(GROUPS, reps, HEAD_DIM, STATE),
        precision=HIGH_BOUND,
    )
    final_output = (
        final_output + incoming * jnp.exp(cumulative).reshape(rows, GROUPS, reps)[..., None]
    )
    final_output = (
        final_output + skip_values.reshape(GROUPS, reps)[None, :, :, None] * payload_lines
    )
    gated = final_output.reshape(rows, GROUPS, -1) * jax.nn.silu(gates).reshape(rows, GROUPS, -1)
    normed = gated * lax.rsqrt(jnp.mean(gated * gated, axis=-1, keepdims=True) + 1e-05)
    return normed.reshape(rows, -1) * gain_values[None, :]


def combine(earlier, later):
    return (earlier[0] * later[0], later[0][:, None] * earlier[1] + later[1])


def shards(
    conv_input,
    gate_input,
    step_input,
    cotangent,
    conv_weight,
    conv_bias,
    step_bias,
    decay_log,
    skip_gain,
    norm_gain,
):
    local_rows = conv_input[0, 0]
    count = local_rows.shape[0]
    taps, initial_offset = (conv_weight[0], conv_bias[0])
    step_shift, damping_exponents = (step_bias[0], decay_log[0])
    skip_values, gain_values = (skip_gain[0], norm_gain[0])
    previous = shifted(local_rows[count - (CONV - 1) :], "ctx", 1)
    extended = jnp.concatenate([previous, local_rows], 0).astype(jnp.float32)
    gates = gate_input[0, 0].astype(jnp.float32)
    steps = step_input[0, 0].astype(jnp.float32)
    (state, total), state_pull = jax.vjp(
        fragment_condition, extended, steps, taps, initial_offset, step_shift, damping_exponents
    )
    decay = jnp.exp(total)
    flat_state = state.reshape(HEADS, HEAD_DIM * STATE)
    unity = (jnp.ones((HEADS,), jnp.float32), jnp.zeros((HEADS, HEAD_DIM * STATE), jnp.float32))

    def advance(index, current):
        return shifted(decay[:, None] * current + flat_state, "ctx", 1)

    incoming = lax.fori_loop(
        0, lax.axis_size("ctx") - 1, advance, jnp.zeros((HEADS, HEAD_DIM * STATE), jnp.float32)
    )
    carried = incoming.reshape(HEADS, HEAD_DIM, STATE)
    final_output, layer_pull = jax.vjp(
        shard_layer,
        extended,
        gates,
        steps,
        taps,
        initial_offset,
        step_shift,
        damping_exponents,
        skip_values,
        gain_values,
        carried,
    )
    forward = shifted(final_output.astype(jnp.bfloat16)[None, None], "section", 1)
    grads = layer_pull(cotangent[0, 0].astype(jnp.float32))
    carry_grad = grads[9].reshape(HEADS, HEAD_DIM * STATE)
    outgoing = prefix((decay, carry_grad), "ctx", combine, unity)[1]
    outgoing_grad = outgoing.reshape(HEADS, HEAD_DIM, STATE)
    total_grad = jnp.sum(outgoing_grad * carried, axis=(1, 2)) * decay
    extra = state_pull((outgoing_grad, total_grad))
    ext_grad = grads[0] + extra[0]
    step_grad = grads[2] + extra[1]
    param_terms = (
        grads[3] + extra[2],
        grads[4] + extra[3],
        grads[5] + extra[4],
        grads[6] + extra[5],
        grads[7],
        grads[8],
    )
    returned = shifted(ext_grad[: CONV - 1], "ctx", -1)
    own_grad = ext_grad[CONV - 1 :]
    row_grad = jnp.concatenate(
        [own_grad[: count - (CONV - 1)], own_grad[count - (CONV - 1) :] + returned], 0
    )
    backward = shifted(
        (
            row_grad.astype(jnp.bfloat16)[None, None],
            grads[1].astype(jnp.bfloat16)[None, None],
            step_grad.astype(jnp.bfloat16)[None, None],
        ),
        "section",
        -1,
    )
    summed = lax.psum(
        (
            param_terms[0],
            param_terms[1],
            param_terms[2],
            param_terms[3],
            param_terms[4],
            param_terms[5],
        ),
        ("ctx", "dp"),
    )
    return (
        forward,
        backward[0],
        backward[1],
        backward[2],
        summed[0][None],
        summed[1][None],
        summed[2][None],
        summed[3][None],
        summed[4][None],
        summed[5][None],
    )


MESH = pl.DeviceIdType.MESH
F32 = jnp.float32
BF16 = jnp.bfloat16
INNER = HEADS * HEAD_DIM
REPS = HEADS // GROUPS
WIDE = REPS * HEAD_DIM
MIX = WIDE + 2 * STATE
HALF = GROUPS // 2
NN = ((1,), (0,))
NT = ((1,), (1,))
TN = ((0,), (0,))


def split(a):
    high = a.astype(BF16)
    return high, (a - high.astype(F32)).astype(BF16)


def dot(a, b, dims):
    return lax.dot_general(a, b, (dims, ((), ())), preferred_element_type=F32)


def dot3(a, b, dims):
    return dot(a[0], b[0], dims) + (dot(a[0], b[1], dims) + dot(a[1], b[0], dims))


def group_columns(g):
    return (
        pl.multiple_of(g * WIDE, 128),
        pl.multiple_of(INNER + g * STATE, 128),
        pl.multiple_of(INNER + (GROUPS + g) * STATE, 128),
    )


def pair_kernel(
    conv_in, gate_in, step_in, cot_in, w_in, b_in, sb_in, dl_in, sk_in, ng_in,
    nxt, gconv, ggate, gstep, gtap, gcb, gsb, gdl, gsk, gng,
    w_ref, b_ref, per_head, ng_ref,
    uin, steps, token_rows, token_cols, upad, zpad, mix, dsl, ddt, drate, small,
    stage_c, stage_o, stage_s, step_parts, partial, final, relay, small_out, small_in,
    own_sem, xr_sem, sent_sem, land_sem, load_sem, step_sem, ship_sem, relay_sem, dstep_sem,
    sum_sem, hand_sem, fin_sem, pair_sem, plane_sem, world_sem,
):
    core = lax.axis_index("ctx")
    sec = lax.axis_index("section")
    dp = lax.axis_index("dp")
    nsec = lax.axis_size("section")
    ndp = lax.axis_size("dp")
    tok = conv_in.shape[2]
    seq = 2 * tok
    other = 1 - core
    gives = (sec + nsec - 1) // nsec
    takes = 1 - sec // (nsec - 1)
    donor = core * gives
    helper = core * takes
    own_groups = HALF - donor
    last = GROUPS - 1
    halves_of = 4 * HEADS

    def place(c, s, d):
        return {"ctx": c, "section": s, "dp": d}

    def remote(src, dst, recv, c, s, d):
        return pltpu.make_async_remote_copy(
            src_ref=src, dst_ref=dst, send_sem=sent_sem, recv_sem=recv,
            device_id=place(c, s, d), device_id_type=MESH,
        )

    after = lax.rem(sec + 1, nsec)
    before = lax.rem(sec + nsec - 1, nsec)
    sb_ref, dl_ref, sk_ref = (per_head.at[:, at] for at in range(3))
    barrier = pltpu.get_barrier_semaphore()

    def greet(c, s, d):
        pl.semaphore_signal(barrier, inc=1, device_id=place(c, s, d), device_id_type=MESH)

    for c in range(2):
        for s in (1, 3):

            @pl.when(jnp.logical_and(sec // 2 == s // 2, jnp.logical_or(sec != s, core != c)))
            def _():
                greet(c, s, dp)

    def pieces(g):
        xc, bc, cc = group_columns(g)
        return (
            (conv_in.at[0, 0, :, pl.ds(xc, WIDE)], 0, WIDE),
            (conv_in.at[0, 0, :, pl.ds(bc, STATE)], WIDE, STATE),
            (conv_in.at[0, 0, :, pl.ds(cc, STATE)], WIDE + STATE, STATE),
            (gate_in.at[0, 0, :, pl.ds(xc, WIDE)], MIX, WIDE),
            (cot_in.at[0, 0, :, pl.ds(xc, WIDE)], MIX + WIDE, WIDE),
        )

    mine = pl.ds(pl.multiple_of(core * tok, tok), tok)
    theirs = pl.ds(pl.multiple_of(other * tok, tok), tok)
    upper = lax.rem(sec, 2) == 1

    def tell(sem, s):
        pl.semaphore_signal(sem, inc=1, device_id=place(core, s, dp), device_id_type=MESH)

    @pl.when(upper)
    def _():
        pl.semaphore_wait(barrier, 3)

    def landed(ref, sem):
        remote(ref, ref, sem, other, sec, dp).wait_recv()

    def sent(ref):
        remote(ref, ref, sent_sem, other, sec, dp).wait_send()

    def hand(src, dst, at):
        return remote(src, dst, ship_sem.at[at], 1, sec - 1, dp)

    def hand_over():
        for src, off, width in pieces(last):
            hand(src, uin.at[HALF, mine, pl.ds(off, width)], 0).start()
        hand(step_in.at[0, 0], steps.at[1, core], 1).start()

    def hand_params():
        xc, bc, cc = group_columns(last)
        for col, width in ((xc, WIDE), (bc, STATE), (cc, STATE)):
            cut = pl.ds(col, width)
            hand(w_in.at[:, :, cut], w_ref.at[pl.ds(1, 1), :, cut], 2).start()
            hand(b_in.at[:, cut], b_ref.at[1, :, cut], 3).start()
        cut = pl.ds(xc, WIDE)
        hand(ng_in.at[:, cut], ng_ref.at[1, :, cut], 4).start()
        hand(sb_in, sb_ref.at[1], 5).start()
        hand(dl_in, dl_ref.at[1], 5).start()
        hand(sk_in, sk_ref.at[1], 5).start()

    @pl.when(upper)
    def _():
        tell(pair_sem, sec - 1)
        hand_over()

    @pl.when(sec == 1)
    def _():
        greet(core, 2, dp)

    own_step = pltpu.make_async_copy(step_in.at[0, 0], steps.at[0, core], load_sem.at[0])
    own_step.start()

    def fetch(j, _):
        for src, off, width in pieces(core * HALF + j):
            pltpu.make_async_copy(
                src, uin.at[j, mine, pl.ds(off, width)], own_sem.at[j]
            ).start()
        return 0

    fetch(0, 0)
    params = [
        pltpu.make_async_copy(src, dst, load_sem.at[at])
        for src, dst, at in (
            (sb_in, sb_ref.at[0], 1), (dl_in, dl_ref.at[0], 1), (sk_in, sk_ref.at[0], 1),
            (w_in, w_ref.at[pl.ds(0, 1)], 2), (b_in, b_ref.at[0], 3), (ng_in, ng_ref.at[0], 4),
        )
    ]
    for copy in params:
        copy.start()
    lax.fori_loop(1, own_groups, fetch, 0)
    upad[0:8, :] = jnp.zeros((8, MIX), F32)
    zpad[seq : seq + 8, :] = jnp.zeros((8, MIX), F32)
    for ref in (token_rows, ddt, drate, small, small_out):
        ref[...] = jnp.zeros_like(ref)

    @pl.when(jnp.logical_not(upper))
    def _():
        pl.semaphore_wait(pair_sem, 1)

    remote(step_in.at[0, 0], steps.at[0, core], step_sem, other, sec, dp).start()

    def exchange(j, _):
        for src, off, width in pieces(other * HALF + j):
            remote(
                src, uin.at[j, mine, pl.ds(off, width)], xr_sem.at[j], other, sec, dp
            ).start()
        return 0

    exchange(0, 0)

    @pl.when(sec == 2)
    def _():
        pl.semaphore_wait(barrier, 1)
        tell(plane_sem, 0)
        tell(plane_sem, 1)
        hand_over()

    @pl.when(jnp.logical_and(sec > 0, core == 0))
    def _():
        hand_params()

    lax.fori_loop(1, HALF - other * gives, exchange, 0)
    own_step.wait()
    pltpu.make_async_copy(per_head.at[0], per_head.at[0], load_sem.at[1]).wait()
    for copy in params[3:]:
        copy.wait()

    def token_terms(which):
        diagonal = lax.broadcasted_iota(jnp.int32, (HEADS, HEADS), 0) == lax.broadcasted_iota(
            jnp.int32, (HEADS, HEADS), 1
        )

        def upright(ref):
            return jnp.sum(jnp.where(diagonal, ref[which], 0.0), axis=1, keepdims=True)

        raw = jnp.concatenate(
            [steps[which, 0].astype(F32), steps[which, 1].astype(F32)], axis=1
        )
        raw = raw + upright(sb_ref)
        delta = jnp.maximum(raw, 0.0) + jnp.log1p(jnp.exp(-jnp.abs(raw)))
        rate = delta * (-jnp.exp(upright(dl_ref)))
        rows2 = lax.broadcasted_iota(jnp.int32, (seq, seq), 0)
        cols2 = lax.broadcasted_iota(jnp.int32, (seq, seq), 1)
        ones_up = jnp.where(rows2 <= cols2, 1.0, 0.0).astype(BF16)
        r_hi, r_rest = rate.astype(BF16), rate - rate.astype(BF16).astype(F32)
        r_mid, r_lo = split(r_rest)
        cumulative = dot(r_hi, ones_up, NN) + (dot(r_mid, ones_up, NN) + dot(r_lo, ones_up, NN))
        for at, value in enumerate((delta, cumulative, jax.nn.sigmoid(raw), rate)):
            top = pl.multiple_of(which * halves_of + at * HEADS, HEADS)
            token_rows[pl.ds(top, HEADS), :] = value
        token_cols[...] = token_rows[...].T

    def group(turn, _):
        j = turn + (turn // (HALF - 1)) * donor
        helping = j // HALF
        g = core * HALF + j - helping
        ours = helping == 0
        slot_p = j + helping
        lane0 = helping * halves_of
        cols = group_columns(g)
        blocks = [(0, cols[0])]
        for base, col in ((WIDE, cols[1]), (WIDE + STATE, cols[2])):
            for part in range(STATE // 128):
                blocks.append((base + part * 128, pl.multiple_of(col + part * 128, 128)))

        def conv_rows(start, count, fresh):
            for off, col in blocks:
                here = slice(off, off + 128)
                if fresh:
                    upad[pl.ds(pl.multiple_of(start + 8, 8), count), here] = uin[
                        j, pl.ds(start, count), here
                    ].astype(F32)
                window = upad[pl.ds(start, count + 8), here]
                z = b_ref[helping, :, pl.ds(col, 128)]
                z = z + w_ref[helping, 3:4, pl.ds(col, 128)] * window[8:]
                for k in range(CONV - 1):
                    tap = w_ref[helping, pl.ds(k, 1), pl.ds(col, 128)]
                    z = z + tap * pltpu.roll(window, 3 - k, 0)[8:]
                s = jax.nn.sigmoid(z)
                mix[pl.ds(start, count), here] = z * s
                dsl[pl.ds(start, count), here] = s * (1.0 + z * (1.0 - s))

        @pl.when(ours)
        def _():
            pltpu.make_async_copy(uin.at[j, mine], uin.at[j, mine], own_sem.at[j]).wait()

        @pl.when(helping == 1)
        def _():
            some = pl.ds(0, WIDE + 2 * STATE)
            for at, ref in enumerate((
                uin.at[HALF], steps.at[1], w_ref.at[pl.ds(1, 1), :, some], b_ref.at[1, :, some],
                ng_ref.at[1, :, pl.ds(0, WIDE)], per_head.at[1],
            )):
                landed(ref, ship_sem.at[at])

        conv_rows(pl.multiple_of(core * tok, tok), tok, True)

        @pl.when(j == 0)
        def _():
            landed(steps.at[0, other], step_sem)

        @pl.when(jnp.logical_and(j == 0, sec == 1))
        def _():
            pl.semaphore_wait(plane_sem, 1)
            for k in range(1, ndp):
                greet(core, 0, lax.rem(dp + k, ndp))

        @pl.when(lax.rem(j, HALF) == 0)
        def _():
            token_terms(helping)

        @pl.when(ours)
        def _():
            landed(uin.at[j, theirs], xr_sem.at[j])

        conv_rows(pl.multiple_of(other * tok, tok), tok, True)
        conv_rows(tok, 8, False)

        lane = lax.broadcasted_iota(jnp.int32, (seq, 128), 1)
        lane1 = lax.broadcasted_iota(jnp.int32, (1, 128), 1)
        lane16 = lax.broadcasted_iota(jnp.int32, (1, HEADS), 1)
        row = lax.broadcasted_iota(jnp.int32, (seq, seq), 0)
        column = lax.broadcasted_iota(jnp.int32, (seq, seq), 1)
        first = lane < HEAD_DIM

        def pick(at):
            return jnp.sum(
                jnp.where(lane == lane0 + at, token_cols[...], 0.0), axis=1, keepdims=True
            )

        def pick1(ref, h):
            return jnp.sum(jnp.where(lane16 == h, ref[helping], 0.0), axis=1, keepdims=True)

        x = mix[:, 0:WIDE]
        bmap = split(mix[:, WIDE : WIDE + STATE])
        cmap = split(mix[:, WIDE + STATE : MIX])
        h0 = g * REPS
        dt2 = jnp.where(first, pick(h0), pick(h0 + 1))
        skip2 = jnp.where(first[0:1], pick1(sk_ref, h0), pick1(sk_ref, h0 + 1))
        xs = x * dt2
        xs_p = split(xs)
        scores = dot3(cmap, bmap, NT)
        decay, mixed, ys = [], [], []
        for r in range(REPS):
            seg = pick(HEADS + h0 + r) - token_rows[pl.ds(lane0 + HEADS + h0 + r, 1), :]
            w = jnp.exp(jnp.where(row >= column, seg, -jnp.inf))
            a = scores * w
            a_p = split(a)
            decay.append(w)
            mixed.append((a, a_p))
            ys.append(dot3(a_p, xs_p, NN))
        y = jnp.where(first, ys[0], ys[1]) + skip2 * x
        gate = uin[j, :, MIX : MIX + WIDE].astype(F32)
        cot = uin[j, :, MIX + WIDE : MIX + 2 * WIDE].astype(F32)
        gain = ng_ref[helping, :, pl.ds(cols[0], WIDE)]
        s = jax.nn.sigmoid(gate)
        act = gate * s
        gated = y * act
        scale = lax.rsqrt(jnp.mean(gated * gated, axis=1, keepdims=True) + 1e-05)
        normed = gated * scale
        stage_o[j, :, 0:WIDE] = (normed * gain).astype(BF16)
        dn = cot * gain
        dgated = scale * (dn - normed * jnp.mean(dn * normed, axis=1, keepdims=True))
        dy = dgated * act
        stage_o[j, :, WIDE : 2 * WIDE] = (dgated * y * (s * (1.0 + gate * (1.0 - s)))).astype(BF16)

        even = lax.rem(j, 2) == 0
        out_cut = pl.ds(cols[0], WIDE)

        def send_half(base, t, dst, sem, s):
            remote(
                stage_o.at[j, pl.ds(t * tok, tok), pl.ds(base, WIDE)], dst, sem, t, s, dp
            ).start()

        direct = jnp.logical_and(
            ours, jnp.logical_and(sec < nsec - 1, jnp.logical_not(jnp.logical_and(sec == 1, even)))
        )

        @pl.when(direct)
        def _():
            for t in range(2):
                send_half(0, t, nxt.at[0, 0, :, out_cut], land_sem.at[0], sec + 1)

        @pl.when(jnp.logical_and(ours, jnp.logical_and(sec == 1, even)))
        def _():
            slot = core * (HALF // 2) + j // 2
            for t in range(2):
                send_half(0, t, relay.at[slot], relay_sem, 3)

        @pl.when(jnp.logical_and(ours, jnp.logical_or(sec == 1, sec == 3)))
        def _():
            for t in range(2):
                send_half(
                    WIDE, t, ggate.at[0, 0, :, out_cut], land_sem.at[1], sec - 1
                )

        @pl.when(jnp.logical_and(ours, sec == 2))
        def _():
            slot = core * HALF + j
            for t in range(2):
                send_half(WIDE, t, relay.at[slot], relay_sem, 0)

        @pl.when(helping == 1)
        def _():
            ggate[0, 0, :, out_cut] = stage_o[j, tok : 2 * tok, WIDE : 2 * WIDE]
            send_half(WIDE, 0, ggate.at[0, 0, :, out_cut], land_sem.at[1], sec)

        @pl.when(jnp.logical_and(helping == 1, sec < nsec - 2))
        def _():
            for t in range(2):
                send_half(0, t, nxt.at[0, 0, :, out_cut], land_sem.at[0], sec + 2)

        partial[dp, slot_p, 6:8, :] = jnp.zeros((2, MIX), F32)
        partial[dp, slot_p, 5:6, WIDE:MIX] = jnp.zeros((1, MIX - WIDE), F32)
        partial[dp, slot_p, 5:6, 0:WIDE] = jnp.sum(cot * normed, axis=0, keepdims=True)
        dyx = jnp.sum(dy * x, axis=0, keepdims=True)
        dscore = jnp.zeros((seq, seq), F32)
        dy_p = split(dy)
        das = []
        for r in range(REPS):
            own = first if r == 0 else jnp.logical_not(first)
            da = dot3(split(jnp.where(own, dy, 0.0)), xs_p, NT)
            das.append(da)
            dscore = dscore + da * decay[r]
        ds_p = split(dscore)

        def conv_back(off, width, start):
            for part in range(width // 128):
                here = slice(off + part * 128, off + part * 128 + 128)
                col = pl.multiple_of(start + part * 128, 128)
                dz = zpad[0:seq, here]
                du = jnp.zeros((seq, 128), F32)
                for k in range(CONV):
                    du = du + (
                        w_ref[helping, pl.ds(k, 1), pl.ds(col, 128)]
                        * zpad[3 - k : 3 - k + seq, here]
                    )
                    partial[dp, slot_p, pl.ds(k, 1), here] = jnp.sum(
                        dz * upad[5 + k : 5 + k + seq, here], axis=0, keepdims=True
                    )
                partial[dp, slot_p, pl.ds(4, 1), here] = jnp.sum(dz, axis=0, keepdims=True)
                stage_c[j, :, here] = du.astype(BF16)

            @pl.when(helping == 1)
            def _():
                gconv[0, 0, :, pl.ds(start, width)] = stage_c[j, tok : 2 * tok, off : off + width]
                remote(
                    stage_c.at[j, pl.ds(0, tok), pl.ds(off, width)],
                    gconv.at[0, 0, :, pl.ds(start, width)],
                    land_sem.at[2], 0, sec, dp,
                ).start()

            @pl.when(jnp.logical_and(ours, sec > 0))
            def _():
                for t in range(2):
                    remote(
                        stage_c.at[j, pl.ds(t * tok, tok), pl.ds(off, width)],
                        gconv.at[0, 0, :, pl.ds(start, width)],
                        land_sem.at[2], t, sec - 1, dp,
                    ).start()

        zpad[0:seq, WIDE + STATE : MIX] = dot3(ds_p, bmap, NN) * dsl[:, WIDE + STATE : MIX]
        conv_back(WIDE + STATE, STATE, cols[2])
        zpad[0:seq, WIDE : WIDE + STATE] = dot3(ds_p, cmap, TN) * dsl[:, WIDE : WIDE + STATE]
        conv_back(WIDE, STATE, cols[1])
        dxs = jnp.where(first, dot3(mixed[0][1], dy_p, TN), dot3(mixed[1][1], dy_p, TN))
        zpad[0:seq, 0:WIDE] = (skip2 * dy + dxs * dt2) * dsl[:, 0:WIDE]
        conv_back(0, WIDE, cols[0])
        upper = jnp.where(row <= column, 1.0, 0.0).astype(BF16)
        dxx = dxs * x
        for r in range(REPS):
            own = first if r == 0 else jnp.logical_not(first)
            p = split(das[r] * mixed[r][0])
            later = dot(upper, p[0], NN) + dot(upper, p[1], NN)
            dr = jnp.sum(jnp.where(row > column, later, 0.0), axis=1, keepdims=True)
            drate[...] += jnp.where(lane == lane0 + h0 + r, dr, 0.0)
            total = jnp.sum(jnp.where(own[0:1], dyx, 0.0), axis=1, keepdims=True)
            small[2:3, :] += jnp.where(lane1 == lane0 + h0 + r, total, 0.0)
            dd = jnp.sum(jnp.where(own, dxx, 0.0), axis=1, keepdims=True)
            ddt[...] += jnp.where(lane == lane0 + h0 + r, dd, 0.0)

        @pl.when(jnp.logical_and(j == 0, sec == 0))
        def _():
            pl.semaphore_wait(plane_sem, 1)
            pl.semaphore_wait(barrier, ndp - 1)
            for s in range(1, 4):
                pl.semaphore_signal(
                    world_sem, inc=1, device_id=place(core, s, dp), device_id_type=MESH
                )

        @pl.when(jnp.logical_and(j == 0, sec > 0))
        def _():
            pl.semaphore_wait(world_sem, 1)

        @pl.when(ours)
        def _():
            spread(j)

        @pl.when(helping == 1)
        def _():
            remote(
                partial.at[dp, HALF + 1], partial.at[dp, HALF - 1],
                hand_sem.at[0], core, sec + 1, dp,
            ).start()

        return 0

    def spread(slot):
        for k in range(1, ndp):
            to = lax.rem(dp + k, ndp)
            remote(
                partial.at[dp, slot], partial.at[dp, slot], sum_sem, core, sec, to
            ).start()

    lax.fori_loop(0, own_groups + helper, group, 0)

    def pass_on(slots, groups, out, sem, s):
        landed(relay.at[pl.ds(0, slots)], relay_sem)
        for slot, g in zip(range(slots), groups):
            remote(
                relay.at[slot], out.at[0, 0, :, pl.ds(g * WIDE, WIDE)], sem, core, s, dp
            ).start()

    @pl.when(sec == 0)
    def _():
        pass_on(GROUPS - 1, range(GROUPS - 1), ggate, land_sem.at[1], 1)

    @pl.when(sec == 3)
    def _():
        pass_on(GROUPS // 2, range(0, GROUPS, 2), nxt, land_sem.at[0], 2)

    @pl.when(sec == 0)
    def _():
        nxt[...] = jnp.zeros_like(nxt)

    @pl.when(sec == nsec - 1)
    def _():
        gconv[...] = jnp.zeros_like(gconv)
        ggate[...] = jnp.zeros_like(ggate)
        gstep[...] = jnp.zeros_like(gstep)

    def step_terms(which, into):
        lane0 = which * halves_of
        heads = slice(lane0, lane0 + HEADS)
        dr16 = drate[:, heads]
        gate = token_cols[:, lane0 + 2 * HEADS : lane0 + 3 * HEADS]
        rate = token_cols[:, lane0 + 3 * HEADS : lane0 + 4 * HEADS]
        dstep = (ddt[:, heads] - dr16 * jnp.exp(dl_ref[which])) * gate
        into[0:1, 0:HEADS] = jnp.sum(dstep, axis=0, keepdims=True)
        into[1:2, 0:HEADS] = jnp.sum(dr16 * rate, axis=0, keepdims=True)
        drate[:, heads] = dstep

    step_terms(0, small)

    @pl.when(helper == 1)
    def _():
        step_terms(1, small_out)
        small_out[2:3, 0:HEADS] = small[2:3, halves_of : halves_of + HEADS]
        remote(
            small_out, small_in, hand_sem.at[1], core, sec + 1, dp
        ).start()

    turned = drate[...].T
    for t in range(2):
        stage_s[t] = turned[0:HEADS, t * tok : (t + 1) * tok].astype(BF16)

    @pl.when(sec > 0)
    def _():
        for t in range(2):
            remote(
                stage_s.at[t], step_parts.at[core],
                dstep_sem.at[0], t, sec - 1, dp,
            ).start()

    @pl.when(helper == 1)
    def _():
        stage_s[2] = turned[halves_of : halves_of + HEADS, 0:tok].astype(BF16)
        step_parts[2] = turned[halves_of : halves_of + HEADS, tok : 2 * tok].astype(BF16)
        remote(
            stage_s.at[2], step_parts.at[2], dstep_sem.at[1], other, sec, dp
        ).start()

    @pl.when(donor == 1)
    def _():
        landed(partial.at[dp, HALF - 1], hand_sem.at[0])
        landed(small_in, hand_sem.at[1])
        spread(HALF - 1)
        small[...] += small_in[...]

    partial[dp, HALF] = jnp.zeros((8, MIX), F32)
    partial[dp, HALF, :, 0:128] = small[...]
    spread(HALF)
    landed(partial.at[pl.ds(0, ndp - 1), pl.ds(0, HALF + 1)], sum_sem)
    total = partial[0, 0 : HALF + 1]
    for k in range(1, ndp):
        total = total + partial[k, 0 : HALF + 1]
    final[core] = total
    remote(final.at[core], final.at[core], fin_sem, other, sec, dp).start()
    landed(final.at[other], fin_sem)
    for g in range(GROUPS):
        c, j = g // HALF, g % HALF
        gng[0:1, g * WIDE : (g + 1) * WIDE] = final[c, j, 5:6, 0:WIDE]
        for off, width, col in (
            (0, WIDE, g * WIDE),
            (WIDE, STATE, INNER + g * STATE),
            (WIDE + STATE, STATE, INNER + (GROUPS + g) * STATE),
        ):
            gtap[0, :, col : col + width] = final[c, j, 0:CONV, off : off + width]
            gcb[0:1, col : col + width] = final[c, j, CONV : CONV + 1, off : off + width]
    for at, ref in enumerate((gsb, gdl, gsk)):
        ref[...] = final[0, HALF, at : at + 1, 0:HEADS] + final[1, HALF, at : at + 1, 0:HEADS]

    @pl.when(sec < nsec - 1)
    def _():
        landed(step_parts.at[pl.ds(0, 2)], dstep_sem.at[0])

        @pl.when(core == 0)
        def _():
            landed(step_parts.at[2], dstep_sem.at[1])

        both = step_parts[0].astype(F32) + step_parts[1].astype(F32)
        gstep[0, 0] = (both + step_parts[2].astype(F32)).astype(BF16)

    first = pl.ds(0, HALF - 1)
    half = pl.ds(0, WIDE)
    sent(steps.at[0, 0])
    sent(uin.at[first, pl.ds(0, tok)])
    sent(partial.at[pl.ds(0, ndp - 1), pl.ds(0, HALF + 1)])
    sent(final.at[0])

    @pl.when(other * gives == 0)
    def _():
        sent(uin.at[0, pl.ds(0, tok)])

    @pl.when(sec == 0)
    def _():
        sent(relay.at[pl.ds(0, GROUPS - 1)])

    @pl.when(sec == nsec - 1)
    def _():
        sent(relay.at[pl.ds(0, GROUPS // 2)])

    @pl.when(sec > 0)
    def _():
        sent(uin.at[HALF, pl.ds(0, tok)])
        sent(steps.at[1, 0])
        sent(stage_c.at[first])
        sent(stage_o.at[first, :, half])
        sent(stage_s.at[pl.ds(0, 2)])

    @pl.when(jnp.logical_and(sec > 0, core == 0))
    def _():
        some = pl.ds(0, WIDE + 2 * STATE)
        for ref in (
            w_ref.at[pl.ds(1, 1), :, some], b_ref.at[1, :, some], ng_ref.at[1, :, half],
            per_head.at[1], stage_c.at[HALF - 1], stage_o.at[HALF - 1, :, half],
        ):
            sent(ref)

    @pl.when(sec < nsec - 1)
    def _():
        sent(stage_o.at[first, :, half])

    @pl.when(jnp.logical_and(sec < nsec - 1, donor == 0))
    def _():
        sent(stage_o.at[HALF - 1, :, half])

    @pl.when(helper == 1)
    def _():
        sent(stage_c.at[HALF, pl.ds(0, tok)])
        sent(stage_o.at[HALF, pl.ds(0, tok), half])
        sent(stage_s.at[2])
        sent(partial.at[dp, HALF + 1])
        sent(small_out)

    @pl.when(jnp.logical_and(helper == 1, sec < nsec - 2))
    def _():
        sent(stage_o.at[HALF, :, half])

    @pl.when(sec > 0)
    def _():
        landed(nxt.at[0, 0], land_sem.at[0])

    @pl.when(helper == 1)
    def _():
        landed(ggate.at[0, 0, :, pl.ds(0, INNER - WIDE)], land_sem.at[1])
        landed(gconv.at[0, 0, :, pl.ds(0, (GROUPS - 1) * MIX)], land_sem.at[2])

    @pl.when(jnp.logical_and(sec < nsec - 1, core == 0))
    def _():
        landed(ggate.at[0, 0], land_sem.at[1])
        landed(gconv.at[0, 0], land_sem.at[2])


def finish_kernel(*refs):
    count = len(refs) // 2
    sem = refs[-1]
    copies = [pltpu.make_async_copy(refs[i], refs[count + i], sem.at[i]) for i in range(count)]
    for copy in copies:
        copy.start()
    for copy in copies:
        copy.wait()


def paired(
    conv_input, gate_input, step_input, cotangent, conv_weight,
    conv_bias, step_bias, decay_log, skip_gain, norm_gain,
):
    tok = conv_input.shape[2]
    seq = 2 * tok
    ndp = lax.axis_size("dp")
    hbm = pl.BlockSpec(memory_space=pl.ANY)
    vmem = pl.BlockSpec(memory_space=pltpu.VMEM)
    scratch = [
        pltpu.VMEM((2,) + conv_weight.shape[1:], F32),
        pltpu.VMEM((2,) + conv_bias.shape, F32),
        pltpu.VMEM((2, 3) + step_bias.shape, F32),
        pltpu.VMEM((2,) + norm_gain.shape, F32),
        pltpu.VMEM((HALF + 1, seq, MIX + 2 * WIDE), BF16),
        pltpu.VMEM((2, 2, HEADS, tok), BF16),
        pltpu.VMEM((128, seq), F32),
        pltpu.VMEM((seq, 128), F32),
        pltpu.VMEM((seq + 8, MIX), F32),
        pltpu.VMEM((seq + 8, MIX), F32),
        pltpu.VMEM((seq, MIX), F32),
        pltpu.VMEM((seq, MIX), F32),
        pltpu.VMEM((seq, 128), F32),
        pltpu.VMEM((seq, 128), F32),
        pltpu.VMEM((8, 128), F32),
        pltpu.VMEM((HALF + 1, seq, MIX), BF16),
        pltpu.VMEM((HALF + 1, seq, 2 * WIDE), BF16),
        pltpu.VMEM((3, HEADS, tok), BF16),
        pltpu.VMEM((3, HEADS, tok), BF16),
        pltpu.VMEM((ndp, HALF + 2, 8, MIX), F32),
        pltpu.VMEM((2, HALF + 1, 8, MIX), F32),
        pltpu.VMEM((GROUPS, tok, WIDE), BF16),
        pltpu.VMEM((8, 128), F32),
        pltpu.VMEM((8, 128), F32),
        pltpu.SemaphoreType.DMA((HALF,)),
        pltpu.SemaphoreType.DMA((HALF,)),
    ]
    one = pltpu.SemaphoreType.DMA
    scratch += [one, one((3,)), one((5,)), one, one((6,)), one, one((2,)), one, one((2,)), one]
    scratch += [pltpu.SemaphoreType.REGULAR] * 3
    turned = jnp.swapaxes(step_input, 2, 3)
    shapes = [
        (gate_input.shape, BF16),
        (conv_input.shape, BF16),
        (gate_input.shape, BF16),
        (turned.shape, BF16),
        (conv_weight.shape, F32),
        (conv_bias.shape, F32),
        (step_bias.shape, F32),
        (decay_log.shape, F32),
        (skip_gain.shape, F32),
        (norm_gain.shape, F32),
    ]
    inputs = [
        pltpu.with_memory_space_constraint(a, pltpu.HBM)
        for a in (
            conv_input, gate_input, turned, cotangent, conv_weight,
            conv_bias, step_bias, decay_log, skip_gain, norm_gain,
        )
    ]
    sent = pl.pallas_call(
        pair_kernel,
        name="mixer_tick",
        in_specs=[hbm] * 10,
        out_specs=[vmem] * 10,
        out_shape=[pltpu.VMEM(shape, kind) for shape, kind in shapes],
        scratch_shapes=scratch,
        compiler_params=pltpu.CompilerParams(
            collective_id=0, has_side_effects=True, vmem_limit_bytes=24 * 1024 * 1024
        ),
    )(*inputs)
    done = pl.pallas_call(
        finish_kernel,
        name="mixer_finish",
        in_specs=[vmem] * 10,
        out_specs=[hbm] * 10,
        out_shape=[jax.ShapeDtypeStruct(shape, kind) for shape, kind in shapes],
        scratch_shapes=[pltpu.SemaphoreType.DMA((10,))],
        compiler_params=pltpu.CompilerParams(vmem_limit_bytes=1024 * 1024),
    )(*sent)
    return tuple(done[:3]) + (jnp.swapaxes(done[3], 2, 3),) + tuple(done[4:])


def solution(mesh):
    in_specs = (
        P("section", "dp", "ctx", None),
        P("section", "dp", "ctx", None),
        P("section", "dp", "ctx", None),
        P("section", "dp", "ctx", None),
        P("section", None, None),
        P("section", None),
        P("section", None),
        P("section", None),
        P("section", None),
        P("section", None),
    )
    out_specs = (
        P("section", "dp", "ctx", None),
        P("section", "dp", "ctx", None),
        P("section", "dp", "ctx", None),
        P("section", "dp", "ctx", None),
        P("section", None, None),
        P("section", None),
        P("section", None),
        P("section", None),
        P("section", None),
        P("section", None),
    )
    body = paired if (mesh.shape["ctx"], mesh.shape["section"]) == (2, 4) else shards
    return jax.shard_map(body, mesh=mesh, in_specs=in_specs, out_specs=out_specs, check_vma=False)
```

```python
import functools
import jax
import jax.numpy as jnp
from jax import lax
from jax.experimental import pallas as pl
from jax.experimental.pallas import tpu as pltpu
from jax.sharding import PartitionSpec as P

HEADS = 16
HEAD_DIM = 64
STATE = 256
GROUPS = 8
CONV = 4


HIGH_BOUND = lax.Precision.HIGHEST


def shifted(block, axis, distance):
    devices = range(lax.axis_size(axis))
    route = [(i - distance, i) for i in devices if i - distance in devices]
    return lax.ppermute(block, axis, route)


def prefix(part, axis, combine, identity):
    count = lax.axis_size(axis)
    place = lax.axis_index(axis)
    ahead = count - 1 - place
    gathered = jax.tree.map(lambda a: lax.all_gather(a, axis), part)
    state = jax.tree.map(lambda a, e: jnp.zeros_like(a) + jnp.asarray(e, a.dtype), part, identity)

    def one(turn, state):
        source = count - 1 - turn
        return combine(
            state, jax.tree.map(lambda a: lax.dynamic_index_in_dim(a, source, 0, False), gathered)
        )

    return lax.fori_loop(0, ahead, one, state)


def conv_mix(extended, taps, initial_offset):
    rows = extended.shape[0] - (CONV - 1)
    total = initial_offset[None, :]
    for tap in range(CONV):
        total = total + taps[tap][None, :] * extended[tap : tap + rows]
    return jax.nn.silu(total)


def split_mix(mixed, steps, step_shift, damping_exponents):
    rows = mixed.shape[0]
    inner = HEADS * HEAD_DIM
    payload_lines = mixed[:, :inner].reshape(rows, GROUPS, HEADS // GROUPS, HEAD_DIM)
    in_maps = mixed[:, inner : inner + GROUPS * STATE].reshape(rows, GROUPS, STATE)
    out_maps = mixed[:, inner + GROUPS * STATE :].reshape(rows, GROUPS, STATE)
    delta = jax.nn.softplus(steps + step_shift[None, :])
    upto = jnp.tril(jnp.ones((rows, rows), jnp.float32))
    rates = delta * (-jnp.exp(damping_exponents))[None, :]
    cumulative = jnp.dot(upto, rates, precision=HIGH_BOUND)
    return (payload_lines, in_maps, out_maps, delta, cumulative)


def fragment_condition(extended, steps, taps, initial_offset, step_shift, damping_exponents):
    payload_lines, in_maps, out_maps, delta, cumulative = split_mix(
        conv_mix(extended, taps, initial_offset), steps, step_shift, damping_exponents
    )
    rows = payload_lines.shape[0]
    total = cumulative[-1]
    weight = (jnp.exp(total[None, :] - cumulative) * delta).reshape(rows, GROUPS, HEADS // GROUPS)
    state = jnp.einsum(
        "tgrp,tgn->grpn", payload_lines * weight[..., None], in_maps, precision=HIGH_BOUND
    )
    return (state.reshape(HEADS, HEAD_DIM, STATE), total)


def shard_layer(
    extended,
    gates,
    steps,
    taps,
    initial_offset,
    step_shift,
    damping_exponents,
    skip_values,
    gain_values,
    carried,
):
    payload_lines, in_maps, out_maps, delta, cumulative = split_mix(
        conv_mix(extended, taps, initial_offset), steps, step_shift, damping_exponents
    )
    rows = payload_lines.shape[0]
    reps = HEADS // GROUPS
    lower = (jnp.arange(rows)[:, None] >= jnp.arange(rows)[None, :])[None]
    seg = cumulative.T[:, :, None] - cumulative.T[:, None, :]
    weight = jnp.exp(jnp.where(lower, seg, -jnp.inf)).reshape(GROUPS, reps, rows, rows)
    intersection_maps = jnp.einsum("tgn,sgn->gts", out_maps, in_maps, precision=HIGH_BOUND)
    score_matrix = weight * intersection_maps[:, None]
    scaled_values = payload_lines * delta.reshape(rows, GROUPS, reps)[..., None]
    final_output = jnp.einsum("jzlh,hjzc->ljzc", score_matrix, scaled_values, precision=HIGH_BOUND)
    incoming = jnp.einsum(
        "tgn,grpn->tgrp",
        out_maps,
        carried.reshape(GROUPS, reps, HEAD_DIM, STATE),
        precision=HIGH_BOUND,
    )
    final_output = (
        final_output + incoming * jnp.exp(cumulative).reshape(rows, GROUPS, reps)[..., None]
    )
    final_output = (
        final_output + skip_values.reshape(GROUPS, reps)[None, :, :, None] * payload_lines
    )
    gated = final_output.reshape(rows, GROUPS, -1) * jax.nn.silu(gates).reshape(rows, GROUPS, -1)
    normed = gated * lax.rsqrt(jnp.mean(gated * gated, axis=-1, keepdims=True) + 1e-05)
    return normed.reshape(rows, -1) * gain_values[None, :]


def combine(earlier, later):
    return (earlier[0] * later[0], later[0][:, None] * earlier[1] + later[1])


def shards(
    conv_input,
    gate_input,
    step_input,
    cotangent,
    conv_weight,
    conv_bias,
    step_bias,
    decay_log,
    skip_gain,
    norm_gain,
):
    local_rows = conv_input[0, 0]
    count = local_rows.shape[0]
    taps, initial_offset = (conv_weight[0], conv_bias[0])
    step_shift, damping_exponents = (step_bias[0], decay_log[0])
    skip_values, gain_values = (skip_gain[0], norm_gain[0])
    previous = shifted(local_rows[count - (CONV - 1) :], "ctx", 1)
    extended = jnp.concatenate([previous, local_rows], 0).astype(jnp.float32)
    gates = gate_input[0, 0].astype(jnp.float32)
    steps = step_input[0, 0].astype(jnp.float32)
    (state, total), state_pull = jax.vjp(
        fragment_condition, extended, steps, taps, initial_offset, step_shift, damping_exponents
    )
    decay = jnp.exp(total)
    flat_state = state.reshape(HEADS, HEAD_DIM * STATE)
    unity = (jnp.ones((HEADS,), jnp.float32), jnp.zeros((HEADS, HEAD_DIM * STATE), jnp.float32))

    def advance(index, current):
        return shifted(decay[:, None] * current + flat_state, "ctx", 1)

    incoming = lax.fori_loop(
        0, lax.axis_size("ctx") - 1, advance, jnp.zeros((HEADS, HEAD_DIM * STATE), jnp.float32)
    )
    carried = incoming.reshape(HEADS, HEAD_DIM, STATE)
    final_output, layer_pull = jax.vjp(
        shard_layer,
        extended,
        gates,
        steps,
        taps,
        initial_offset,
        step_shift,
        damping_exponents,
        skip_values,
        gain_values,
        carried,
    )
    forward = shifted(final_output.astype(jnp.bfloat16)[None, None], "section", 1)
    grads = layer_pull(cotangent[0, 0].astype(jnp.float32))
    carry_grad = grads[9].reshape(HEADS, HEAD_DIM * STATE)
    outgoing = prefix((decay, carry_grad), "ctx", combine, unity)[1]
    outgoing_grad = outgoing.reshape(HEADS, HEAD_DIM, STATE)
    total_grad = jnp.sum(outgoing_grad * carried, axis=(1, 2)) * decay
    extra = state_pull((outgoing_grad, total_grad))
    ext_grad = grads[0] + extra[0]
    step_grad = grads[2] + extra[1]
    param_terms = (
        grads[3] + extra[2],
        grads[4] + extra[3],
        grads[5] + extra[4],
        grads[6] + extra[5],
        grads[7],
        grads[8],
    )
    returned = shifted(ext_grad[: CONV - 1], "ctx", -1)
    own_grad = ext_grad[CONV - 1 :]
    row_grad = jnp.concatenate(
        [own_grad[: count - (CONV - 1)], own_grad[count - (CONV - 1) :] + returned], 0
    )
    backward = shifted(
        (
            row_grad.astype(jnp.bfloat16)[None, None],
            grads[1].astype(jnp.bfloat16)[None, None],
            step_grad.astype(jnp.bfloat16)[None, None],
        ),
        "section",
        -1,
    )
    summed = lax.psum(
        (
            param_terms[0],
            param_terms[1],
            param_terms[2],
            param_terms[3],
            param_terms[4],
            param_terms[5],
        ),
        ("ctx", "dp"),
    )
    return (
        forward,
        backward[0],
        backward[1],
        backward[2],
        summed[0][None],
        summed[1][None],
        summed[2][None],
        summed[3][None],
        summed[4][None],
        summed[5][None],
    )


MESH = pl.DeviceIdType.MESH
F32 = jnp.float32
BF16 = jnp.bfloat16
INNER = HEADS * HEAD_DIM
REPS = HEADS // GROUPS
WIDE = REPS * HEAD_DIM
MIX = WIDE + 2 * STATE
HALF = GROUPS // 2
NN = ((1,), (0,))
NT = ((1,), (1,))
TN = ((0,), (0,))


def split(a):
    high = a.astype(BF16)
    return high, (a - high.astype(F32)).astype(BF16)


def dot(a, b, dims):
    return lax.dot_general(a, b, (dims, ((), ())), preferred_element_type=F32)


def dot3(a, b, dims):
    return dot(a[0], b[0], dims) + (dot(a[0], b[1], dims) + dot(a[1], b[0], dims))


def group_columns(g):
    return (
        pl.multiple_of(g * WIDE, 128),
        pl.multiple_of(INNER + g * STATE, 128),
        pl.multiple_of(INNER + (GROUPS + g) * STATE, 128),
    )


def pair_kernel(
    conv_in, gate_in, step_in, cot_in, w_in, b_in, sb_in, dl_in, sk_in, ng_in,
    rows_out, table_out, heads_out,
    w_ref, b_ref, per_head, ng_ref,
    uin, steps, token_rows, token_cols, upad, zpad, mix, dsl, ddt, drate, small,
    stage_c, stage_o, stage_s, step_parts, partial, final, relay, small_out, small_in,
    own_sem, xr_sem, sent_sem, land_sem, load_sem, step_sem, ship_sem, relay_sem, dstep_sem,
    sum_sem, hand_sem, fin_sem, pair_sem, mate_sem, plane_sem, world_sem,
):
    core = lax.axis_index("ctx")
    sec = lax.axis_index("section")
    dp = lax.axis_index("dp")
    nsec = lax.axis_size("section")
    ndp = lax.axis_size("dp")
    tok = conv_in.shape[2]
    seq = 2 * tok
    other = 1 - core
    gives = (sec + nsec - 1) // nsec
    takes = 1 - sec // (nsec - 1)
    donor = core * gives
    helper = core * takes
    own_groups = HALF - donor
    last = GROUPS - 1
    halves_of = 4 * HEADS

    def place(c, s, d):
        return {"ctx": c, "section": s, "dp": d}

    def remote(src, dst, recv, c, s, d):
        return pltpu.make_async_remote_copy(
            src_ref=src, dst_ref=dst, send_sem=sent_sem, recv_sem=recv,
            device_id=place(c, s, d), device_id_type=MESH,
        )

    after = lax.rem(sec + 1, nsec)
    before = lax.rem(sec + nsec - 1, nsec)
    sb_ref, dl_ref, sk_ref = (per_head.at[:, at] for at in range(3))
    nxt = rows_out.at[:, pl.ds(0, INNER)]
    gconv = rows_out.at[:, pl.ds(INNER, 5 * INNER)]
    ggate = rows_out.at[:, pl.ds(6 * INNER, INNER)]
    gstep = rows_out.at[pl.ds(0, HEADS), pl.ds(7 * INNER, tok)]
    barrier = pltpu.get_barrier_semaphore()

    def greet(c, s, d):
        pl.semaphore_signal(barrier, inc=1, device_id=place(c, s, d), device_id_type=MESH)

    upper = lax.rem(sec, 2) == 1

    @pl.when(jnp.logical_not(upper))
    def _():
        for c in range(2):
            greet(c, sec + 1, dp)

    def pieces(g):
        xc, bc, cc = group_columns(g)
        return (
            (conv_in.at[0, 0, :, pl.ds(xc, WIDE)], 0, WIDE),
            (conv_in.at[0, 0, :, pl.ds(bc, STATE)], WIDE, STATE),
            (conv_in.at[0, 0, :, pl.ds(cc, STATE)], WIDE + STATE, STATE),
            (gate_in.at[0, 0, :, pl.ds(xc, WIDE)], MIX, WIDE),
            (cot_in.at[0, 0, :, pl.ds(xc, WIDE)], MIX + WIDE, WIDE),
        )

    mine = pl.ds(pl.multiple_of(core * tok, tok), tok)
    theirs = pl.ds(pl.multiple_of(other * tok, tok), tok)
    def tell(sem, s, c=core):
        pl.semaphore_signal(sem, inc=1, device_id=place(c, s, dp), device_id_type=MESH)

    @pl.when(upper)
    def _():
        pl.semaphore_wait(barrier, 2)

    def landed(ref, sem):
        remote(ref, ref, sem, other, sec, dp).wait_recv()

    def sent(ref):
        remote(ref, ref, sent_sem, other, sec, dp).wait_send()

    def hand(src, dst, at):
        return remote(src, dst, ship_sem.at[at], 1, sec - 1, dp)

    def hand_over():
        for src, off, width in pieces(last):
            hand(src, uin.at[HALF, mine, pl.ds(off, width)], 0).start()
        hand(step_in.at[0, 0], steps.at[1, core], 1).start()

    def hand_params():
        xc, bc, cc = group_columns(last)
        for col, width in ((xc, WIDE), (bc, STATE), (cc, STATE)):
            cut = pl.ds(col, width)
            hand(w_in.at[:, :, cut], w_ref.at[pl.ds(1, 1), :, cut], 2).start()
            hand(b_in.at[:, cut], b_ref.at[1, :, cut], 3).start()
        cut = pl.ds(xc, WIDE)
        hand(ng_in.at[:, cut], ng_ref.at[1, :, cut], 4).start()
        hand(sb_in, sb_ref.at[1], 5).start()
        hand(dl_in, dl_ref.at[1], 5).start()
        hand(sk_in, sk_ref.at[1], 5).start()

    @pl.when(upper)
    def _():
        hand_over()
        for c in range(2):
            tell(pair_sem, sec - 1, c)

    @pl.when(sec == 1)
    def _():
        for c in range(2):
            greet(c, 2, dp)

    own_step = pltpu.make_async_copy(step_in.at[0, 0], steps.at[0, core], load_sem.at[0])
    own_step.start()

    def fetch(j, _):
        for src, off, width in pieces(core * HALF + j):
            pltpu.make_async_copy(
                src, uin.at[j, mine, pl.ds(off, width)], own_sem.at[j]
            ).start()
        return 0

    fetch(0, 0)
    params = [
        pltpu.make_async_copy(src, dst, load_sem.at[at])
        for src, dst, at in (
            (sb_in, sb_ref.at[0], 1), (dl_in, dl_ref.at[0], 1), (sk_in, sk_ref.at[0], 1),
            (w_in, w_ref.at[pl.ds(0, 1)], 2), (b_in, b_ref.at[0], 3), (ng_in, ng_ref.at[0], 4),
        )
    ]
    for copy in params:
        copy.start()
    lax.fori_loop(1, own_groups, fetch, 0)
    upad[0:8, :] = jnp.zeros((8, MIX), F32)
    zpad[seq : seq + 8, :] = jnp.zeros((8, MIX), F32)
    for ref in (token_rows, ddt, drate, small, small_out):
        ref[...] = jnp.zeros_like(ref)

    @pl.when(jnp.logical_not(upper))
    def _():
        pl.semaphore_wait(pair_sem, 2)
        tell(mate_sem, sec + 1)

    @pl.when(upper)
    def _():
        pl.semaphore_wait(mate_sem, 1)

    remote(step_in.at[0, 0], steps.at[0, core], step_sem, other, sec, dp).start()

    def exchange(j, _):
        for src, off, width in pieces(other * HALF + j):
            remote(
                src, uin.at[j, mine, pl.ds(off, width)], xr_sem.at[j], other, sec, dp
            ).start()
        return 0

    exchange(0, 0)

    @pl.when(sec == 2)
    def _():
        pl.semaphore_wait(barrier, 2)
        tell(plane_sem, 0)
        tell(plane_sem, 1)
        hand_over()

    @pl.when(jnp.logical_and(sec > 0, core == 0))
    def _():
        hand_params()

    lax.fori_loop(1, HALF - other * gives, exchange, 0)
    own_step.wait()
    pltpu.make_async_copy(per_head.at[0], per_head.at[0], load_sem.at[1]).wait()
    for copy in params[3:]:
        copy.wait()

    def token_terms(which):
        diagonal = lax.broadcasted_iota(jnp.int32, (HEADS, HEADS), 0) == lax.broadcasted_iota(
            jnp.int32, (HEADS, HEADS), 1
        )

        def upright(ref):
            return jnp.sum(jnp.where(diagonal, ref[which], 0.0), axis=1, keepdims=True)

        raw = jnp.concatenate(
            [steps[which, 0].astype(F32), steps[which, 1].astype(F32)], axis=1
        )
        raw = raw + upright(sb_ref)
        delta = jnp.maximum(raw, 0.0) + jnp.log1p(jnp.exp(-jnp.abs(raw)))
        rate = delta * (-jnp.exp(upright(dl_ref)))
        rows2 = lax.broadcasted_iota(jnp.int32, (seq, seq), 0)
        cols2 = lax.broadcasted_iota(jnp.int32, (seq, seq), 1)
        ones_up = jnp.where(rows2 <= cols2, 1.0, 0.0).astype(BF16)
        r_hi, r_rest = rate.astype(BF16), rate - rate.astype(BF16).astype(F32)
        r_mid, r_lo = split(r_rest)
        cumulative = dot(r_hi, ones_up, NN) + (dot(r_mid, ones_up, NN) + dot(r_lo, ones_up, NN))
        for at, value in enumerate((delta, cumulative, jax.nn.sigmoid(raw), rate)):
            top = pl.multiple_of(which * halves_of + at * HEADS, HEADS)
            token_rows[pl.ds(top, HEADS), :] = value
        token_cols[...] = token_rows[...].T

    def group(turn, _):
        j = turn + (turn // (HALF - 1)) * donor
        helping = j // HALF
        g = core * HALF + j - helping
        ours = helping == 0
        slot_p = j + helping
        lane0 = helping * halves_of
        cols = group_columns(g)
        blocks = [(0, cols[0])]
        for base, col in ((WIDE, cols[1]), (WIDE + STATE, cols[2])):
            for part in range(STATE // 128):
                blocks.append((base + part * 128, pl.multiple_of(col + part * 128, 128)))

        def conv_rows(start, count, fresh):
            for off, col in blocks:
                here = slice(off, off + 128)
                if fresh:
                    upad[pl.ds(pl.multiple_of(start + 8, 8), count), here] = uin[
                        j, pl.ds(start, count), here
                    ].astype(F32)
                window = upad[pl.ds(start, count + 8), here]
                z = b_ref[helping, :, pl.ds(col, 128)]
                z = z + w_ref[helping, 3:4, pl.ds(col, 128)] * window[8:]
                for k in range(CONV - 1):
                    tap = w_ref[helping, pl.ds(k, 1), pl.ds(col, 128)]
                    z = z + tap * pltpu.roll(window, 3 - k, 0)[8:]
                s = jax.nn.sigmoid(z)
                mix[pl.ds(start, count), here] = z * s
                dsl[pl.ds(start, count), here] = s * (1.0 + z * (1.0 - s))

        @pl.when(ours)
        def _():
            pltpu.make_async_copy(uin.at[j, mine], uin.at[j, mine], own_sem.at[j]).wait()

        @pl.when(helping == 1)
        def _():
            some = pl.ds(0, WIDE + 2 * STATE)
            for at, ref in enumerate((
                uin.at[HALF], steps.at[1], w_ref.at[pl.ds(1, 1), :, some], b_ref.at[1, :, some],
                ng_ref.at[1, :, pl.ds(0, WIDE)], per_head.at[1],
            )):
                landed(ref, ship_sem.at[at])

        conv_rows(pl.multiple_of(core * tok, tok), tok, True)

        @pl.when(j == 0)
        def _():
            landed(steps.at[0, other], step_sem)

        @pl.when(jnp.logical_and(j == 0, sec == 1))
        def _():
            pl.semaphore_wait(plane_sem, 1)
            for k in range(1, ndp):
                greet(core, 0, lax.rem(dp + k, ndp))

        @pl.when(lax.rem(j, HALF) == 0)
        def _():
            token_terms(helping)

        @pl.when(ours)
        def _():
            landed(uin.at[j, theirs], xr_sem.at[j])

        conv_rows(pl.multiple_of(other * tok, tok), tok, True)
        conv_rows(tok, 8, False)

        lane = lax.broadcasted_iota(jnp.int32, (seq, 128), 1)
        lane1 = lax.broadcasted_iota(jnp.int32, (1, 128), 1)
        lane16 = lax.broadcasted_iota(jnp.int32, (1, HEADS), 1)
        row = lax.broadcasted_iota(jnp.int32, (seq, seq), 0)
        column = lax.broadcasted_iota(jnp.int32, (seq, seq), 1)
        first = lane < HEAD_DIM

        def pick(at):
            return jnp.sum(
                jnp.where(lane == lane0 + at, token_cols[...], 0.0), axis=1, keepdims=True
            )

        def pick1(ref, h):
            return jnp.sum(jnp.where(lane16 == h, ref[helping], 0.0), axis=1, keepdims=True)

        x = mix[:, 0:WIDE]
        bmap = split(mix[:, WIDE : WIDE + STATE])
        cmap = split(mix[:, WIDE + STATE : MIX])
        h0 = g * REPS
        dt2 = jnp.where(first, pick(h0), pick(h0 + 1))
        skip2 = jnp.where(first[0:1], pick1(sk_ref, h0), pick1(sk_ref, h0 + 1))
        xs = x * dt2
        xs_p = split(xs)
        scores = dot3(cmap, bmap, NT)
        decay, mixed, ys = [], [], []
        for r in range(REPS):
            seg = pick(HEADS + h0 + r) - token_rows[pl.ds(lane0 + HEADS + h0 + r, 1), :]
            w = jnp.exp(jnp.where(row >= column, seg, -jnp.inf))
            a = scores * w
            a_p = split(a)
            decay.append(w)
            mixed.append((a, a_p))
            ys.append(dot3(a_p, xs_p, NN))
        y = jnp.where(first, ys[0], ys[1]) + skip2 * x
        gate = uin[j, :, MIX : MIX + WIDE].astype(F32)
        cot = uin[j, :, MIX + WIDE : MIX + 2 * WIDE].astype(F32)
        gain = ng_ref[helping, :, pl.ds(cols[0], WIDE)]
        s = jax.nn.sigmoid(gate)
        act = gate * s
        gated = y * act
        scale = lax.rsqrt(jnp.mean(gated * gated, axis=1, keepdims=True) + 1e-05)
        normed = gated * scale
        stage_o[j, :, 0:WIDE] = (normed * gain).astype(BF16)
        dn = cot * gain
        dgated = scale * (dn - normed * jnp.mean(dn * normed, axis=1, keepdims=True))
        dy = dgated * act
        stage_o[j, :, WIDE : 2 * WIDE] = (dgated * y * (s * (1.0 + gate * (1.0 - s)))).astype(BF16)

        even = lax.rem(j, 2) == 0
        out_cut = pl.ds(cols[0], WIDE)

        def send_half(base, t, dst, sem, s):
            remote(
                stage_o.at[j, pl.ds(t * tok, tok), pl.ds(base, WIDE)], dst, sem, t, s, dp
            ).start()

        direct = jnp.logical_and(
            ours, jnp.logical_and(sec < nsec - 1, jnp.logical_not(jnp.logical_and(sec == 1, even)))
        )

        @pl.when(direct)
        def _():
            for t in range(2):
                send_half(0, t, nxt.at[:, out_cut], land_sem.at[0], sec + 1)

        @pl.when(jnp.logical_and(ours, jnp.logical_and(sec == 1, even)))
        def _():
            slot = core * (HALF // 2) + j // 2
            for t in range(2):
                send_half(0, t, relay.at[slot], relay_sem, 3)

        @pl.when(jnp.logical_and(ours, jnp.logical_or(sec == 1, sec == 3)))
        def _():
            for t in range(2):
                send_half(
                    WIDE, t, ggate.at[:, out_cut], land_sem.at[1], sec - 1
                )

        @pl.when(jnp.logical_and(ours, sec == 2))
        def _():
            slot = core * HALF + j
            for t in range(2):
                send_half(WIDE, t, relay.at[slot], relay_sem, 0)

        @pl.when(helping == 1)
        def _():
            ggate[:, out_cut] = stage_o[j, tok : 2 * tok, WIDE : 2 * WIDE]
            send_half(WIDE, 0, ggate.at[:, out_cut], land_sem.at[1], sec)

        @pl.when(jnp.logical_and(helping == 1, sec < nsec - 2))
        def _():
            for t in range(2):
                send_half(0, t, nxt.at[:, out_cut], land_sem.at[0], sec + 2)

        partial[dp, slot_p, 6:8, :] = jnp.zeros((2, MIX), F32)
        partial[dp, slot_p, 5:6, WIDE:MIX] = jnp.zeros((1, MIX - WIDE), F32)
        partial[dp, slot_p, 5:6, 0:WIDE] = jnp.sum(cot * normed, axis=0, keepdims=True)
        dyx = jnp.sum(dy * x, axis=0, keepdims=True)
        dscore = jnp.zeros((seq, seq), F32)
        dy_p = split(dy)
        das = []
        for r in range(REPS):
            own = first if r == 0 else jnp.logical_not(first)
            da = dot3(split(jnp.where(own, dy, 0.0)), xs_p, NT)
            das.append(da)
            dscore = dscore + da * decay[r]
        ds_p = split(dscore)

        def conv_back(off, width, start):
            for part in range(width // 128):
                here = slice(off + part * 128, off + part * 128 + 128)
                col = pl.multiple_of(start + part * 128, 128)
                dz = zpad[0:seq, here]
                du = jnp.zeros((seq, 128), F32)
                for k in range(CONV):
                    du = du + (
                        w_ref[helping, pl.ds(k, 1), pl.ds(col, 128)]
                        * zpad[3 - k : 3 - k + seq, here]
                    )
                    partial[dp, slot_p, pl.ds(k, 1), here] = jnp.sum(
                        dz * upad[5 + k : 5 + k + seq, here], axis=0, keepdims=True
                    )
                partial[dp, slot_p, pl.ds(4, 1), here] = jnp.sum(dz, axis=0, keepdims=True)
                stage_c[j, :, here] = du.astype(BF16)

            @pl.when(helping == 1)
            def _():
                gconv[:, pl.ds(start, width)] = stage_c[j, tok : 2 * tok, off : off + width]
                remote(
                    stage_c.at[j, pl.ds(0, tok), pl.ds(off, width)],
                    gconv.at[:, pl.ds(start, width)],
                    land_sem.at[2], 0, sec, dp,
                ).start()

            @pl.when(jnp.logical_and(ours, sec > 0))
            def _():
                for t in range(2):
                    remote(
                        stage_c.at[j, pl.ds(t * tok, tok), pl.ds(off, width)],
                        gconv.at[:, pl.ds(start, width)],
                        land_sem.at[2], t, sec - 1, dp,
                    ).start()

        zpad[0:seq, WIDE + STATE : MIX] = dot3(ds_p, bmap, NN) * dsl[:, WIDE + STATE : MIX]
        conv_back(WIDE + STATE, STATE, cols[2])
        zpad[0:seq, WIDE : WIDE + STATE] = dot3(ds_p, cmap, TN) * dsl[:, WIDE : WIDE + STATE]
        conv_back(WIDE, STATE, cols[1])
        dxs = jnp.where(first, dot3(mixed[0][1], dy_p, TN), dot3(mixed[1][1], dy_p, TN))
        zpad[0:seq, 0:WIDE] = (skip2 * dy + dxs * dt2) * dsl[:, 0:WIDE]
        conv_back(0, WIDE, cols[0])
        upper = jnp.where(row <= column, 1.0, 0.0).astype(BF16)
        dxx = dxs * x
        for r in range(REPS):
            own = first if r == 0 else jnp.logical_not(first)
            p = split(das[r] * mixed[r][0])
            later = dot(upper, p[0], NN) + dot(upper, p[1], NN)
            dr = jnp.sum(jnp.where(row > column, later, 0.0), axis=1, keepdims=True)
            drate[...] += jnp.where(lane == lane0 + h0 + r, dr, 0.0)
            total = jnp.sum(jnp.where(own[0:1], dyx, 0.0), axis=1, keepdims=True)
            small[2:3, :] += jnp.where(lane1 == lane0 + h0 + r, total, 0.0)
            dd = jnp.sum(jnp.where(own, dxx, 0.0), axis=1, keepdims=True)
            ddt[...] += jnp.where(lane == lane0 + h0 + r, dd, 0.0)

        @pl.when(jnp.logical_and(j == 0, sec == 0))
        def _():
            pl.semaphore_wait(plane_sem, 1)
            pl.semaphore_wait(barrier, ndp - 1)
            for s in range(1, 4):
                pl.semaphore_signal(
                    world_sem, inc=1, device_id=place(core, s, dp), device_id_type=MESH
                )

        @pl.when(jnp.logical_and(j == 0, sec > 0))
        def _():
            pl.semaphore_wait(world_sem, 1)

        @pl.when(ours)
        def _():
            spread(j)

        @pl.when(helping == 1)
        def _():
            remote(
                partial.at[dp, HALF + 1], partial.at[dp, HALF - 1],
                hand_sem.at[0], core, sec + 1, dp,
            ).start()

        return 0

    def spread(slot):
        for k in range(1, ndp):
            to = lax.rem(dp + k, ndp)
            remote(
                partial.at[dp, slot], partial.at[dp, slot], sum_sem, core, sec, to
            ).start()

    lax.fori_loop(0, own_groups + helper, group, 0)

    def pass_on(slots, groups, out, sem, s):
        landed(relay.at[pl.ds(0, slots)], relay_sem)
        for slot, g in zip(range(slots), groups):
            remote(
                relay.at[slot], out.at[:, pl.ds(g * WIDE, WIDE)], sem, core, s, dp
            ).start()

    @pl.when(sec == 0)
    def _():
        pass_on(GROUPS - 1, range(GROUPS - 1), ggate, land_sem.at[1], 1)

    @pl.when(sec == 3)
    def _():
        pass_on(GROUPS // 2, range(0, GROUPS, 2), nxt, land_sem.at[0], 2)

    @pl.when(sec == 0)
    def _():
        nxt[...] = jnp.zeros_like(nxt)

    @pl.when(sec == nsec - 1)
    def _():
        gconv[...] = jnp.zeros_like(gconv)
        ggate[...] = jnp.zeros_like(ggate)
        gstep[...] = jnp.zeros_like(gstep)

    def step_terms(which, into):
        lane0 = which * halves_of
        heads = slice(lane0, lane0 + HEADS)
        dr16 = drate[:, heads]
        gate = token_cols[:, lane0 + 2 * HEADS : lane0 + 3 * HEADS]
        rate = token_cols[:, lane0 + 3 * HEADS : lane0 + 4 * HEADS]
        dstep = (ddt[:, heads] - dr16 * jnp.exp(dl_ref[which])) * gate
        into[0:1, 0:HEADS] = jnp.sum(dstep, axis=0, keepdims=True)
        into[1:2, 0:HEADS] = jnp.sum(dr16 * rate, axis=0, keepdims=True)
        drate[:, heads] = dstep

    step_terms(0, small)

    @pl.when(helper == 1)
    def _():
        step_terms(1, small_out)
        small_out[2:3, 0:HEADS] = small[2:3, halves_of : halves_of + HEADS]
        remote(
            small_out, small_in, hand_sem.at[1], core, sec + 1, dp
        ).start()

    turned = drate[...].T
    for t in range(2):
        stage_s[t] = turned[0:HEADS, t * tok : (t + 1) * tok].astype(BF16)

    @pl.when(sec > 0)
    def _():
        for t in range(2):
            remote(
                stage_s.at[t], step_parts.at[core],
                dstep_sem.at[0], t, sec - 1, dp,
            ).start()

    @pl.when(helper == 1)
    def _():
        stage_s[2] = turned[halves_of : halves_of + HEADS, 0:tok].astype(BF16)
        step_parts[2] = turned[halves_of : halves_of + HEADS, tok : 2 * tok].astype(BF16)
        remote(
            stage_s.at[2], step_parts.at[2], dstep_sem.at[1], other, sec, dp
        ).start()

    @pl.when(donor == 1)
    def _():
        landed(partial.at[dp, HALF - 1], hand_sem.at[0])
        landed(small_in, hand_sem.at[1])
        spread(HALF - 1)
        small[...] += small_in[...]

    partial[dp, HALF] = jnp.zeros((8, MIX), F32)
    partial[dp, HALF, :, 0:128] = small[...]
    spread(HALF)
    landed(partial.at[pl.ds(0, ndp - 1), pl.ds(0, HALF + 1)], sum_sem)
    total = partial[0, 0 : HALF + 1]
    for k in range(1, ndp):
        total = total + partial[k, 0 : HALF + 1]
    final[core] = total
    remote(final.at[core], final.at[core], fin_sem, other, sec, dp).start()
    landed(final.at[other], fin_sem)
    for g in range(GROUPS):
        c, j = g // HALF, g % HALF
        table_out[5:6, g * WIDE : (g + 1) * WIDE] = final[c, j, 5:6, 0:WIDE]
        for off, width, col in (
            (0, WIDE, g * WIDE),
            (WIDE, STATE, INNER + g * STATE),
            (WIDE + STATE, STATE, INNER + (GROUPS + g) * STATE),
        ):
            table_out[0:CONV, col : col + width] = final[c, j, 0:CONV, off : off + width]
            table_out[CONV : CONV + 1, col : col + width] = final[c, j, CONV : CONV + 1, off : off + width]
    for at in range(3):
        heads_out[at] = final[0, HALF, at : at + 1, 0:HEADS] + final[1, HALF, at : at + 1, 0:HEADS]

    @pl.when(sec < nsec - 1)
    def _():
        landed(step_parts.at[pl.ds(0, 2)], dstep_sem.at[0])

        @pl.when(core == 0)
        def _():
            landed(step_parts.at[2], dstep_sem.at[1])

        both = step_parts[0].astype(F32) + step_parts[1].astype(F32)
        gstep[...] = (both + step_parts[2].astype(F32)).astype(BF16)

    first = pl.ds(0, HALF - 1)
    half = pl.ds(0, WIDE)
    sent(steps.at[0, 0])
    sent(uin.at[first, pl.ds(0, tok)])
    sent(partial.at[pl.ds(0, ndp - 1), pl.ds(0, HALF + 1)])
    sent(final.at[0])

    @pl.when(other * gives == 0)
    def _():
        sent(uin.at[0, pl.ds(0, tok)])

    @pl.when(sec == 0)
    def _():
        sent(relay.at[pl.ds(0, GROUPS - 1)])

    @pl.when(sec == nsec - 1)
    def _():
        sent(relay.at[pl.ds(0, GROUPS // 2)])

    @pl.when(sec > 0)
    def _():
        sent(uin.at[HALF, pl.ds(0, tok)])
        sent(steps.at[1, 0])
        sent(stage_c.at[first])
        sent(stage_o.at[first, :, half])
        sent(stage_s.at[pl.ds(0, 2)])

    @pl.when(jnp.logical_and(sec > 0, core == 0))
    def _():
        some = pl.ds(0, WIDE + 2 * STATE)
        for ref in (
            w_ref.at[pl.ds(1, 1), :, some], b_ref.at[1, :, some], ng_ref.at[1, :, half],
            per_head.at[1], stage_c.at[HALF - 1], stage_o.at[HALF - 1, :, half],
        ):
            sent(ref)

    @pl.when(sec < nsec - 1)
    def _():
        sent(stage_o.at[first, :, half])

    @pl.when(jnp.logical_and(sec < nsec - 1, donor == 0))
    def _():
        sent(stage_o.at[HALF - 1, :, half])

    @pl.when(helper == 1)
    def _():
        sent(stage_c.at[HALF, pl.ds(0, tok)])
        sent(stage_o.at[HALF, pl.ds(0, tok), half])
        sent(stage_s.at[2])
        sent(partial.at[dp, HALF + 1])
        sent(small_out)

    @pl.when(jnp.logical_and(helper == 1, sec < nsec - 2))
    def _():
        sent(stage_o.at[HALF, :, half])

    @pl.when(sec > 0)
    def _():
        landed(nxt, land_sem.at[0])

    @pl.when(helper == 1)
    def _():
        landed(ggate.at[:, pl.ds(0, INNER - WIDE)], land_sem.at[1])
        landed(gconv.at[:, pl.ds(0, (GROUPS - 1) * MIX)], land_sem.at[2])

    @pl.when(jnp.logical_and(sec < nsec - 1, core == 0))
    def _():
        landed(ggate, land_sem.at[1])
        landed(gconv, land_sem.at[2])


def finish_kernel(
    rows_in, table_in, heads_in, nxt, gconv, ggate, gstep, gtap, gcb, gsb, gdl, gsk, gng, sem
):
    tok = rows_in.shape[0]
    copies = [
        (rows_in.at[:, pl.ds(INNER, 5 * INNER)], gconv.at[0, 0]),
        (rows_in.at[:, pl.ds(0, INNER)], nxt.at[0, 0]),
        (rows_in.at[:, pl.ds(6 * INNER, INNER)], ggate.at[0, 0]),
        (table_in.at[pl.ds(0, CONV)], gtap.at[0]),
        (table_in.at[pl.ds(CONV, 1)], gcb),
        (table_in.at[pl.ds(CONV + 1, 1), pl.ds(0, INNER)], gng),
        (rows_in.at[pl.ds(0, HEADS), pl.ds(7 * INNER, tok)], gstep.at[0, 0]),
        (heads_in.at[0], gsb),
        (heads_in.at[1], gdl),
        (heads_in.at[2], gsk),
    ]
    copies = [pltpu.make_async_copy(a, b, sem.at[at]) for at, (a, b) in enumerate(copies)]
    for copy in copies:
        copy.start()
    for copy in copies:
        copy.wait()


def paired(
    conv_input, gate_input, step_input, cotangent, conv_weight,
    conv_bias, step_bias, decay_log, skip_gain, norm_gain,
):
    tok = conv_input.shape[2]
    seq = 2 * tok
    ndp = lax.axis_size("dp")
    hbm = pl.BlockSpec(memory_space=pl.ANY)
    vmem = pl.BlockSpec(memory_space=pltpu.VMEM)
    scratch = [
        pltpu.VMEM((2,) + conv_weight.shape[1:], F32),
        pltpu.VMEM((2,) + conv_bias.shape, F32),
        pltpu.VMEM((2, 3) + step_bias.shape, F32),
        pltpu.VMEM((2,) + norm_gain.shape, F32),
        pltpu.VMEM((HALF + 1, seq, MIX + 2 * WIDE), BF16),
        pltpu.VMEM((2, 2, HEADS, tok), BF16),
        pltpu.VMEM((128, seq), F32),
        pltpu.VMEM((seq, 128), F32),
        pltpu.VMEM((seq + 8, MIX), F32),
        pltpu.VMEM((seq + 8, MIX), F32),
        pltpu.VMEM((seq, MIX), F32),
        pltpu.VMEM((seq, MIX), F32),
        pltpu.VMEM((seq, 128), F32),
        pltpu.VMEM((seq, 128), F32),
        pltpu.VMEM((8, 128), F32),
        pltpu.VMEM((HALF + 1, seq, MIX), BF16),
        pltpu.VMEM((HALF + 1, seq, 2 * WIDE), BF16),
        pltpu.VMEM((3, HEADS, tok), BF16),
        pltpu.VMEM((3, HEADS, tok), BF16),
        pltpu.VMEM((ndp, HALF + 2, 8, MIX), F32),
        pltpu.VMEM((2, HALF + 1, 8, MIX), F32),
        pltpu.VMEM((GROUPS, tok, WIDE), BF16),
        pltpu.VMEM((8, 128), F32),
        pltpu.VMEM((8, 128), F32),
        pltpu.SemaphoreType.DMA((HALF,)),
        pltpu.SemaphoreType.DMA((HALF,)),
    ]
    one = pltpu.SemaphoreType.DMA
    scratch += [one, one((3,)), one((5,)), one, one((6,)), one, one((2,)), one, one((2,)), one]
    scratch += [pltpu.SemaphoreType.REGULAR] * 4
    turned = jnp.swapaxes(step_input, 2, 3)
    shapes = [
        (gate_input.shape, BF16),
        (conv_input.shape, BF16),
        (gate_input.shape, BF16),
        (turned.shape, BF16),
        (conv_weight.shape, F32),
        (conv_bias.shape, F32),
        (step_bias.shape, F32),
        (decay_log.shape, F32),
        (skip_gain.shape, F32),
        (norm_gain.shape, F32),
    ]
    inputs = [
        pltpu.with_memory_space_constraint(a, pltpu.HBM)
        for a in (
            conv_input, gate_input, turned, cotangent, conv_weight,
            conv_bias, step_bias, decay_log, skip_gain, norm_gain,
        )
    ]
    sent = pl.pallas_call(
        pair_kernel,
        name="mixer_tick",
        in_specs=[hbm] * 10,
        out_specs=[vmem] * 3,
        out_shape=[
            pltpu.VMEM((tok, 7 * INNER + tok), BF16),
            pltpu.VMEM((8, conv_bias.shape[1]), F32),
            pltpu.VMEM((3,) + step_bias.shape, F32),
        ],
        scratch_shapes=scratch,
        compiler_params=pltpu.CompilerParams(
            collective_id=0, has_side_effects=True, vmem_limit_bytes=24 * 1024 * 1024
        ),
    )(*inputs)
    done = pl.pallas_call(
        finish_kernel,
        name="mixer_finish",
        in_specs=[vmem] * 3,
        out_specs=[hbm] * 10,
        out_shape=[jax.ShapeDtypeStruct(shape, kind) for shape, kind in shapes],
        scratch_shapes=[pltpu.SemaphoreType.DMA((10,))],
        compiler_params=pltpu.CompilerParams(vmem_limit_bytes=1024 * 1024),
    )(*sent)
    return tuple(done[:3]) + (jnp.swapaxes(done[3], 2, 3),) + tuple(done[4:])


def solution(mesh):
    in_specs = (
        P("section", "dp", "ctx", None),
        P("section", "dp", "ctx", None),
        P("section", "dp", "ctx", None),
        P("section", "dp", "ctx", None),
        P("section", None, None),
        P("section", None),
        P("section", None),
        P("section", None),
        P("section", None),
        P("section", None),
    )
    out_specs = (
        P("section", "dp", "ctx", None),
        P("section", "dp", "ctx", None),
        P("section", "dp", "ctx", None),
        P("section", "dp", "ctx", None),
        P("section", None, None),
        P("section", None),
        P("section", None),
        P("section", None),
        P("section", None),
        P("section", None),
    )
    body = paired if (mesh.shape["ctx"], mesh.shape["section"]) == (2, 4) else shards
    return jax.shard_map(body, mesh=mesh, in_specs=in_specs, out_specs=out_specs, check_vma=False)
```

```python
import functools
import jax
import jax.numpy as jnp
from jax import lax
from jax.experimental import pallas as pl
from jax.experimental.pallas import tpu as pltpu
from jax.sharding import PartitionSpec as P

HEADS = 16
HEAD_DIM = 64
STATE = 256
GROUPS = 8
CONV = 4


HIGH_BOUND = lax.Precision.HIGHEST


def shifted(block, axis, distance):
    devices = range(lax.axis_size(axis))
    route = [(i - distance, i) for i in devices if i - distance in devices]
    return lax.ppermute(block, axis, route)


def prefix(part, axis, combine, identity):
    count = lax.axis_size(axis)
    place = lax.axis_index(axis)
    ahead = count - 1 - place
    gathered = jax.tree.map(lambda a: lax.all_gather(a, axis), part)
    state = jax.tree.map(lambda a, e: jnp.zeros_like(a) + jnp.asarray(e, a.dtype), part, identity)

    def one(turn, state):
        source = count - 1 - turn
        return combine(
            state, jax.tree.map(lambda a: lax.dynamic_index_in_dim(a, source, 0, False), gathered)
        )

    return lax.fori_loop(0, ahead, one, state)


def conv_mix(extended, taps, initial_offset):
    rows = extended.shape[0] - (CONV - 1)
    total = initial_offset[None, :]
    for tap in range(CONV):
        total = total + taps[tap][None, :] * extended[tap : tap + rows]
    return jax.nn.silu(total)


def split_mix(mixed, steps, step_shift, damping_exponents):
    rows = mixed.shape[0]
    inner = HEADS * HEAD_DIM
    payload_lines = mixed[:, :inner].reshape(rows, GROUPS, HEADS // GROUPS, HEAD_DIM)
    in_maps = mixed[:, inner : inner + GROUPS * STATE].reshape(rows, GROUPS, STATE)
    out_maps = mixed[:, inner + GROUPS * STATE :].reshape(rows, GROUPS, STATE)
    delta = jax.nn.softplus(steps + step_shift[None, :])
    upto = jnp.tril(jnp.ones((rows, rows), jnp.float32))
    rates = delta * (-jnp.exp(damping_exponents))[None, :]
    cumulative = jnp.dot(upto, rates, precision=HIGH_BOUND)
    return (payload_lines, in_maps, out_maps, delta, cumulative)


def fragment_condition(extended, steps, taps, initial_offset, step_shift, damping_exponents):
    payload_lines, in_maps, out_maps, delta, cumulative = split_mix(
        conv_mix(extended, taps, initial_offset), steps, step_shift, damping_exponents
    )
    rows = payload_lines.shape[0]
    total = cumulative[-1]
    weight = (jnp.exp(total[None, :] - cumulative) * delta).reshape(rows, GROUPS, HEADS // GROUPS)
    state = jnp.einsum(
        "tgrp,tgn->grpn", payload_lines * weight[..., None], in_maps, precision=HIGH_BOUND
    )
    return (state.reshape(HEADS, HEAD_DIM, STATE), total)


def shard_layer(
    extended,
    gates,
    steps,
    taps,
    initial_offset,
    step_shift,
    damping_exponents,
    skip_values,
    gain_values,
    carried,
):
    payload_lines, in_maps, out_maps, delta, cumulative = split_mix(
        conv_mix(extended, taps, initial_offset), steps, step_shift, damping_exponents
    )
    rows = payload_lines.shape[0]
    reps = HEADS // GROUPS
    lower = (jnp.arange(rows)[:, None] >= jnp.arange(rows)[None, :])[None]
    seg = cumulative.T[:, :, None] - cumulative.T[:, None, :]
    weight = jnp.exp(jnp.where(lower, seg, -jnp.inf)).reshape(GROUPS, reps, rows, rows)
    intersection_maps = jnp.einsum("tgn,sgn->gts", out_maps, in_maps, precision=HIGH_BOUND)
    score_matrix = weight * intersection_maps[:, None]
    scaled_values = payload_lines * delta.reshape(rows, GROUPS, reps)[..., None]
    final_output = jnp.einsum("jzlh,hjzc->ljzc", score_matrix, scaled_values, precision=HIGH_BOUND)
    incoming = jnp.einsum(
        "tgn,grpn->tgrp",
        out_maps,
        carried.reshape(GROUPS, reps, HEAD_DIM, STATE),
        precision=HIGH_BOUND,
    )
    final_output = (
        final_output + incoming * jnp.exp(cumulative).reshape(rows, GROUPS, reps)[..., None]
    )
    final_output = (
        final_output + skip_values.reshape(GROUPS, reps)[None, :, :, None] * payload_lines
    )
    gated = final_output.reshape(rows, GROUPS, -1) * jax.nn.silu(gates).reshape(rows, GROUPS, -1)
    normed = gated * lax.rsqrt(jnp.mean(gated * gated, axis=-1, keepdims=True) + 1e-05)
    return normed.reshape(rows, -1) * gain_values[None, :]


def combine(earlier, later):
    return (earlier[0] * later[0], later[0][:, None] * earlier[1] + later[1])


def shards(
    conv_input,
    gate_input,
    step_input,
    cotangent,
    conv_weight,
    conv_bias,
    step_bias,
    decay_log,
    skip_gain,
    norm_gain,
):
    local_rows = conv_input[0, 0]
    count = local_rows.shape[0]
    taps, initial_offset = (conv_weight[0], conv_bias[0])
    step_shift, damping_exponents = (step_bias[0], decay_log[0])
    skip_values, gain_values = (skip_gain[0], norm_gain[0])
    previous = shifted(local_rows[count - (CONV - 1) :], "ctx", 1)
    extended = jnp.concatenate([previous, local_rows], 0).astype(jnp.float32)
    gates = gate_input[0, 0].astype(jnp.float32)
    steps = step_input[0, 0].astype(jnp.float32)
    (state, total), state_pull = jax.vjp(
        fragment_condition, extended, steps, taps, initial_offset, step_shift, damping_exponents
    )
    decay = jnp.exp(total)
    flat_state = state.reshape(HEADS, HEAD_DIM * STATE)
    unity = (jnp.ones((HEADS,), jnp.float32), jnp.zeros((HEADS, HEAD_DIM * STATE), jnp.float32))

    def advance(index, current):
        return shifted(decay[:, None] * current + flat_state, "ctx", 1)

    incoming = lax.fori_loop(
        0, lax.axis_size("ctx") - 1, advance, jnp.zeros((HEADS, HEAD_DIM * STATE), jnp.float32)
    )
    carried = incoming.reshape(HEADS, HEAD_DIM, STATE)
    final_output, layer_pull = jax.vjp(
        shard_layer,
        extended,
        gates,
        steps,
        taps,
        initial_offset,
        step_shift,
        damping_exponents,
        skip_values,
        gain_values,
        carried,
    )
    forward = shifted(final_output.astype(jnp.bfloat16)[None, None], "section", 1)
    grads = layer_pull(cotangent[0, 0].astype(jnp.float32))
    carry_grad = grads[9].reshape(HEADS, HEAD_DIM * STATE)
    outgoing = prefix((decay, carry_grad), "ctx", combine, unity)[1]
    outgoing_grad = outgoing.reshape(HEADS, HEAD_DIM, STATE)
    total_grad = jnp.sum(outgoing_grad * carried, axis=(1, 2)) * decay
    extra = state_pull((outgoing_grad, total_grad))
    ext_grad = grads[0] + extra[0]
    step_grad = grads[2] + extra[1]
    param_terms = (
        grads[3] + extra[2],
        grads[4] + extra[3],
        grads[5] + extra[4],
        grads[6] + extra[5],
        grads[7],
        grads[8],
    )
    returned = shifted(ext_grad[: CONV - 1], "ctx", -1)
    own_grad = ext_grad[CONV - 1 :]
    row_grad = jnp.concatenate(
        [own_grad[: count - (CONV - 1)], own_grad[count - (CONV - 1) :] + returned], 0
    )
    backward = shifted(
        (
            row_grad.astype(jnp.bfloat16)[None, None],
            grads[1].astype(jnp.bfloat16)[None, None],
            step_grad.astype(jnp.bfloat16)[None, None],
        ),
        "section",
        -1,
    )
    summed = lax.psum(
        (
            param_terms[0],
            param_terms[1],
            param_terms[2],
            param_terms[3],
            param_terms[4],
            param_terms[5],
        ),
        ("ctx", "dp"),
    )
    return (
        forward,
        backward[0],
        backward[1],
        backward[2],
        summed[0][None],
        summed[1][None],
        summed[2][None],
        summed[3][None],
        summed[4][None],
        summed[5][None],
    )


MESH = pl.DeviceIdType.MESH
F32 = jnp.float32
BF16 = jnp.bfloat16
INNER = HEADS * HEAD_DIM
REPS = HEADS // GROUPS
WIDE = REPS * HEAD_DIM
MIX = WIDE + 2 * STATE
HALF = GROUPS // 2
NN = ((1,), (0,))
NT = ((1,), (1,))
TN = ((0,), (0,))


def split(a):
    high = a.astype(BF16)
    return high, (a - high.astype(F32)).astype(BF16)


def dot(a, b, dims):
    return lax.dot_general(a, b, (dims, ((), ())), preferred_element_type=F32)


def dot3(a, b, dims):
    return dot(a[0], b[0], dims) + (dot(a[0], b[1], dims) + dot(a[1], b[0], dims))


def group_columns(g):
    return (
        pl.multiple_of(g * WIDE, 128),
        pl.multiple_of(INNER + g * STATE, 128),
        pl.multiple_of(INNER + (GROUPS + g) * STATE, 128),
    )


def pair_kernel(
    conv_in, gate_in, step_in, cot_in, w_in, b_in, sb_in, dl_in, sk_in, ng_in,
    rows_out, table_out, heads_out,
    w_ref, b_ref, per_head, ng_ref,
    uin, steps, token_rows, token_cols, upad, zpad, mix, dsl, ddt, drate, small,
    stage_c, stage_o, stage_s, step_parts, partial, final, relay, small_out, small_in,
    own_sem, xr_sem, sent_sem, land_sem, load_sem, step_sem, ship_sem, relay_sem, dstep_sem,
    sum_sem, hand_sem, fin_sem, pair_sem, mate_sem, plane_sem, world_sem,
):
    core = lax.axis_index("ctx")
    sec = lax.axis_index("section")
    dp = lax.axis_index("dp")
    nsec = lax.axis_size("section")
    ndp = lax.axis_size("dp")
    tok = conv_in.shape[2]
    seq = 2 * tok
    other = 1 - core
    gives = (sec + nsec - 1) // nsec
    takes = 1 - sec // (nsec - 1)
    donor = core * gives
    helper = core * takes
    own_groups = HALF - donor
    last = GROUPS - 1
    halves_of = 4 * HEADS

    def place(c, s, d):
        return {"ctx": c, "section": s, "dp": d}

    def remote(src, dst, recv, c, s, d):
        return pltpu.make_async_remote_copy(
            src_ref=src, dst_ref=dst, send_sem=sent_sem, recv_sem=recv,
            device_id=place(c, s, d), device_id_type=MESH,
        )

    after = lax.rem(sec + 1, nsec)
    before = lax.rem(sec + nsec - 1, nsec)
    sb_ref, dl_ref, sk_ref = (per_head.at[:, at] for at in range(3))
    nxt = rows_out.at[:, pl.ds(0, INNER)]
    gconv = rows_out.at[:, pl.ds(INNER, 5 * INNER)]
    ggate = rows_out.at[:, pl.ds(6 * INNER, INNER)]
    gstep = rows_out.at[pl.ds(0, HEADS), pl.ds(7 * INNER, tok)]
    barrier = pltpu.get_barrier_semaphore()

    def greet(c, s, d):
        pl.semaphore_signal(barrier, inc=1, device_id=place(c, s, d), device_id_type=MESH)

    upper = lax.rem(sec, 2) == 1

    @pl.when(jnp.logical_not(upper))
    def _():
        for c in range(2):
            greet(c, sec + 1, dp)

    def pieces(g):
        xc, bc, cc = group_columns(g)
        return (
            (conv_in.at[0, 0, :, pl.ds(xc, WIDE)], 0, WIDE),
            (conv_in.at[0, 0, :, pl.ds(bc, STATE)], WIDE, STATE),
            (conv_in.at[0, 0, :, pl.ds(cc, STATE)], WIDE + STATE, STATE),
            (gate_in.at[0, 0, :, pl.ds(xc, WIDE)], MIX, WIDE),
            (cot_in.at[0, 0, :, pl.ds(xc, WIDE)], MIX + WIDE, WIDE),
        )

    mine = pl.ds(pl.multiple_of(core * tok, tok), tok)
    theirs = pl.ds(pl.multiple_of(other * tok, tok), tok)
    def tell(sem, s, c=core):
        pl.semaphore_signal(sem, inc=1, device_id=place(c, s, dp), device_id_type=MESH)

    @pl.when(upper)
    def _():
        pl.semaphore_wait(barrier, 2)

    def landed(ref, sem):
        remote(ref, ref, sem, other, sec, dp).wait_recv()

    def sent(ref):
        remote(ref, ref, sent_sem, other, sec, dp).wait_send()

    def hand(src, dst, at):
        return remote(src, dst, ship_sem.at[at], 1, sec - 1, dp)

    def hand_over():
        for src, off, width in pieces(last):
            hand(src, uin.at[HALF, mine, pl.ds(off, width)], 0).start()
        hand(step_in.at[0, 0], steps.at[1, core], 1).start()

    def hand_params():
        xc, bc, cc = group_columns(last)
        for col, width in ((xc, WIDE), (bc, STATE), (cc, STATE)):
            cut = pl.ds(col, width)
            hand(w_in.at[:, :, cut], w_ref.at[pl.ds(1, 1), :, cut], 2).start()
            hand(b_in.at[:, cut], b_ref.at[1, :, cut], 3).start()
        cut = pl.ds(xc, WIDE)
        hand(ng_in.at[:, cut], ng_ref.at[1, :, cut], 4).start()
        hand(sb_in, sb_ref.at[1], 5).start()
        hand(dl_in, dl_ref.at[1], 5).start()
        hand(sk_in, sk_ref.at[1], 5).start()

    @pl.when(upper)
    def _():
        hand_over()
        for c in range(2):
            tell(pair_sem, sec - 1, c)

    @pl.when(sec == 1)
    def _():
        for c in range(2):
            greet(c, 2, dp)

    def later(j):
        return (j + HALF - 1) // HALF

    own_step = pltpu.make_async_copy(step_in.at[0, 0], steps.at[0, core], load_sem.at[0])
    own_step.start()

    def fetch(j, _):
        for src, off, width in pieces(core * HALF + j):
            pltpu.make_async_copy(
                src, uin.at[j, mine, pl.ds(off, width)], own_sem.at[later(j)]
            ).start()
        return 0

    fetch(0, 0)
    params = [
        pltpu.make_async_copy(src, dst, load_sem.at[at])
        for src, dst, at in (
            (sb_in, sb_ref.at[0], 1), (dl_in, dl_ref.at[0], 1), (sk_in, sk_ref.at[0], 1),
            (w_in, w_ref.at[pl.ds(0, 1)], 2), (b_in, b_ref.at[0], 3), (ng_in, ng_ref.at[0], 4),
        )
    ]
    for copy in params:
        copy.start()
    lax.fori_loop(1, own_groups, fetch, 0)
    upad[0:8, :] = jnp.zeros((8, MIX), F32)
    zpad[seq : seq + 8, :] = jnp.zeros((8, MIX), F32)
    for ref in (token_rows, ddt, drate, small, small_out):
        ref[...] = jnp.zeros_like(ref)

    @pl.when(jnp.logical_not(upper))
    def _():
        pl.semaphore_wait(pair_sem, 2)
        tell(mate_sem, sec + 1)

    @pl.when(upper)
    def _():
        pl.semaphore_wait(mate_sem, 1)

    remote(step_in.at[0, 0], steps.at[0, core], step_sem, other, sec, dp).start()

    def exchange(j, _):
        for src, off, width in pieces(other * HALF + j):
            remote(
                src, uin.at[j, mine, pl.ds(off, width)], xr_sem.at[later(j)], other, sec, dp
            ).start()
        return 0

    exchange(0, 0)

    @pl.when(sec == 2)
    def _():
        pl.semaphore_wait(barrier, 2)
        tell(plane_sem, 0)
        tell(plane_sem, 1)
        hand_over()

    @pl.when(jnp.logical_and(sec > 0, core == 0))
    def _():
        hand_params()

    lax.fori_loop(1, HALF - other * gives, exchange, 0)
    own_step.wait()
    pltpu.make_async_copy(per_head.at[0], per_head.at[0], load_sem.at[1]).wait()
    for copy in params[3:]:
        copy.wait()

    def token_terms(which):
        diagonal = lax.broadcasted_iota(jnp.int32, (HEADS, HEADS), 0) == lax.broadcasted_iota(
            jnp.int32, (HEADS, HEADS), 1
        )

        def upright(ref):
            return jnp.sum(jnp.where(diagonal, ref[which], 0.0), axis=1, keepdims=True)

        raw = jnp.concatenate(
            [steps[which, 0].astype(F32), steps[which, 1].astype(F32)], axis=1
        )
        raw = raw + upright(sb_ref)
        delta = jnp.maximum(raw, 0.0) + jnp.log1p(jnp.exp(-jnp.abs(raw)))
        rate = delta * (-jnp.exp(upright(dl_ref)))
        rows2 = lax.broadcasted_iota(jnp.int32, (seq, seq), 0)
        cols2 = lax.broadcasted_iota(jnp.int32, (seq, seq), 1)
        ones_up = jnp.where(rows2 <= cols2, 1.0, 0.0).astype(BF16)
        r_hi, r_rest = rate.astype(BF16), rate - rate.astype(BF16).astype(F32)
        r_mid, r_lo = split(r_rest)
        cumulative = dot(r_hi, ones_up, NN) + (dot(r_mid, ones_up, NN) + dot(r_lo, ones_up, NN))
        for at, value in enumerate((delta, cumulative, jax.nn.sigmoid(raw), rate)):
            top = pl.multiple_of(which * halves_of + at * HEADS, HEADS)
            token_rows[pl.ds(top, HEADS), :] = value
        token_cols[...] = token_rows[...].T

    def group(turn, _):
        j = turn + (turn // (HALF - 1)) * donor
        helping = j // HALF
        g = core * HALF + j - helping
        ours = helping == 0
        slot_p = j + helping
        lane0 = helping * halves_of
        cols = group_columns(g)
        blocks = [(0, cols[0])]
        for base, col in ((WIDE, cols[1]), (WIDE + STATE, cols[2])):
            for part in range(STATE // 128):
                blocks.append((base + part * 128, pl.multiple_of(col + part * 128, 128)))

        def conv_rows(start, count, fresh):
            for off, col in blocks:
                here = slice(off, off + 128)
                if fresh:
                    upad[pl.ds(pl.multiple_of(start + 8, 8), count), here] = uin[
                        j, pl.ds(start, count), here
                    ].astype(F32)
                window = upad[pl.ds(start, count + 8), here]
                z = b_ref[helping, :, pl.ds(col, 128)]
                z = z + w_ref[helping, 3:4, pl.ds(col, 128)] * window[8:]
                for k in range(CONV - 1):
                    tap = w_ref[helping, pl.ds(k, 1), pl.ds(col, 128)]
                    z = z + tap * pltpu.roll(window, 3 - k, 0)[8:]
                s = jax.nn.sigmoid(z)
                mix[pl.ds(start, count), here] = z * s
                dsl[pl.ds(start, count), here] = s * (1.0 + z * (1.0 - s))

        def arrived(at, rows, done):
            @pl.when(j == 0)
            def _():
                done(uin.at[0, rows], at.at[0])

            for count, case in ((HALF - 1, 0), (HALF - 2, 1)):

                @pl.when(jnp.logical_and(j == 1, donor == case))
                def _():
                    done(uin.at[pl.ds(1, count), rows], at.at[1])

        arrived(own_sem, mine, lambda ref, sem: pltpu.make_async_copy(ref, ref, sem).wait())

        @pl.when(helping == 1)
        def _():
            some = pl.ds(0, WIDE + 2 * STATE)
            for at, ref in enumerate((
                uin.at[HALF], steps.at[1], w_ref.at[pl.ds(1, 1), :, some], b_ref.at[1, :, some],
                ng_ref.at[1, :, pl.ds(0, WIDE)], per_head.at[1],
            )):
                landed(ref, ship_sem.at[at])

        conv_rows(pl.multiple_of(core * tok, tok), tok, True)

        @pl.when(j == 0)
        def _():
            landed(steps.at[0, other], step_sem)

        @pl.when(jnp.logical_and(j == 0, sec == 1))
        def _():
            pl.semaphore_wait(plane_sem, 1)
            for k in range(1, ndp):
                greet(core, 0, lax.rem(dp + k, ndp))

        @pl.when(lax.rem(j, HALF) == 0)
        def _():
            token_terms(helping)

        arrived(xr_sem, theirs, landed)

        conv_rows(pl.multiple_of(other * tok, tok), tok, True)
        conv_rows(tok, 8, False)

        lane = lax.broadcasted_iota(jnp.int32, (seq, 128), 1)
        lane1 = lax.broadcasted_iota(jnp.int32, (1, 128), 1)
        lane16 = lax.broadcasted_iota(jnp.int32, (1, HEADS), 1)
        row = lax.broadcasted_iota(jnp.int32, (seq, seq), 0)
        column = lax.broadcasted_iota(jnp.int32, (seq, seq), 1)
        first = lane < HEAD_DIM

        def pick(at):
            return jnp.sum(
                jnp.where(lane == lane0 + at, token_cols[...], 0.0), axis=1, keepdims=True
            )

        def pick1(ref, h):
            return jnp.sum(jnp.where(lane16 == h, ref[helping], 0.0), axis=1, keepdims=True)

        x = mix[:, 0:WIDE]
        bmap = split(mix[:, WIDE : WIDE + STATE])
        cmap = split(mix[:, WIDE + STATE : MIX])
        h0 = g * REPS
        dt2 = jnp.where(first, pick(h0), pick(h0 + 1))
        skip2 = jnp.where(first[0:1], pick1(sk_ref, h0), pick1(sk_ref, h0 + 1))
        xs = x * dt2
        xs_p = split(xs)
        scores = dot3(cmap, bmap, NT)
        decay, mixed, ys = [], [], []
        for r in range(REPS):
            seg = pick(HEADS + h0 + r) - token_rows[pl.ds(lane0 + HEADS + h0 + r, 1), :]
            w = jnp.exp(jnp.where(row >= column, seg, -jnp.inf))
            a = scores * w
            a_p = split(a)
            decay.append(w)
            mixed.append((a, a_p))
            ys.append(dot3(a_p, xs_p, NN))
        y = jnp.where(first, ys[0], ys[1]) + skip2 * x
        gate = uin[j, :, MIX : MIX + WIDE].astype(F32)
        cot = uin[j, :, MIX + WIDE : MIX + 2 * WIDE].astype(F32)
        gain = ng_ref[helping, :, pl.ds(cols[0], WIDE)]
        s = jax.nn.sigmoid(gate)
        act = gate * s
        gated = y * act
        scale = lax.rsqrt(jnp.mean(gated * gated, axis=1, keepdims=True) + 1e-05)
        normed = gated * scale
        stage_o[j, :, 0:WIDE] = (normed * gain).astype(BF16)
        dn = cot * gain
        dgated = scale * (dn - normed * jnp.mean(dn * normed, axis=1, keepdims=True))
        dy = dgated * act
        stage_o[j, :, WIDE : 2 * WIDE] = (dgated * y * (s * (1.0 + gate * (1.0 - s)))).astype(BF16)

        even = lax.rem(j, 2) == 0
        out_cut = pl.ds(cols[0], WIDE)

        def send_half(base, t, dst, sem, s):
            remote(
                stage_o.at[j, pl.ds(t * tok, tok), pl.ds(base, WIDE)], dst, sem, t, s, dp
            ).start()

        direct = jnp.logical_and(
            ours, jnp.logical_and(sec < nsec - 1, jnp.logical_not(jnp.logical_and(sec == 1, even)))
        )

        @pl.when(direct)
        def _():
            for t in range(2):
                send_half(0, t, nxt.at[:, out_cut], land_sem, sec + 1)

        @pl.when(jnp.logical_and(ours, jnp.logical_and(sec == 1, even)))
        def _():
            slot = core * (HALF // 2) + j // 2
            for t in range(2):
                send_half(0, t, relay.at[slot], relay_sem, 3)

        @pl.when(jnp.logical_and(ours, jnp.logical_or(sec == 1, sec == 3)))
        def _():
            for t in range(2):
                send_half(
                    WIDE, t, ggate.at[:, out_cut], land_sem, sec - 1
                )

        @pl.when(jnp.logical_and(ours, sec == 2))
        def _():
            slot = core * HALF + j
            for t in range(2):
                send_half(WIDE, t, relay.at[slot], relay_sem, 0)

        @pl.when(helping == 1)
        def _():
            ggate[:, out_cut] = stage_o[j, tok : 2 * tok, WIDE : 2 * WIDE]
            send_half(WIDE, 0, ggate.at[:, out_cut], land_sem, sec)

        @pl.when(jnp.logical_and(helping == 1, sec < nsec - 2))
        def _():
            for t in range(2):
                send_half(0, t, nxt.at[:, out_cut], land_sem, sec + 2)

        partial[dp, slot_p, 6:8, :] = jnp.zeros((2, MIX), F32)
        partial[dp, slot_p, 5:6, WIDE:MIX] = jnp.zeros((1, MIX - WIDE), F32)
        partial[dp, slot_p, 5:6, 0:WIDE] = jnp.sum(cot * normed, axis=0, keepdims=True)
        dyx = jnp.sum(dy * x, axis=0, keepdims=True)
        dscore = jnp.zeros((seq, seq), F32)
        dy_p = split(dy)
        das = []
        for r in range(REPS):
            own = first if r == 0 else jnp.logical_not(first)
            da = dot3(split(jnp.where(own, dy, 0.0)), xs_p, NT)
            das.append(da)
            dscore = dscore + da * decay[r]
        ds_p = split(dscore)

        def conv_back(off, width, start):
            for part in range(width // 128):
                here = slice(off + part * 128, off + part * 128 + 128)
                col = pl.multiple_of(start + part * 128, 128)
                dz = zpad[0:seq, here]
                du = jnp.zeros((seq, 128), F32)
                for k in range(CONV):
                    du = du + (
                        w_ref[helping, pl.ds(k, 1), pl.ds(col, 128)]
                        * zpad[3 - k : 3 - k + seq, here]
                    )
                    partial[dp, slot_p, pl.ds(k, 1), here] = jnp.sum(
                        dz * upad[5 + k : 5 + k + seq, here], axis=0, keepdims=True
                    )
                partial[dp, slot_p, pl.ds(4, 1), here] = jnp.sum(dz, axis=0, keepdims=True)
                stage_c[j, :, here] = du.astype(BF16)

            @pl.when(helping == 1)
            def _():
                gconv[:, pl.ds(start, width)] = stage_c[j, tok : 2 * tok, off : off + width]
                remote(
                    stage_c.at[j, pl.ds(0, tok), pl.ds(off, width)],
                    gconv.at[:, pl.ds(start, width)],
                    land_sem, 0, sec, dp,
                ).start()

            @pl.when(jnp.logical_and(ours, sec > 0))
            def _():
                for t in range(2):
                    remote(
                        stage_c.at[j, pl.ds(t * tok, tok), pl.ds(off, width)],
                        gconv.at[:, pl.ds(start, width)],
                        land_sem, t, sec - 1, dp,
                    ).start()

        zpad[0:seq, WIDE + STATE : MIX] = dot3(ds_p, bmap, NN) * dsl[:, WIDE + STATE : MIX]
        conv_back(WIDE + STATE, STATE, cols[2])
        zpad[0:seq, WIDE : WIDE + STATE] = dot3(ds_p, cmap, TN) * dsl[:, WIDE : WIDE + STATE]
        conv_back(WIDE, STATE, cols[1])
        dxs = jnp.where(first, dot3(mixed[0][1], dy_p, TN), dot3(mixed[1][1], dy_p, TN))
        zpad[0:seq, 0:WIDE] = (skip2 * dy + dxs * dt2) * dsl[:, 0:WIDE]
        conv_back(0, WIDE, cols[0])
        upper = jnp.where(row <= column, 1.0, 0.0).astype(BF16)
        dxx = dxs * x
        for r in range(REPS):
            own = first if r == 0 else jnp.logical_not(first)
            p = split(das[r] * mixed[r][0])
            later = dot(upper, p[0], NN) + dot(upper, p[1], NN)
            dr = jnp.sum(jnp.where(row > column, later, 0.0), axis=1, keepdims=True)
            drate[...] += jnp.where(lane == lane0 + h0 + r, dr, 0.0)
            total = jnp.sum(jnp.where(own[0:1], dyx, 0.0), axis=1, keepdims=True)
            small[2:3, :] += jnp.where(lane1 == lane0 + h0 + r, total, 0.0)
            dd = jnp.sum(jnp.where(own, dxx, 0.0), axis=1, keepdims=True)
            ddt[...] += jnp.where(lane == lane0 + h0 + r, dd, 0.0)

        @pl.when(jnp.logical_and(j == 0, sec == 0))
        def _():
            pl.semaphore_wait(plane_sem, 1)
            pl.semaphore_wait(barrier, ndp - 1)
            for s in range(1, 4):
                pl.semaphore_signal(
                    world_sem, inc=1, device_id=place(core, s, dp), device_id_type=MESH
                )

        @pl.when(jnp.logical_and(j == 0, sec > 0))
        def _():
            pl.semaphore_wait(world_sem, 1)

        @pl.when(ours)
        def _():
            spread(j)

        @pl.when(helping == 1)
        def _():
            remote(
                partial.at[dp, HALF + 1], partial.at[dp, HALF - 1],
                hand_sem.at[0], core, sec + 1, dp,
            ).start()

        return 0

    def spread(slot):
        for k in range(1, ndp):
            to = lax.rem(dp + k, ndp)
            remote(
                partial.at[dp, slot], partial.at[dp, slot], sum_sem, core, sec, to
            ).start()

    lax.fori_loop(0, own_groups + helper, group, 0)

    def pass_on(slots, groups, out, sem, s):
        landed(relay.at[pl.ds(0, slots)], relay_sem)
        for slot, g in zip(range(slots), groups):
            remote(
                relay.at[slot], out.at[:, pl.ds(g * WIDE, WIDE)], sem, core, s, dp
            ).start()

    @pl.when(sec == 0)
    def _():
        pass_on(GROUPS - 1, range(GROUPS - 1), ggate, land_sem, 1)

    @pl.when(sec == 3)
    def _():
        pass_on(GROUPS // 2, range(0, GROUPS, 2), nxt, land_sem, 2)

    @pl.when(sec == 0)
    def _():
        nxt[...] = jnp.zeros_like(nxt)

    @pl.when(sec == nsec - 1)
    def _():
        gconv[...] = jnp.zeros_like(gconv)
        ggate[...] = jnp.zeros_like(ggate)
        gstep[...] = jnp.zeros_like(gstep)

    def step_terms(which, into):
        lane0 = which * halves_of
        heads = slice(lane0, lane0 + HEADS)
        dr16 = drate[:, heads]
        gate = token_cols[:, lane0 + 2 * HEADS : lane0 + 3 * HEADS]
        rate = token_cols[:, lane0 + 3 * HEADS : lane0 + 4 * HEADS]
        dstep = (ddt[:, heads] - dr16 * jnp.exp(dl_ref[which])) * gate
        into[0:1, 0:HEADS] = jnp.sum(dstep, axis=0, keepdims=True)
        into[1:2, 0:HEADS] = jnp.sum(dr16 * rate, axis=0, keepdims=True)
        drate[:, heads] = dstep

    step_terms(0, small)

    @pl.when(helper == 1)
    def _():
        step_terms(1, small_out)
        small_out[2:3, 0:HEADS] = small[2:3, halves_of : halves_of + HEADS]
        remote(
            small_out, small_in, hand_sem.at[1], core, sec + 1, dp
        ).start()

    turned = drate[...].T
    for t in range(2):
        for c in range(2):
            stage_s[t, c] = turned[c * 8 : c * 8 + 8, t * tok : (t + 1) * tok].astype(BF16)

    @pl.when(sec > 0)
    def _():
        for t in range(2):
            remote(
                stage_s.at[t, core], step_parts.at[0, core], dstep_sem, t, sec - 1, dp
            ).start()

    @pl.when(helper == 1)
    def _():
        for c in range(2):
            top = halves_of + c * 8
            stage_s[2, c] = turned[top : top + 8, 0:tok].astype(BF16)
            step_parts[1, c] = turned[top : top + 8, tok : 2 * tok].astype(BF16)
        remote(stage_s.at[2], step_parts.at[1], dstep_sem, other, sec, dp).start()

    @pl.when(donor == 1)
    def _():
        landed(partial.at[dp, HALF - 1], hand_sem.at[0])
        landed(small_in, hand_sem.at[1])
        spread(HALF - 1)
        small[...] += small_in[...]

    partial[dp, HALF] = jnp.zeros((8, MIX), F32)
    partial[dp, HALF, :, 0:128] = small[...]
    spread(HALF)
    landed(partial.at[pl.ds(0, ndp - 1), pl.ds(0, HALF + 1)], sum_sem)
    total = partial[0, 0 : HALF + 1]
    for k in range(1, ndp):
        total = total + partial[k, 0 : HALF + 1]
    final[core] = total
    remote(final.at[core], final.at[core], fin_sem, other, sec, dp).start()
    landed(final.at[other], fin_sem)
    for g in range(GROUPS):
        c, j = g // HALF, g % HALF
        table_out[5:6, g * WIDE : (g + 1) * WIDE] = final[c, j, 5:6, 0:WIDE]
        for off, width, col in (
            (0, WIDE, g * WIDE),
            (WIDE, STATE, INNER + g * STATE),
            (WIDE + STATE, STATE, INNER + (GROUPS + g) * STATE),
        ):
            table_out[0:CONV, col : col + width] = final[c, j, 0:CONV, off : off + width]
            table_out[CONV : CONV + 1, col : col + width] = final[c, j, CONV : CONV + 1, off : off + width]
    for at in range(3):
        heads_out[at] = final[0, HALF, at : at + 1, 0:HEADS] + final[1, HALF, at : at + 1, 0:HEADS]

    @pl.when(sec < nsec - 1)
    def _():
        @pl.when(core == 0)
        def _():
            landed(step_parts, dstep_sem)

        @pl.when(core == 1)
        def _():
            landed(step_parts.at[0], dstep_sem)

        for c in range(2):
            both = step_parts[0, c].astype(F32) + step_parts[1, c].astype(F32)
            gstep[c * 8 : c * 8 + 8, :] = both.astype(BF16)

    first = pl.ds(0, HALF - 1)
    half = pl.ds(0, WIDE)
    sent(steps.at[0, 0])
    sent(uin.at[first, pl.ds(0, tok)])
    sent(partial.at[pl.ds(0, ndp - 1), pl.ds(0, HALF + 1)])
    sent(final.at[0])

    @pl.when(other * gives == 0)
    def _():
        sent(uin.at[0, pl.ds(0, tok)])

    @pl.when(sec == 0)
    def _():
        sent(relay.at[pl.ds(0, GROUPS - 1)])

    @pl.when(sec == nsec - 1)
    def _():
        sent(relay.at[pl.ds(0, GROUPS // 2)])

    @pl.when(sec > 0)
    def _():
        sent(uin.at[HALF, pl.ds(0, tok)])
        sent(steps.at[1, 0])
        sent(stage_c.at[first])
        sent(stage_o.at[first, :, half])
        sent(stage_s.at[0])

    @pl.when(jnp.logical_and(sec > 0, core == 0))
    def _():
        some = pl.ds(0, WIDE + 2 * STATE)
        for ref in (
            w_ref.at[pl.ds(1, 1), :, some], b_ref.at[1, :, some], ng_ref.at[1, :, half],
            per_head.at[1], stage_c.at[HALF - 1], stage_o.at[HALF - 1, :, half],
        ):
            sent(ref)

    @pl.when(sec < nsec - 1)
    def _():
        sent(stage_o.at[first, :, half])

    @pl.when(jnp.logical_and(sec < nsec - 1, donor == 0))
    def _():
        sent(stage_o.at[HALF - 1, :, half])

    @pl.when(helper == 1)
    def _():
        sent(stage_c.at[HALF, pl.ds(0, tok)])
        sent(stage_o.at[HALF, pl.ds(0, tok), half])
        sent(stage_s.at[2])
        sent(partial.at[dp, HALF + 1])
        sent(small_out)

    @pl.when(jnp.logical_and(helper == 1, sec < nsec - 2))
    def _():
        sent(stage_o.at[HALF, :, half])

    whole, less = 6 * INNER, 6 * (INNER - WIDE)

    @pl.when(sec == nsec - 1)
    def _():
        landed(nxt, land_sem)

    for c, columns in ((0, whole), (1, less)):

        @pl.when(jnp.logical_and(sec == 0, core == c))
        def _():
            landed(rows_out.at[:, pl.ds(0, columns)], land_sem)

        @pl.when(jnp.logical_and(sec * (nsec - 1 - sec) > 0, core == c))
        def _():
            landed(rows_out.at[:, pl.ds(0, INNER + columns)], land_sem)


def finish_kernel(
    rows_in, table_in, heads_in, nxt, gconv, ggate, gstep, gtap, gcb, gsb, gdl, gsk, gng, sem
):
    tok = rows_in.shape[0]
    copies = [
        (rows_in.at[:, pl.ds(INNER, 5 * INNER)], gconv.at[0, 0]),
        (rows_in.at[:, pl.ds(0, INNER)], nxt.at[0, 0]),
        (rows_in.at[:, pl.ds(6 * INNER, INNER)], ggate.at[0, 0]),
        (table_in.at[pl.ds(0, CONV)], gtap.at[0]),
        (table_in.at[pl.ds(CONV, 1)], gcb),
        (table_in.at[pl.ds(CONV + 1, 1), pl.ds(0, INNER)], gng),
        (rows_in.at[pl.ds(0, HEADS), pl.ds(7 * INNER, tok)], gstep.at[0, 0]),
        (heads_in.at[0], gsb),
        (heads_in.at[1], gdl),
        (heads_in.at[2], gsk),
    ]
    copies = [pltpu.make_async_copy(a, b, sem.at[at]) for at, (a, b) in enumerate(copies)]
    for copy in copies:
        copy.start()
    for copy in copies:
        copy.wait()


def paired(
    conv_input, gate_input, step_input, cotangent, conv_weight,
    conv_bias, step_bias, decay_log, skip_gain, norm_gain,
):
    tok = conv_input.shape[2]
    seq = 2 * tok
    ndp = lax.axis_size("dp")
    hbm = pl.BlockSpec(memory_space=pl.ANY)
    vmem = pl.BlockSpec(memory_space=pltpu.VMEM)
    scratch = [
        pltpu.VMEM((2,) + conv_weight.shape[1:], F32),
        pltpu.VMEM((2,) + conv_bias.shape, F32),
        pltpu.VMEM((2, 3) + step_bias.shape, F32),
        pltpu.VMEM((2,) + norm_gain.shape, F32),
        pltpu.VMEM((HALF + 1, seq, MIX + 2 * WIDE), BF16),
        pltpu.VMEM((2, 2, HEADS, tok), BF16),
        pltpu.VMEM((128, seq), F32),
        pltpu.VMEM((seq, 128), F32),
        pltpu.VMEM((seq + 8, MIX), F32),
        pltpu.VMEM((seq + 8, MIX), F32),
        pltpu.VMEM((seq, MIX), F32),
        pltpu.VMEM((seq, MIX), F32),
        pltpu.VMEM((seq, 128), F32),
        pltpu.VMEM((seq, 128), F32),
        pltpu.VMEM((8, 128), F32),
        pltpu.VMEM((HALF + 1, seq, MIX), BF16),
        pltpu.VMEM((HALF + 1, seq, 2 * WIDE), BF16),
        pltpu.VMEM((3, 2, HEADS // 2, tok), BF16),
        pltpu.VMEM((2, 2, HEADS // 2, tok), BF16),
        pltpu.VMEM((ndp, HALF + 2, 8, MIX), F32),
        pltpu.VMEM((2, HALF + 1, 8, MIX), F32),
        pltpu.VMEM((GROUPS, tok, WIDE), BF16),
        pltpu.VMEM((8, 128), F32),
        pltpu.VMEM((8, 128), F32),
        pltpu.SemaphoreType.DMA((2,)),
        pltpu.SemaphoreType.DMA((2,)),
    ]
    one = pltpu.SemaphoreType.DMA
    scratch += [one, one, one((5,)), one, one((6,)), one, one, one, one((2,)), one]
    scratch += [pltpu.SemaphoreType.REGULAR] * 4
    turned = jnp.swapaxes(step_input, 2, 3)
    shapes = [
        (gate_input.shape, BF16),
        (conv_input.shape, BF16),
        (gate_input.shape, BF16),
        (turned.shape, BF16),
        (conv_weight.shape, F32),
        (conv_bias.shape, F32),
        (step_bias.shape, F32),
        (decay_log.shape, F32),
        (skip_gain.shape, F32),
        (norm_gain.shape, F32),
    ]
    inputs = [
        pltpu.with_memory_space_constraint(a, pltpu.HBM)
        for a in (
            conv_input, gate_input, turned, cotangent, conv_weight,
            conv_bias, step_bias, decay_log, skip_gain, norm_gain,
        )
    ]
    sent = pl.pallas_call(
        pair_kernel,
        name="mixer_tick",
        in_specs=[hbm] * 10,
        out_specs=[vmem] * 3,
        out_shape=[
            pltpu.VMEM((tok, 7 * INNER + tok), BF16),
            pltpu.VMEM((8, conv_bias.shape[1]), F32),
            pltpu.VMEM((3,) + step_bias.shape, F32),
        ],
        scratch_shapes=scratch,
        compiler_params=pltpu.CompilerParams(
            collective_id=0, has_side_effects=True, vmem_limit_bytes=24 * 1024 * 1024
        ),
    )(*inputs)
    done = pl.pallas_call(
        finish_kernel,
        name="mixer_finish",
        in_specs=[vmem] * 3,
        out_specs=[hbm] * 10,
        out_shape=[jax.ShapeDtypeStruct(shape, kind) for shape, kind in shapes],
        scratch_shapes=[pltpu.SemaphoreType.DMA((10,))],
        compiler_params=pltpu.CompilerParams(vmem_limit_bytes=1024 * 1024),
    )(*sent)
    return tuple(done[:3]) + (jnp.swapaxes(done[3], 2, 3),) + tuple(done[4:])


def solution(mesh):
    in_specs = (
        P("section", "dp", "ctx", None),
        P("section", "dp", "ctx", None),
        P("section", "dp", "ctx", None),
        P("section", "dp", "ctx", None),
        P("section", None, None),
        P("section", None),
        P("section", None),
        P("section", None),
        P("section", None),
        P("section", None),
    )
    out_specs = (
        P("section", "dp", "ctx", None),
        P("section", "dp", "ctx", None),
        P("section", "dp", "ctx", None),
        P("section", "dp", "ctx", None),
        P("section", None, None),
        P("section", None),
        P("section", None),
        P("section", None),
        P("section", None),
        P("section", None),
    )
    body = paired if (mesh.shape["ctx"], mesh.shape["section"]) == (2, 4) else shards
    return jax.shard_map(body, mesh=mesh, in_specs=in_specs, out_specs=out_specs, check_vma=False)
```

```python
import functools
import jax
import jax.numpy as jnp
from jax import lax
from jax.experimental import pallas as pl
from jax.experimental.pallas import tpu as pltpu
from jax.sharding import PartitionSpec as P

HEADS = 16
HEAD_DIM = 64
STATE = 256
GROUPS = 8
CONV = 4


HIGH_BOUND = lax.Precision.HIGHEST


def shifted(block, axis, distance):
    devices = range(lax.axis_size(axis))
    route = [(i - distance, i) for i in devices if i - distance in devices]
    return lax.ppermute(block, axis, route)


def prefix(part, axis, combine, identity):
    count = lax.axis_size(axis)
    place = lax.axis_index(axis)
    ahead = count - 1 - place
    gathered = jax.tree.map(lambda a: lax.all_gather(a, axis), part)
    state = jax.tree.map(lambda a, e: jnp.zeros_like(a) + jnp.asarray(e, a.dtype), part, identity)

    def one(turn, state):
        source = count - 1 - turn
        return combine(
            state, jax.tree.map(lambda a: lax.dynamic_index_in_dim(a, source, 0, False), gathered)
        )

    return lax.fori_loop(0, ahead, one, state)


def conv_mix(extended, taps, initial_offset):
    rows = extended.shape[0] - (CONV - 1)
    total = initial_offset[None, :]
    for tap in range(CONV):
        total = total + taps[tap][None, :] * extended[tap : tap + rows]
    return jax.nn.silu(total)


def split_mix(mixed, steps, step_shift, damping_exponents):
    rows = mixed.shape[0]
    inner = HEADS * HEAD_DIM
    payload_lines = mixed[:, :inner].reshape(rows, GROUPS, HEADS // GROUPS, HEAD_DIM)
    in_maps = mixed[:, inner : inner + GROUPS * STATE].reshape(rows, GROUPS, STATE)
    out_maps = mixed[:, inner + GROUPS * STATE :].reshape(rows, GROUPS, STATE)
    delta = jax.nn.softplus(steps + step_shift[None, :])
    upto = jnp.tril(jnp.ones((rows, rows), jnp.float32))
    rates = delta * (-jnp.exp(damping_exponents))[None, :]
    cumulative = jnp.dot(upto, rates, precision=HIGH_BOUND)
    return (payload_lines, in_maps, out_maps, delta, cumulative)


def fragment_condition(extended, steps, taps, initial_offset, step_shift, damping_exponents):
    payload_lines, in_maps, out_maps, delta, cumulative = split_mix(
        conv_mix(extended, taps, initial_offset), steps, step_shift, damping_exponents
    )
    rows = payload_lines.shape[0]
    total = cumulative[-1]
    weight = (jnp.exp(total[None, :] - cumulative) * delta).reshape(rows, GROUPS, HEADS // GROUPS)
    state = jnp.einsum(
        "tgrp,tgn->grpn", payload_lines * weight[..., None], in_maps, precision=HIGH_BOUND
    )
    return (state.reshape(HEADS, HEAD_DIM, STATE), total)


def shard_layer(
    extended,
    gates,
    steps,
    taps,
    initial_offset,
    step_shift,
    damping_exponents,
    skip_values,
    gain_values,
    carried,
):
    payload_lines, in_maps, out_maps, delta, cumulative = split_mix(
        conv_mix(extended, taps, initial_offset), steps, step_shift, damping_exponents
    )
    rows = payload_lines.shape[0]
    reps = HEADS // GROUPS
    lower = (jnp.arange(rows)[:, None] >= jnp.arange(rows)[None, :])[None]
    seg = cumulative.T[:, :, None] - cumulative.T[:, None, :]
    weight = jnp.exp(jnp.where(lower, seg, -jnp.inf)).reshape(GROUPS, reps, rows, rows)
    intersection_maps = jnp.einsum("tgn,sgn->gts", out_maps, in_maps, precision=HIGH_BOUND)
    score_matrix = weight * intersection_maps[:, None]
    scaled_values = payload_lines * delta.reshape(rows, GROUPS, reps)[..., None]
    final_output = jnp.einsum("jzlh,hjzc->ljzc", score_matrix, scaled_values, precision=HIGH_BOUND)
    incoming = jnp.einsum(
        "tgn,grpn->tgrp",
        out_maps,
        carried.reshape(GROUPS, reps, HEAD_DIM, STATE),
        precision=HIGH_BOUND,
    )
    final_output = (
        final_output + incoming * jnp.exp(cumulative).reshape(rows, GROUPS, reps)[..., None]
    )
    final_output = (
        final_output + skip_values.reshape(GROUPS, reps)[None, :, :, None] * payload_lines
    )
    gated = final_output.reshape(rows, GROUPS, -1) * jax.nn.silu(gates).reshape(rows, GROUPS, -1)
    normed = gated * lax.rsqrt(jnp.mean(gated * gated, axis=-1, keepdims=True) + 1e-05)
    return normed.reshape(rows, -1) * gain_values[None, :]


def combine(earlier, later):
    return (earlier[0] * later[0], later[0][:, None] * earlier[1] + later[1])


def shards(
    conv_input,
    gate_input,
    step_input,
    cotangent,
    conv_weight,
    conv_bias,
    step_bias,
    decay_log,
    skip_gain,
    norm_gain,
):
    local_rows = conv_input[0, 0]
    count = local_rows.shape[0]
    taps, initial_offset = (conv_weight[0], conv_bias[0])
    step_shift, damping_exponents = (step_bias[0], decay_log[0])
    skip_values, gain_values = (skip_gain[0], norm_gain[0])
    previous = shifted(local_rows[count - (CONV - 1) :], "ctx", 1)
    extended = jnp.concatenate([previous, local_rows], 0).astype(jnp.float32)
    gates = gate_input[0, 0].astype(jnp.float32)
    steps = step_input[0, 0].astype(jnp.float32)
    (state, total), state_pull = jax.vjp(
        fragment_condition, extended, steps, taps, initial_offset, step_shift, damping_exponents
    )
    decay = jnp.exp(total)
    flat_state = state.reshape(HEADS, HEAD_DIM * STATE)
    unity = (jnp.ones((HEADS,), jnp.float32), jnp.zeros((HEADS, HEAD_DIM * STATE), jnp.float32))

    def advance(index, current):
        return shifted(decay[:, None] * current + flat_state, "ctx", 1)

    incoming = lax.fori_loop(
        0, lax.axis_size("ctx") - 1, advance, jnp.zeros((HEADS, HEAD_DIM * STATE), jnp.float32)
    )
    carried = incoming.reshape(HEADS, HEAD_DIM, STATE)
    final_output, layer_pull = jax.vjp(
        shard_layer,
        extended,
        gates,
        steps,
        taps,
        initial_offset,
        step_shift,
        damping_exponents,
        skip_values,
        gain_values,
        carried,
    )
    forward = shifted(final_output.astype(jnp.bfloat16)[None, None], "section", 1)
    grads = layer_pull(cotangent[0, 0].astype(jnp.float32))
    carry_grad = grads[9].reshape(HEADS, HEAD_DIM * STATE)
    outgoing = prefix((decay, carry_grad), "ctx", combine, unity)[1]
    outgoing_grad = outgoing.reshape(HEADS, HEAD_DIM, STATE)
    total_grad = jnp.sum(outgoing_grad * carried, axis=(1, 2)) * decay
    extra = state_pull((outgoing_grad, total_grad))
    ext_grad = grads[0] + extra[0]
    step_grad = grads[2] + extra[1]
    param_terms = (
        grads[3] + extra[2],
        grads[4] + extra[3],
        grads[5] + extra[4],
        grads[6] + extra[5],
        grads[7],
        grads[8],
    )
    returned = shifted(ext_grad[: CONV - 1], "ctx", -1)
    own_grad = ext_grad[CONV - 1 :]
    row_grad = jnp.concatenate(
        [own_grad[: count - (CONV - 1)], own_grad[count - (CONV - 1) :] + returned], 0
    )
    backward = shifted(
        (
            row_grad.astype(jnp.bfloat16)[None, None],
            grads[1].astype(jnp.bfloat16)[None, None],
            step_grad.astype(jnp.bfloat16)[None, None],
        ),
        "section",
        -1,
    )
    summed = lax.psum(
        (
            param_terms[0],
            param_terms[1],
            param_terms[2],
            param_terms[3],
            param_terms[4],
            param_terms[5],
        ),
        ("ctx", "dp"),
    )
    return (
        forward,
        backward[0],
        backward[1],
        backward[2],
        summed[0][None],
        summed[1][None],
        summed[2][None],
        summed[3][None],
        summed[4][None],
        summed[5][None],
    )


MESH = pl.DeviceIdType.MESH
F32 = jnp.float32
BF16 = jnp.bfloat16
INNER = HEADS * HEAD_DIM
REPS = HEADS // GROUPS
WIDE = REPS * HEAD_DIM
MIX = WIDE + 2 * STATE
HALF = GROUPS // 2
NN = ((1,), (0,))
NT = ((1,), (1,))
TN = ((0,), (0,))


def split(a):
    high = a.astype(BF16)
    return high, (a - high.astype(F32)).astype(BF16)


def dot(a, b, dims):
    return lax.dot_general(a, b, (dims, ((), ())), preferred_element_type=F32)


def dot3(a, b, dims):
    return dot(a[0], b[0], dims) + (dot(a[0], b[1], dims) + dot(a[1], b[0], dims))


def group_columns(g):
    return (
        pl.multiple_of(g * WIDE, 128),
        pl.multiple_of(INNER + g * STATE, 128),
        pl.multiple_of(INNER + (GROUPS + g) * STATE, 128),
    )


def pair_kernel(
    conv_in, gate_in, step_in, cot_in, w_in, b_in, sb_in, dl_in, sk_in, ng_in,
    rows_out, table_out, heads_out,
    w_ref, b_ref, per_head, ng_ref,
    uin, steps, token_rows, token_cols, upad, zpad, mix, dsl, ddt, drate, small,
    stage_c, stage_o, stage_s, step_parts, partial, final, relay, small_out, small_in,
    own_sem, xr_sem, sent_sem, land_sem, load_sem, step_sem, ship_sem, relay_sem, dstep_sem,
    sum_sem, hand_sem, fin_sem, pair_sem, mate_sem, plane_sem, world_sem,
):
    core = lax.axis_index("ctx")
    sec = lax.axis_index("section")
    dp = lax.axis_index("dp")
    nsec = lax.axis_size("section")
    ndp = lax.axis_size("dp")
    tok = conv_in.shape[2]
    seq = 2 * tok
    other = 1 - core
    gives = (sec + nsec - 1) // nsec
    takes = 1 - sec // (nsec - 1)
    donor = core * gives
    helper = core * takes
    own_groups = HALF - donor
    last = GROUPS - 1
    halves_of = 4 * HEADS

    def place(c, s, d):
        return {"ctx": c, "section": s, "dp": d}

    def remote(src, dst, recv, c, s, d):
        return pltpu.make_async_remote_copy(
            src_ref=src, dst_ref=dst, send_sem=sent_sem, recv_sem=recv,
            device_id=place(c, s, d), device_id_type=MESH,
        )

    after = lax.rem(sec + 1, nsec)
    before = lax.rem(sec + nsec - 1, nsec)
    sb_ref, dl_ref, sk_ref = (per_head.at[:, at] for at in range(3))
    nxt = rows_out.at[:, pl.ds(0, INNER)]
    gconv = rows_out.at[:, pl.ds(INNER, 5 * INNER)]
    ggate = rows_out.at[:, pl.ds(6 * INNER, INNER)]
    gstep = rows_out.at[pl.ds(0, HEADS), pl.ds(7 * INNER, tok)]
    barrier = pltpu.get_barrier_semaphore()

    def greet(c, s, d):
        pl.semaphore_signal(barrier, inc=1, device_id=place(c, s, d), device_id_type=MESH)

    upper = lax.rem(sec, 2) == 1

    @pl.when(jnp.logical_not(upper))
    def _():
        for c in range(2):
            greet(c, sec + 1, dp)

    def pieces(g):
        xc, bc, cc = group_columns(g)
        return (
            (conv_in.at[0, 0, :, pl.ds(xc, WIDE)], 0, WIDE),
            (conv_in.at[0, 0, :, pl.ds(bc, STATE)], WIDE, STATE),
            (conv_in.at[0, 0, :, pl.ds(cc, STATE)], WIDE + STATE, STATE),
            (gate_in.at[0, 0, :, pl.ds(xc, WIDE)], MIX, WIDE),
            (cot_in.at[0, 0, :, pl.ds(xc, WIDE)], MIX + WIDE, WIDE),
        )

    mine = pl.ds(pl.multiple_of(core * tok, tok), tok)
    theirs = pl.ds(pl.multiple_of(other * tok, tok), tok)
    def tell(sem, s, c=core):
        pl.semaphore_signal(sem, inc=1, device_id=place(c, s, dp), device_id_type=MESH)

    @pl.when(upper)
    def _():
        pl.semaphore_wait(barrier, 2)

    def landed(ref, sem):
        remote(ref, ref, sem, other, sec, dp).wait_recv()

    def sent(ref):
        remote(ref, ref, sent_sem, other, sec, dp).wait_send()

    def hand(src, dst, at):
        return remote(src, dst, ship_sem.at[at], 1, sec - 1, dp)

    def hand_over():
        for src, off, width in pieces(last):
            hand(src, uin.at[HALF, mine, pl.ds(off, width)], 0).start()
        hand(step_in.at[0, 0], steps.at[1, core], 1).start()

    def hand_params():
        xc, bc, cc = group_columns(last)
        for col, width in ((xc, WIDE), (bc, STATE), (cc, STATE)):
            cut = pl.ds(col, width)
            hand(w_in.at[:, :, cut], w_ref.at[pl.ds(1, 1), :, cut], 2).start()
            hand(b_in.at[:, cut], b_ref.at[1, :, cut], 3).start()
        cut = pl.ds(xc, WIDE)
        hand(ng_in.at[:, cut], ng_ref.at[1, :, cut], 4).start()
        hand(sb_in, sb_ref.at[1], 5).start()
        hand(dl_in, dl_ref.at[1], 5).start()
        hand(sk_in, sk_ref.at[1], 5).start()

    @pl.when(upper)
    def _():
        hand_over()
        for c in range(2):
            tell(pair_sem, sec - 1, c)

    @pl.when(sec == 1)
    def _():
        for c in range(2):
            greet(c, 2, dp)

    def later(j):
        return (j + HALF - 1) // HALF

    own_step = pltpu.make_async_copy(step_in.at[0, 0], steps.at[0, core], load_sem.at[0])
    own_step.start()

    def fetch(j, _):
        for src, off, width in pieces(core * HALF + j):
            pltpu.make_async_copy(
                src, uin.at[j, mine, pl.ds(off, width)], own_sem.at[later(j)]
            ).start()
        return 0

    fetch(0, 0)
    params = [
        pltpu.make_async_copy(src, dst, load_sem.at[at])
        for src, dst, at in (
            (sb_in, sb_ref.at[0], 1), (dl_in, dl_ref.at[0], 1), (sk_in, sk_ref.at[0], 1),
            (w_in, w_ref.at[pl.ds(0, 1)], 2), (b_in, b_ref.at[0], 3), (ng_in, ng_ref.at[0], 4),
        )
    ]
    for copy in params:
        copy.start()
    lax.fori_loop(1, own_groups, fetch, 0)
    upad[0:8, :] = jnp.zeros((8, MIX), F32)
    zpad[seq : seq + 8, :] = jnp.zeros((8, MIX), F32)
    for ref in (token_rows, ddt, drate, small, small_out):
        ref[...] = jnp.zeros_like(ref)

    @pl.when(sec == 2)
    def _():
        pl.semaphore_wait(barrier, 2)
        hand_over()

    @pl.when(jnp.logical_not(upper))
    def _():
        pl.semaphore_wait(pair_sem, 2)
        tell(mate_sem, sec + 1)

    @pl.when(upper)
    def _():
        pl.semaphore_wait(mate_sem, 1)

    remote(step_in.at[0, 0], steps.at[0, core], step_sem, other, sec, dp).start()

    def exchange(j, _):
        for src, off, width in pieces(other * HALF + j):
            remote(
                src, uin.at[j, mine, pl.ds(off, width)], xr_sem.at[later(j)], other, sec, dp
            ).start()
        return 0

    exchange(0, 0)

    @pl.when(sec == 2)
    def _():
        tell(plane_sem, 0)
        tell(plane_sem, 1)

    @pl.when(jnp.logical_and(sec > 0, core == 0))
    def _():
        hand_params()

    lax.fori_loop(1, HALF - other * gives, exchange, 0)
    own_step.wait()
    pltpu.make_async_copy(per_head.at[0], per_head.at[0], load_sem.at[1]).wait()
    for copy in params[3:]:
        copy.wait()

    def token_terms(which):
        diagonal = lax.broadcasted_iota(jnp.int32, (HEADS, HEADS), 0) == lax.broadcasted_iota(
            jnp.int32, (HEADS, HEADS), 1
        )

        def upright(ref):
            return jnp.sum(jnp.where(diagonal, ref[which], 0.0), axis=1, keepdims=True)

        raw = jnp.concatenate(
            [steps[which, 0].astype(F32), steps[which, 1].astype(F32)], axis=1
        )
        raw = raw + upright(sb_ref)
        delta = jnp.maximum(raw, 0.0) + jnp.log1p(jnp.exp(-jnp.abs(raw)))
        rate = delta * (-jnp.exp(upright(dl_ref)))
        rows2 = lax.broadcasted_iota(jnp.int32, (seq, seq), 0)
        cols2 = lax.broadcasted_iota(jnp.int32, (seq, seq), 1)
        ones_up = jnp.where(rows2 <= cols2, 1.0, 0.0).astype(BF16)
        r_hi, r_rest = rate.astype(BF16), rate - rate.astype(BF16).astype(F32)
        r_mid, r_lo = split(r_rest)
        cumulative = dot(r_hi, ones_up, NN) + (dot(r_mid, ones_up, NN) + dot(r_lo, ones_up, NN))
        for at, value in enumerate((delta, cumulative, jax.nn.sigmoid(raw), rate)):
            top = pl.multiple_of(which * halves_of + at * HEADS, HEADS)
            token_rows[pl.ds(top, HEADS), :] = value
        token_cols[...] = token_rows[...].T

    def group(turn, _):
        j = turn + (turn // (HALF - 1)) * donor
        helping = j // HALF
        g = core * HALF + j - helping
        ours = helping == 0
        slot_p = j + helping
        lane0 = helping * halves_of
        cols = group_columns(g)
        blocks = [(0, cols[0])]
        for base, col in ((WIDE, cols[1]), (WIDE + STATE, cols[2])):
            for part in range(STATE // 128):
                blocks.append((base + part * 128, pl.multiple_of(col + part * 128, 128)))

        def conv_rows(start, count, fresh):
            for off, col in blocks:
                here = slice(off, off + 128)
                if fresh:
                    upad[pl.ds(pl.multiple_of(start + 8, 8), count), here] = uin[
                        j, pl.ds(start, count), here
                    ].astype(F32)
                window = upad[pl.ds(start, count + 8), here]
                z = b_ref[helping, :, pl.ds(col, 128)]
                z = z + w_ref[helping, 3:4, pl.ds(col, 128)] * window[8:]
                for k in range(CONV - 1):
                    tap = w_ref[helping, pl.ds(k, 1), pl.ds(col, 128)]
                    z = z + tap * pltpu.roll(window, 3 - k, 0)[8:]
                s = jax.nn.sigmoid(z)
                mix[pl.ds(start, count), here] = z * s
                dsl[pl.ds(start, count), here] = s * (1.0 + z * (1.0 - s))

        def arrived(at, rows, done):
            @pl.when(j == 0)
            def _():
                done(uin.at[0, rows], at.at[0])

            for count, case in ((HALF - 1, 0), (HALF - 2, 1)):

                @pl.when(jnp.logical_and(j == 1, donor == case))
                def _():
                    done(uin.at[pl.ds(1, count), rows], at.at[1])

        arrived(own_sem, mine, lambda ref, sem: pltpu.make_async_copy(ref, ref, sem).wait())

        @pl.when(helping == 1)
        def _():
            some = pl.ds(0, WIDE + 2 * STATE)
            for at, ref in enumerate((
                uin.at[HALF], steps.at[1], w_ref.at[pl.ds(1, 1), :, some], b_ref.at[1, :, some],
                ng_ref.at[1, :, pl.ds(0, WIDE)], per_head.at[1],
            )):
                landed(ref, ship_sem.at[at])

        conv_rows(pl.multiple_of(core * tok, tok), tok, True)

        @pl.when(j == 0)
        def _():
            landed(steps.at[0, other], step_sem)

        @pl.when(jnp.logical_and(j == 0, sec == 1))
        def _():
            pl.semaphore_wait(plane_sem, 1)
            for k in range(1, ndp):
                greet(core, 0, lax.rem(dp + k, ndp))

        @pl.when(lax.rem(j, HALF) == 0)
        def _():
            token_terms(helping)

        arrived(xr_sem, theirs, landed)

        conv_rows(pl.multiple_of(other * tok, tok), tok, True)
        conv_rows(tok, 8, False)

        lane = lax.broadcasted_iota(jnp.int32, (seq, 128), 1)
        lane1 = lax.broadcasted_iota(jnp.int32, (1, 128), 1)
        lane16 = lax.broadcasted_iota(jnp.int32, (1, HEADS), 1)
        row = lax.broadcasted_iota(jnp.int32, (seq, seq), 0)
        column = lax.broadcasted_iota(jnp.int32, (seq, seq), 1)
        first = lane < HEAD_DIM

        def pick(at):
            return jnp.sum(
                jnp.where(lane == lane0 + at, token_cols[...], 0.0), axis=1, keepdims=True
            )

        def pick1(ref, h):
            return jnp.sum(jnp.where(lane16 == h, ref[helping], 0.0), axis=1, keepdims=True)

        x = mix[:, 0:WIDE]
        bmap = split(mix[:, WIDE : WIDE + STATE])
        cmap = split(mix[:, WIDE + STATE : MIX])
        h0 = g * REPS
        dt2 = jnp.where(first, pick(h0), pick(h0 + 1))
        skip2 = jnp.where(first[0:1], pick1(sk_ref, h0), pick1(sk_ref, h0 + 1))
        xs = x * dt2
        xs_p = split(xs)
        scores = dot3(cmap, bmap, NT)
        decay, mixed, ys = [], [], []
        for r in range(REPS):
            seg = pick(HEADS + h0 + r) - token_rows[pl.ds(lane0 + HEADS + h0 + r, 1), :]
            w = jnp.exp(jnp.where(row >= column, seg, -jnp.inf))
            a = scores * w
            a_p = split(a)
            decay.append(w)
            mixed.append((a, a_p))
            ys.append(dot3(a_p, xs_p, NN))
        y = jnp.where(first, ys[0], ys[1]) + skip2 * x
        gate = uin[j, :, MIX : MIX + WIDE].astype(F32)
        cot = uin[j, :, MIX + WIDE : MIX + 2 * WIDE].astype(F32)
        gain = ng_ref[helping, :, pl.ds(cols[0], WIDE)]
        s = jax.nn.sigmoid(gate)
        act = gate * s
        gated = y * act
        scale = lax.rsqrt(jnp.mean(gated * gated, axis=1, keepdims=True) + 1e-05)
        normed = gated * scale
        stage_o[j, :, 0:WIDE] = (normed * gain).astype(BF16)
        dn = cot * gain
        dgated = scale * (dn - normed * jnp.mean(dn * normed, axis=1, keepdims=True))
        dy = dgated * act
        stage_o[j, :, WIDE : 2 * WIDE] = (dgated * y * (s * (1.0 + gate * (1.0 - s)))).astype(BF16)

        even = lax.rem(j, 2) == 0
        out_cut = pl.ds(cols[0], WIDE)

        def send_half(base, t, dst, sem, s):
            remote(
                stage_o.at[j, pl.ds(t * tok, tok), pl.ds(base, WIDE)], dst, sem, t, s, dp
            ).start()

        direct = jnp.logical_and(
            ours, jnp.logical_and(sec < nsec - 1, jnp.logical_not(jnp.logical_and(sec == 1, even)))
        )

        @pl.when(direct)
        def _():
            for t in range(2):
                send_half(0, t, nxt.at[:, out_cut], land_sem, sec + 1)

        @pl.when(jnp.logical_and(ours, jnp.logical_and(sec == 1, even)))
        def _():
            slot = core * (HALF // 2) + j // 2
            for t in range(2):
                send_half(0, t, relay.at[slot], relay_sem, 3)

        @pl.when(jnp.logical_and(ours, jnp.logical_or(sec == 1, sec == 3)))
        def _():
            for t in range(2):
                send_half(
                    WIDE, t, ggate.at[:, out_cut], land_sem, sec - 1
                )

        @pl.when(jnp.logical_and(ours, sec == 2))
        def _():
            slot = core * HALF + j
            for t in range(2):
                send_half(WIDE, t, relay.at[slot], relay_sem, 0)

        @pl.when(helping == 1)
        def _():
            ggate[:, out_cut] = stage_o[j, tok : 2 * tok, WIDE : 2 * WIDE]
            send_half(WIDE, 0, ggate.at[:, out_cut], land_sem, sec)

        @pl.when(jnp.logical_and(helping == 1, sec < nsec - 2))
        def _():
            for t in range(2):
                send_half(0, t, nxt.at[:, out_cut], land_sem, sec + 2)

        partial[dp, slot_p, 6:8, :] = jnp.zeros((2, MIX), F32)
        partial[dp, slot_p, 5:6, WIDE:MIX] = jnp.zeros((1, MIX - WIDE), F32)
        partial[dp, slot_p, 5:6, 0:WIDE] = jnp.sum(cot * normed, axis=0, keepdims=True)
        dyx = jnp.sum(dy * x, axis=0, keepdims=True)
        dscore = jnp.zeros((seq, seq), F32)
        dy_p = split(dy)
        das = []
        for r in range(REPS):
            own = first if r == 0 else jnp.logical_not(first)
            da = dot3(split(jnp.where(own, dy, 0.0)), xs_p, NT)
            das.append(da)
            dscore = dscore + da * decay[r]
        ds_p = split(dscore)

        def conv_back(off, width, start):
            for part in range(width // 128):
                here = slice(off + part * 128, off + part * 128 + 128)
                col = pl.multiple_of(start + part * 128, 128)
                dz = zpad[0:seq, here]
                du = jnp.zeros((seq, 128), F32)
                for k in range(CONV):
                    du = du + (
                        w_ref[helping, pl.ds(k, 1), pl.ds(col, 128)]
                        * zpad[3 - k : 3 - k + seq, here]
                    )
                    partial[dp, slot_p, pl.ds(k, 1), here] = jnp.sum(
                        dz * upad[5 + k : 5 + k + seq, here], axis=0, keepdims=True
                    )
                partial[dp, slot_p, pl.ds(4, 1), here] = jnp.sum(dz, axis=0, keepdims=True)
                stage_c[j, :, here] = du.astype(BF16)

            @pl.when(helping == 1)
            def _():
                gconv[:, pl.ds(start, width)] = stage_c[j, tok : 2 * tok, off : off + width]
                remote(
                    stage_c.at[j, pl.ds(0, tok), pl.ds(off, width)],
                    gconv.at[:, pl.ds(start, width)],
                    land_sem, 0, sec, dp,
                ).start()

            @pl.when(jnp.logical_and(ours, sec > 0))
            def _():
                for t in range(2):
                    remote(
                        stage_c.at[j, pl.ds(t * tok, tok), pl.ds(off, width)],
                        gconv.at[:, pl.ds(start, width)],
                        land_sem, t, sec - 1, dp,
                    ).start()

        zpad[0:seq, WIDE + STATE : MIX] = dot3(ds_p, bmap, NN) * dsl[:, WIDE + STATE : MIX]
        conv_back(WIDE + STATE, STATE, cols[2])
        zpad[0:seq, WIDE : WIDE + STATE] = dot3(ds_p, cmap, TN) * dsl[:, WIDE : WIDE + STATE]
        conv_back(WIDE, STATE, cols[1])
        dxs = jnp.where(first, dot3(mixed[0][1], dy_p, TN), dot3(mixed[1][1], dy_p, TN))
        zpad[0:seq, 0:WIDE] = (skip2 * dy + dxs * dt2) * dsl[:, 0:WIDE]
        conv_back(0, WIDE, cols[0])
        upper = jnp.where(row <= column, 1.0, 0.0).astype(BF16)
        dxx = dxs * x
        for r in range(REPS):
            own = first if r == 0 else jnp.logical_not(first)
            p = split(das[r] * mixed[r][0])
            later = dot(upper, p[0], NN) + dot(upper, p[1], NN)
            dr = jnp.sum(jnp.where(row > column, later, 0.0), axis=1, keepdims=True)
            drate[...] += jnp.where(lane == lane0 + h0 + r, dr, 0.0)
            total = jnp.sum(jnp.where(own[0:1], dyx, 0.0), axis=1, keepdims=True)
            small[2:3, :] += jnp.where(lane1 == lane0 + h0 + r, total, 0.0)
            dd = jnp.sum(jnp.where(own, dxx, 0.0), axis=1, keepdims=True)
            ddt[...] += jnp.where(lane == lane0 + h0 + r, dd, 0.0)

        @pl.when(jnp.logical_and(j == 0, sec == 0))
        def _():
            pl.semaphore_wait(plane_sem, 1)
            pl.semaphore_wait(barrier, ndp - 1)
            for s in range(1, 4):
                pl.semaphore_signal(
                    world_sem, inc=1, device_id=place(core, s, dp), device_id_type=MESH
                )

        @pl.when(jnp.logical_and(j == 0, sec > 0))
        def _():
            pl.semaphore_wait(world_sem, 1)

        @pl.when(ours)
        def _():
            spread(j)

        @pl.when(helping == 1)
        def _():
            remote(
                partial.at[dp, HALF + 1], partial.at[dp, HALF - 1],
                hand_sem.at[0], core, sec + 1, dp,
            ).start()

        return 0

    def spread(slot):
        for k in range(1, ndp):
            to = lax.rem(dp + k, ndp)
            remote(
                partial.at[dp, slot], partial.at[dp, slot], sum_sem, core, sec, to
            ).start()

    lax.fori_loop(0, own_groups + helper, group, 0)

    def pass_on(slots, groups, out, sem, s):
        landed(relay.at[pl.ds(0, slots)], relay_sem)
        for slot, g in zip(range(slots), groups):
            remote(
                relay.at[slot], out.at[:, pl.ds(g * WIDE, WIDE)], sem, core, s, dp
            ).start()

    @pl.when(sec == 0)
    def _():
        pass_on(GROUPS - 1, range(GROUPS - 1), ggate, land_sem, 1)

    @pl.when(sec == 3)
    def _():
        pass_on(GROUPS // 2, range(0, GROUPS, 2), nxt, land_sem, 2)

    @pl.when(sec == 0)
    def _():
        nxt[...] = jnp.zeros_like(nxt)

    @pl.when(sec == nsec - 1)
    def _():
        gconv[...] = jnp.zeros_like(gconv)
        ggate[...] = jnp.zeros_like(ggate)
        gstep[...] = jnp.zeros_like(gstep)

    def step_terms(which, into):
        lane0 = which * halves_of
        heads = slice(lane0, lane0 + HEADS)
        dr16 = drate[:, heads]
        gate = token_cols[:, lane0 + 2 * HEADS : lane0 + 3 * HEADS]
        rate = token_cols[:, lane0 + 3 * HEADS : lane0 + 4 * HEADS]
        dstep = (ddt[:, heads] - dr16 * jnp.exp(dl_ref[which])) * gate
        into[0:1, 0:HEADS] = jnp.sum(dstep, axis=0, keepdims=True)
        into[1:2, 0:HEADS] = jnp.sum(dr16 * rate, axis=0, keepdims=True)
        drate[:, heads] = dstep

    step_terms(0, small)

    @pl.when(helper == 1)
    def _():
        step_terms(1, small_out)
        small_out[2:3, 0:HEADS] = small[2:3, halves_of : halves_of + HEADS]
        remote(
            small_out, small_in, hand_sem.at[1], core, sec + 1, dp
        ).start()

    turned = drate[...].T
    for t in range(2):
        for c in range(2):
            stage_s[t, c] = turned[c * 8 : c * 8 + 8, t * tok : (t + 1) * tok].astype(BF16)

    @pl.when(sec > 0)
    def _():
        for t in range(2):
            remote(
                stage_s.at[t, core], step_parts.at[0, core], dstep_sem, t, sec - 1, dp
            ).start()

    @pl.when(helper == 1)
    def _():
        for c in range(2):
            top = halves_of + c * 8
            stage_s[2, c] = turned[top : top + 8, 0:tok].astype(BF16)
            step_parts[1, c] = turned[top : top + 8, tok : 2 * tok].astype(BF16)
        remote(stage_s.at[2], step_parts.at[1], dstep_sem, other, sec, dp).start()

    @pl.when(donor == 1)
    def _():
        landed(partial.at[dp, HALF - 1], hand_sem.at[0])
        landed(small_in, hand_sem.at[1])
        spread(HALF - 1)
        small[...] += small_in[...]

    partial[dp, HALF] = jnp.zeros((8, MIX), F32)
    partial[dp, HALF, :, 0:128] = small[...]
    spread(HALF)
    landed(partial.at[pl.ds(0, ndp - 1), pl.ds(0, HALF + 1)], sum_sem)
    total = partial[0, 0 : HALF + 1]
    for k in range(1, ndp):
        total = total + partial[k, 0 : HALF + 1]
    final[core] = total
    remote(final.at[core], final.at[core], fin_sem, other, sec, dp).start()
    landed(final.at[other], fin_sem)
    for g in range(GROUPS):
        c, j = g // HALF, g % HALF
        table_out[5:6, g * WIDE : (g + 1) * WIDE] = final[c, j, 5:6, 0:WIDE]
        for off, width, col in (
            (0, WIDE, g * WIDE),
            (WIDE, STATE, INNER + g * STATE),
            (WIDE + STATE, STATE, INNER + (GROUPS + g) * STATE),
        ):
            table_out[0:CONV, col : col + width] = final[c, j, 0:CONV, off : off + width]
            table_out[CONV : CONV + 1, col : col + width] = final[c, j, CONV : CONV + 1, off : off + width]
    for at in range(3):
        heads_out[at] = final[0, HALF, at : at + 1, 0:HEADS] + final[1, HALF, at : at + 1, 0:HEADS]

    @pl.when(sec < nsec - 1)
    def _():
        @pl.when(core == 0)
        def _():
            landed(step_parts, dstep_sem)

        @pl.when(core == 1)
        def _():
            landed(step_parts.at[0], dstep_sem)

        for c in range(2):
            both = step_parts[0, c].astype(F32) + step_parts[1, c].astype(F32)
            gstep[c * 8 : c * 8 + 8, :] = both.astype(BF16)

    first = pl.ds(0, HALF - 1)
    half = pl.ds(0, WIDE)
    sent(steps.at[0, 0])
    sent(uin.at[first, pl.ds(0, tok)])
    sent(partial.at[pl.ds(0, ndp - 1), pl.ds(0, HALF + 1)])
    sent(final.at[0])

    @pl.when(other * gives == 0)
    def _():
        sent(uin.at[0, pl.ds(0, tok)])

    @pl.when(sec == 0)
    def _():
        sent(relay.at[pl.ds(0, GROUPS - 1)])

    @pl.when(sec == nsec - 1)
    def _():
        sent(relay.at[pl.ds(0, GROUPS // 2)])

    @pl.when(sec > 0)
    def _():
        sent(uin.at[HALF, pl.ds(0, tok)])
        sent(steps.at[1, 0])
        sent(stage_c.at[first])
        sent(stage_o.at[first, :, half])
        sent(stage_s.at[0])

    @pl.when(jnp.logical_and(sec > 0, core == 0))
    def _():
        some = pl.ds(0, WIDE + 2 * STATE)
        for ref in (
            w_ref.at[pl.ds(1, 1), :, some], b_ref.at[1, :, some], ng_ref.at[1, :, half],
            per_head.at[1], stage_c.at[HALF - 1], stage_o.at[HALF - 1, :, half],
        ):
            sent(ref)

    @pl.when(sec < nsec - 1)
    def _():
        sent(stage_o.at[first, :, half])

    @pl.when(jnp.logical_and(sec < nsec - 1, donor == 0))
    def _():
        sent(stage_o.at[HALF - 1, :, half])

    @pl.when(helper == 1)
    def _():
        sent(stage_c.at[HALF, pl.ds(0, tok)])
        sent(stage_o.at[HALF, pl.ds(0, tok), half])
        sent(stage_s.at[2])
        sent(partial.at[dp, HALF + 1])
        sent(small_out)

    @pl.when(jnp.logical_and(helper == 1, sec < nsec - 2))
    def _():
        sent(stage_o.at[HALF, :, half])

    whole, less = 6 * INNER, 6 * (INNER - WIDE)

    @pl.when(sec == nsec - 1)
    def _():
        landed(nxt, land_sem)

    for c, columns in ((0, whole), (1, less)):

        @pl.when(jnp.logical_and(sec == 0, core == c))
        def _():
            landed(rows_out.at[:, pl.ds(0, columns)], land_sem)

        @pl.when(jnp.logical_and(sec * (nsec - 1 - sec) > 0, core == c))
        def _():
            landed(rows_out.at[:, pl.ds(0, INNER + columns)], land_sem)


def finish_kernel(
    rows_in, table_in, heads_in, nxt, gconv, ggate, gstep, gtap, gcb, gsb, gdl, gsk, gng, sem
):
    tok = rows_in.shape[0]
    copies = [
        (rows_in.at[:, pl.ds(INNER, 5 * INNER)], gconv.at[0, 0]),
        (rows_in.at[:, pl.ds(0, INNER)], nxt.at[0, 0]),
        (rows_in.at[:, pl.ds(6 * INNER, INNER)], ggate.at[0, 0]),
        (table_in.at[pl.ds(0, CONV)], gtap.at[0]),
        (table_in.at[pl.ds(CONV, 1)], gcb),
        (table_in.at[pl.ds(CONV + 1, 1), pl.ds(0, INNER)], gng),
        (rows_in.at[pl.ds(0, HEADS), pl.ds(7 * INNER, tok)], gstep.at[0, 0]),
        (heads_in.at[0], gsb),
        (heads_in.at[1], gdl),
        (heads_in.at[2], gsk),
    ]
    copies = [pltpu.make_async_copy(a, b, sem.at[at]) for at, (a, b) in enumerate(copies)]
    for copy in copies:
        copy.start()
    for copy in copies:
        copy.wait()


def paired(
    conv_input, gate_input, step_input, cotangent, conv_weight,
    conv_bias, step_bias, decay_log, skip_gain, norm_gain,
):
    tok = conv_input.shape[2]
    seq = 2 * tok
    ndp = lax.axis_size("dp")
    hbm = pl.BlockSpec(memory_space=pl.ANY)
    vmem = pl.BlockSpec(memory_space=pltpu.VMEM)
    scratch = [
        pltpu.VMEM((2,) + conv_weight.shape[1:], F32),
        pltpu.VMEM((2,) + conv_bias.shape, F32),
        pltpu.VMEM((2, 3) + step_bias.shape, F32),
        pltpu.VMEM((2,) + norm_gain.shape, F32),
        pltpu.VMEM((HALF + 1, seq, MIX + 2 * WIDE), BF16),
        pltpu.VMEM((2, 2, HEADS, tok), BF16),
        pltpu.VMEM((128, seq), F32),
        pltpu.VMEM((seq, 128), F32),
        pltpu.VMEM((seq + 8, MIX), F32),
        pltpu.VMEM((seq + 8, MIX), F32),
        pltpu.VMEM((seq, MIX), F32),
        pltpu.VMEM((seq, MIX), F32),
        pltpu.VMEM((seq, 128), F32),
        pltpu.VMEM((seq, 128), F32),
        pltpu.VMEM((8, 128), F32),
        pltpu.VMEM((HALF + 1, seq, MIX), BF16),
        pltpu.VMEM((HALF + 1, seq, 2 * WIDE), BF16),
        pltpu.VMEM((3, 2, HEADS // 2, tok), BF16),
        pltpu.VMEM((2, 2, HEADS // 2, tok), BF16),
        pltpu.VMEM((ndp, HALF + 2, 8, MIX), F32),
        pltpu.VMEM((2, HALF + 1, 8, MIX), F32),
        pltpu.VMEM((GROUPS, tok, WIDE), BF16),
        pltpu.VMEM((8, 128), F32),
        pltpu.VMEM((8, 128), F32),
        pltpu.SemaphoreType.DMA((2,)),
        pltpu.SemaphoreType.DMA((2,)),
    ]
    one = pltpu.SemaphoreType.DMA
    scratch += [one, one, one((5,)), one, one((6,)), one, one, one, one((2,)), one]
    scratch += [pltpu.SemaphoreType.REGULAR] * 4
    turned = jnp.swapaxes(step_input, 2, 3)
    shapes = [
        (gate_input.shape, BF16),
        (conv_input.shape, BF16),
        (gate_input.shape, BF16),
        (turned.shape, BF16),
        (conv_weight.shape, F32),
        (conv_bias.shape, F32),
        (step_bias.shape, F32),
        (decay_log.shape, F32),
        (skip_gain.shape, F32),
        (norm_gain.shape, F32),
    ]
    inputs = [
        pltpu.with_memory_space_constraint(a, pltpu.HBM)
        for a in (
            conv_input, gate_input, turned, cotangent, conv_weight,
            conv_bias, step_bias, decay_log, skip_gain, norm_gain,
        )
    ]
    sent = pl.pallas_call(
        pair_kernel,
        name="mixer_tick",
        in_specs=[hbm] * 10,
        out_specs=[vmem] * 3,
        out_shape=[
            pltpu.VMEM((tok, 7 * INNER + tok), BF16),
            pltpu.VMEM((8, conv_bias.shape[1]), F32),
            pltpu.VMEM((3,) + step_bias.shape, F32),
        ],
        scratch_shapes=scratch,
        compiler_params=pltpu.CompilerParams(
            collective_id=0, has_side_effects=True, vmem_limit_bytes=24 * 1024 * 1024
        ),
    )(*inputs)
    done = pl.pallas_call(
        finish_kernel,
        name="mixer_finish",
        in_specs=[vmem] * 3,
        out_specs=[hbm] * 10,
        out_shape=[jax.ShapeDtypeStruct(shape, kind) for shape, kind in shapes],
        scratch_shapes=[pltpu.SemaphoreType.DMA((10,))],
        compiler_params=pltpu.CompilerParams(vmem_limit_bytes=1024 * 1024),
    )(*sent)
    return tuple(done[:3]) + (jnp.swapaxes(done[3], 2, 3),) + tuple(done[4:])


def solution(mesh):
    in_specs = (
        P("section", "dp", "ctx", None),
        P("section", "dp", "ctx", None),
        P("section", "dp", "ctx", None),
        P("section", "dp", "ctx", None),
        P("section", None, None),
        P("section", None),
        P("section", None),
        P("section", None),
        P("section", None),
        P("section", None),
    )
    out_specs = (
        P("section", "dp", "ctx", None),
        P("section", "dp", "ctx", None),
        P("section", "dp", "ctx", None),
        P("section", "dp", "ctx", None),
        P("section", None, None),
        P("section", None),
        P("section", None),
        P("section", None),
        P("section", None),
        P("section", None),
    )
    body = paired if (mesh.shape["ctx"], mesh.shape["section"]) == (2, 4) else shards
    return jax.shard_map(body, mesh=mesh, in_specs=in_specs, out_specs=out_specs, check_vma=False)
```

```python
import functools
import jax
import jax.numpy as jnp
from jax import lax
from jax.experimental import pallas as pl
from jax.experimental.pallas import tpu as pltpu
from jax.sharding import PartitionSpec as P

HEADS = 16
HEAD_DIM = 64
STATE = 256
GROUPS = 8
CONV = 4


HIGH_BOUND = lax.Precision.HIGHEST


def shifted(block, axis, distance):
    devices = range(lax.axis_size(axis))
    route = [(i - distance, i) for i in devices if i - distance in devices]
    return lax.ppermute(block, axis, route)


def prefix(part, axis, combine, identity):
    count = lax.axis_size(axis)
    place = lax.axis_index(axis)
    ahead = count - 1 - place
    gathered = jax.tree.map(lambda a: lax.all_gather(a, axis), part)
    state = jax.tree.map(lambda a, e: jnp.zeros_like(a) + jnp.asarray(e, a.dtype), part, identity)

    def one(turn, state):
        source = count - 1 - turn
        return combine(
            state, jax.tree.map(lambda a: lax.dynamic_index_in_dim(a, source, 0, False), gathered)
        )

    return lax.fori_loop(0, ahead, one, state)


def conv_mix(extended, taps, initial_offset):
    rows = extended.shape[0] - (CONV - 1)
    total = initial_offset[None, :]
    for tap in range(CONV):
        total = total + taps[tap][None, :] * extended[tap : tap + rows]
    return jax.nn.silu(total)


def split_mix(mixed, steps, step_shift, damping_exponents):
    rows = mixed.shape[0]
    inner = HEADS * HEAD_DIM
    payload_lines = mixed[:, :inner].reshape(rows, GROUPS, HEADS // GROUPS, HEAD_DIM)
    in_maps = mixed[:, inner : inner + GROUPS * STATE].reshape(rows, GROUPS, STATE)
    out_maps = mixed[:, inner + GROUPS * STATE :].reshape(rows, GROUPS, STATE)
    delta = jax.nn.softplus(steps + step_shift[None, :])
    upto = jnp.tril(jnp.ones((rows, rows), jnp.float32))
    rates = delta * (-jnp.exp(damping_exponents))[None, :]
    cumulative = jnp.dot(upto, rates, precision=HIGH_BOUND)
    return (payload_lines, in_maps, out_maps, delta, cumulative)


def fragment_condition(extended, steps, taps, initial_offset, step_shift, damping_exponents):
    payload_lines, in_maps, out_maps, delta, cumulative = split_mix(
        conv_mix(extended, taps, initial_offset), steps, step_shift, damping_exponents
    )
    rows = payload_lines.shape[0]
    total = cumulative[-1]
    weight = (jnp.exp(total[None, :] - cumulative) * delta).reshape(rows, GROUPS, HEADS // GROUPS)
    state = jnp.einsum(
        "tgrp,tgn->grpn", payload_lines * weight[..., None], in_maps, precision=HIGH_BOUND
    )
    return (state.reshape(HEADS, HEAD_DIM, STATE), total)


def shard_layer(
    extended,
    gates,
    steps,
    taps,
    initial_offset,
    step_shift,
    damping_exponents,
    skip_values,
    gain_values,
    carried,
):
    payload_lines, in_maps, out_maps, delta, cumulative = split_mix(
        conv_mix(extended, taps, initial_offset), steps, step_shift, damping_exponents
    )
    rows = payload_lines.shape[0]
    reps = HEADS // GROUPS
    lower = (jnp.arange(rows)[:, None] >= jnp.arange(rows)[None, :])[None]
    seg = cumulative.T[:, :, None] - cumulative.T[:, None, :]
    weight = jnp.exp(jnp.where(lower, seg, -jnp.inf)).reshape(GROUPS, reps, rows, rows)
    intersection_maps = jnp.einsum("tgn,sgn->gts", out_maps, in_maps, precision=HIGH_BOUND)
    score_matrix = weight * intersection_maps[:, None]
    scaled_values = payload_lines * delta.reshape(rows, GROUPS, reps)[..., None]
    final_output = jnp.einsum("jzlh,hjzc->ljzc", score_matrix, scaled_values, precision=HIGH_BOUND)
    incoming = jnp.einsum(
        "tgn,grpn->tgrp",
        out_maps,
        carried.reshape(GROUPS, reps, HEAD_DIM, STATE),
        precision=HIGH_BOUND,
    )
    final_output = (
        final_output + incoming * jnp.exp(cumulative).reshape(rows, GROUPS, reps)[..., None]
    )
    final_output = (
        final_output + skip_values.reshape(GROUPS, reps)[None, :, :, None] * payload_lines
    )
    gated = final_output.reshape(rows, GROUPS, -1) * jax.nn.silu(gates).reshape(rows, GROUPS, -1)
    normed = gated * lax.rsqrt(jnp.mean(gated * gated, axis=-1, keepdims=True) + 1e-05)
    return normed.reshape(rows, -1) * gain_values[None, :]


def combine(earlier, later):
    return (earlier[0] * later[0], later[0][:, None] * earlier[1] + later[1])


def shards(
    conv_input,
    gate_input,
    step_input,
    cotangent,
    conv_weight,
    conv_bias,
    step_bias,
    decay_log,
    skip_gain,
    norm_gain,
):
    local_rows = conv_input[0, 0]
    count = local_rows.shape[0]
    taps, initial_offset = (conv_weight[0], conv_bias[0])
    step_shift, damping_exponents = (step_bias[0], decay_log[0])
    skip_values, gain_values = (skip_gain[0], norm_gain[0])
    previous = shifted(local_rows[count - (CONV - 1) :], "ctx", 1)
    extended = jnp.concatenate([previous, local_rows], 0).astype(jnp.float32)
    gates = gate_input[0, 0].astype(jnp.float32)
    steps = step_input[0, 0].astype(jnp.float32)
    (state, total), state_pull = jax.vjp(
        fragment_condition, extended, steps, taps, initial_offset, step_shift, damping_exponents
    )
    decay = jnp.exp(total)
    flat_state = state.reshape(HEADS, HEAD_DIM * STATE)
    unity = (jnp.ones((HEADS,), jnp.float32), jnp.zeros((HEADS, HEAD_DIM * STATE), jnp.float32))

    def advance(index, current):
        return shifted(decay[:, None] * current + flat_state, "ctx", 1)

    incoming = lax.fori_loop(
        0, lax.axis_size("ctx") - 1, advance, jnp.zeros((HEADS, HEAD_DIM * STATE), jnp.float32)
    )
    carried = incoming.reshape(HEADS, HEAD_DIM, STATE)
    final_output, layer_pull = jax.vjp(
        shard_layer,
        extended,
        gates,
        steps,
        taps,
        initial_offset,
        step_shift,
        damping_exponents,
        skip_values,
        gain_values,
        carried,
    )
    forward = shifted(final_output.astype(jnp.bfloat16)[None, None], "section", 1)
    grads = layer_pull(cotangent[0, 0].astype(jnp.float32))
    carry_grad = grads[9].reshape(HEADS, HEAD_DIM * STATE)
    outgoing = prefix((decay, carry_grad), "ctx", combine, unity)[1]
    outgoing_grad = outgoing.reshape(HEADS, HEAD_DIM, STATE)
    total_grad = jnp.sum(outgoing_grad * carried, axis=(1, 2)) * decay
    extra = state_pull((outgoing_grad, total_grad))
    ext_grad = grads[0] + extra[0]
    step_grad = grads[2] + extra[1]
    param_terms = (
        grads[3] + extra[2],
        grads[4] + extra[3],
        grads[5] + extra[4],
        grads[6] + extra[5],
        grads[7],
        grads[8],
    )
    returned = shifted(ext_grad[: CONV - 1], "ctx", -1)
    own_grad = ext_grad[CONV - 1 :]
    row_grad = jnp.concatenate(
        [own_grad[: count - (CONV - 1)], own_grad[count - (CONV - 1) :] + returned], 0
    )
    backward = shifted(
        (
            row_grad.astype(jnp.bfloat16)[None, None],
            grads[1].astype(jnp.bfloat16)[None, None],
            step_grad.astype(jnp.bfloat16)[None, None],
        ),
        "section",
        -1,
    )
    summed = lax.psum(
        (
            param_terms[0],
            param_terms[1],
            param_terms[2],
            param_terms[3],
            param_terms[4],
            param_terms[5],
        ),
        ("ctx", "dp"),
    )
    return (
        forward,
        backward[0],
        backward[1],
        backward[2],
        summed[0][None],
        summed[1][None],
        summed[2][None],
        summed[3][None],
        summed[4][None],
        summed[5][None],
    )


MESH = pl.DeviceIdType.MESH
F32 = jnp.float32
BF16 = jnp.bfloat16
INNER = HEADS * HEAD_DIM
REPS = HEADS // GROUPS
WIDE = REPS * HEAD_DIM
MIX = WIDE + 2 * STATE
HALF = GROUPS // 2
NN = ((1,), (0,))
NT = ((1,), (1,))
TN = ((0,), (0,))


def split(a):
    high = a.astype(BF16)
    return high, (a - high.astype(F32)).astype(BF16)


def dot(a, b, dims):
    return lax.dot_general(a, b, (dims, ((), ())), preferred_element_type=F32)


def dot3(a, b, dims):
    return dot(a[0], b[0], dims) + (dot(a[0], b[1], dims) + dot(a[1], b[0], dims))


def group_columns(g):
    return (
        pl.multiple_of(g * WIDE, 128),
        pl.multiple_of(INNER + g * STATE, 128),
        pl.multiple_of(INNER + (GROUPS + g) * STATE, 128),
    )


def pair_kernel(
    conv_in, gate_in, step_in, cot_in, w_in, b_in, sb_in, dl_in, sk_in, ng_in,
    rows_out, table_out, heads_out,
    w_ref, b_ref, per_head, ng_ref,
    uin, steps, token_rows, token_cols, upad, zpad, mix, dsl, ddt, drate, small,
    stage_c, stage_o, stage_s, step_parts, partial, final, relay, small_out, small_in,
    own_sem, xr_sem, sent_sem, land_sem, load_sem, step_sem, ship_sem, relay_sem, dstep_sem,
    sum_sem, hand_sem, fin_sem, pair_sem, mate_sem, plane_sem, world_sem,
):
    core = lax.axis_index("ctx")
    sec = lax.axis_index("section")
    dp = lax.axis_index("dp")
    nsec = lax.axis_size("section")
    ndp = lax.axis_size("dp")
    tok = conv_in.shape[2]
    seq = 2 * tok
    other = 1 - core
    gives = (sec + nsec - 1) // nsec
    takes = 1 - sec // (nsec - 1)
    donor = core * gives
    helper = core * takes
    own_groups = HALF - donor
    last = GROUPS - 1
    halves_of = 4 * HEADS

    def place(c, s, d):
        return {"ctx": c, "section": s, "dp": d}

    def remote(src, dst, recv, c, s, d):
        return pltpu.make_async_remote_copy(
            src_ref=src, dst_ref=dst, send_sem=sent_sem, recv_sem=recv,
            device_id=place(c, s, d), device_id_type=MESH,
        )

    after = lax.rem(sec + 1, nsec)
    before = lax.rem(sec + nsec - 1, nsec)
    sb_ref, dl_ref, sk_ref = (per_head.at[:, at] for at in range(3))
    nxt = rows_out.at[:, pl.ds(0, INNER)]
    gconv = rows_out.at[:, pl.ds(INNER, 5 * INNER)]
    ggate = rows_out.at[:, pl.ds(6 * INNER, INNER)]
    gstep = rows_out.at[pl.ds(0, HEADS), pl.ds(7 * INNER, tok)]
    barrier = pltpu.get_barrier_semaphore()

    def greet(c, s, d):
        pl.semaphore_signal(barrier, inc=1, device_id=place(c, s, d), device_id_type=MESH)

    upper = lax.rem(sec, 2) == 1

    @pl.when(jnp.logical_not(upper))
    def _():
        for c in range(2):
            greet(c, sec + 1, dp)

    def pieces(g):
        xc, bc, cc = group_columns(g)
        return (
            (conv_in.at[0, 0, :, pl.ds(xc, WIDE)], 0, WIDE),
            (conv_in.at[0, 0, :, pl.ds(bc, STATE)], WIDE, STATE),
            (conv_in.at[0, 0, :, pl.ds(cc, STATE)], WIDE + STATE, STATE),
            (gate_in.at[0, 0, :, pl.ds(xc, WIDE)], MIX, WIDE),
            (cot_in.at[0, 0, :, pl.ds(xc, WIDE)], MIX + WIDE, WIDE),
        )

    mine = pl.ds(pl.multiple_of(core * tok, tok), tok)
    theirs = pl.ds(pl.multiple_of(other * tok, tok), tok)
    def tell(sem, s, c=core):
        pl.semaphore_signal(sem, inc=1, device_id=place(c, s, dp), device_id_type=MESH)

    @pl.when(upper)
    def _():
        pl.semaphore_wait(barrier, 2)

    def landed(ref, sem):
        remote(ref, ref, sem, other, sec, dp).wait_recv()

    def sent(ref):
        remote(ref, ref, sent_sem, other, sec, dp).wait_send()

    def hand(src, dst, at):
        return remote(src, dst, ship_sem.at[at], 1, sec - 1, dp)

    def hand_over():
        for src, off, width in pieces(last):
            hand(src, uin.at[HALF, mine, pl.ds(off, width)], 0).start()
        hand(step_in.at[0, 0], steps.at[1, core], 1).start()

    def hand_params():
        xc, bc, cc = group_columns(last)
        for col, width in ((xc, WIDE), (bc, STATE), (cc, STATE)):
            cut = pl.ds(col, width)
            hand(w_in.at[:, :, cut], w_ref.at[pl.ds(1, 1), :, cut], 2).start()
            hand(b_in.at[:, cut], b_ref.at[1, :, cut], 3).start()
        cut = pl.ds(xc, WIDE)
        hand(ng_in.at[:, cut], ng_ref.at[1, :, cut], 4).start()
        hand(sb_in, sb_ref.at[1], 5).start()
        hand(dl_in, dl_ref.at[1], 5).start()
        hand(sk_in, sk_ref.at[1], 5).start()

    @pl.when(upper)
    def _():
        hand_over()
        for c in range(2):
            tell(pair_sem, sec - 1, c)

    @pl.when(sec == 1)
    def _():
        for c in range(2):
            greet(c, 2, dp)

    def later(j):
        return (j + HALF - 1) // HALF

    own_step = pltpu.make_async_copy(step_in.at[0, 0], steps.at[0, core], load_sem.at[0])
    own_step.start()

    def fetch(j, _):
        for src, off, width in pieces(core * HALF + j):
            pltpu.make_async_copy(
                src, uin.at[j, mine, pl.ds(off, width)], own_sem.at[later(j)]
            ).start()
        return 0

    fetch(0, 0)
    params = [
        pltpu.make_async_copy(src, dst, load_sem.at[at])
        for src, dst, at in (
            (sb_in, sb_ref.at[0], 1), (dl_in, dl_ref.at[0], 1), (sk_in, sk_ref.at[0], 1),
            (w_in, w_ref.at[pl.ds(0, 1)], 2), (b_in, b_ref.at[0], 3), (ng_in, ng_ref.at[0], 4),
        )
    ]
    for copy in params:
        copy.start()
    lax.fori_loop(1, own_groups, fetch, 0)
    upad[0:8, :] = jnp.zeros((8, MIX), F32)
    zpad[seq : seq + 8, :] = jnp.zeros((8, MIX), F32)
    for ref in (token_rows, ddt, drate, small, small_out):
        ref[...] = jnp.zeros_like(ref)

    @pl.when(sec == 2)
    def _():
        pl.semaphore_wait(barrier, 2)
        hand_over()

    @pl.when(jnp.logical_not(upper))
    def _():
        pl.semaphore_wait(pair_sem, 2)
        tell(mate_sem, sec + 1)

    @pl.when(upper)
    def _():
        pl.semaphore_wait(mate_sem, 1)

    remote(step_in.at[0, 0], steps.at[0, core], step_sem, other, sec, dp).start()

    def exchange(j, _):
        for src, off, width in pieces(other * HALF + j):
            remote(
                src, uin.at[j, mine, pl.ds(off, width)], xr_sem.at[later(j)], other, sec, dp
            ).start()
        return 0

    exchange(0, 0)

    @pl.when(sec == 2)
    def _():
        tell(plane_sem, 0)
        tell(plane_sem, 1)

    @pl.when(jnp.logical_and(sec > 0, core == 0))
    def _():
        hand_params()

    lax.fori_loop(1, HALF - other * gives, exchange, 0)
    own_step.wait()
    pltpu.make_async_copy(per_head.at[0], per_head.at[0], load_sem.at[1]).wait()
    for copy in params[3:]:
        copy.wait()

    def token_terms(which):
        diagonal = lax.broadcasted_iota(jnp.int32, (HEADS, HEADS), 0) == lax.broadcasted_iota(
            jnp.int32, (HEADS, HEADS), 1
        )

        def upright(ref):
            return jnp.sum(jnp.where(diagonal, ref[which], 0.0), axis=1, keepdims=True)

        raw = jnp.concatenate(
            [steps[which, 0].astype(F32), steps[which, 1].astype(F32)], axis=1
        )
        raw = raw + upright(sb_ref)
        delta = jnp.maximum(raw, 0.0) + jnp.log1p(jnp.exp(-jnp.abs(raw)))
        rate = delta * (-jnp.exp(upright(dl_ref)))
        rows2 = lax.broadcasted_iota(jnp.int32, (seq, seq), 0)
        cols2 = lax.broadcasted_iota(jnp.int32, (seq, seq), 1)
        ones_up = jnp.where(rows2 <= cols2, 1.0, 0.0).astype(BF16)
        r_hi, r_rest = rate.astype(BF16), rate - rate.astype(BF16).astype(F32)
        r_mid, r_lo = split(r_rest)
        cumulative = dot(r_hi, ones_up, NN) + (dot(r_mid, ones_up, NN) + dot(r_lo, ones_up, NN))
        for at, value in enumerate((delta, cumulative, jax.nn.sigmoid(raw), rate)):
            top = pl.multiple_of(which * halves_of + at * HEADS, HEADS)
            token_rows[pl.ds(top, HEADS), :] = value
        token_cols[...] = token_rows[...].T

    def group(turn, _):
        j = turn + (turn // (HALF - 1)) * donor
        helping = j // HALF
        g = core * HALF + j - helping
        ours = helping == 0
        slot_p = j + helping
        lane0 = helping * halves_of
        cols = group_columns(g)
        blocks = [(0, cols[0])]
        for base, col in ((WIDE, cols[1]), (WIDE + STATE, cols[2])):
            for part in range(STATE // 128):
                blocks.append((base + part * 128, pl.multiple_of(col + part * 128, 128)))

        def conv_rows(start, count, fresh):
            for off, col in blocks:
                here = slice(off, off + 128)
                if fresh:
                    upad[pl.ds(pl.multiple_of(start + 8, 8), count), here] = uin[
                        j, pl.ds(start, count), here
                    ].astype(F32)
                window = upad[pl.ds(start, count + 8), here]
                z = b_ref[helping, :, pl.ds(col, 128)]
                z = z + w_ref[helping, 3:4, pl.ds(col, 128)] * window[8:]
                for k in range(CONV - 1):
                    tap = w_ref[helping, pl.ds(k, 1), pl.ds(col, 128)]
                    z = z + tap * pltpu.roll(window, 3 - k, 0)[8:]
                s = jax.nn.sigmoid(z)
                mix[pl.ds(start, count), here] = z * s
                dsl[pl.ds(start, count), here] = s * (1.0 + z * (1.0 - s))

        def arrived(at, rows, done):
            @pl.when(j == 0)
            def _():
                done(uin.at[0, rows], at.at[0])

            for count, case in ((HALF - 1, 0), (HALF - 2, 1)):

                @pl.when(jnp.logical_and(j == 1, donor == case))
                def _():
                    done(uin.at[pl.ds(1, count), rows], at.at[1])

        arrived(own_sem, mine, lambda ref, sem: pltpu.make_async_copy(ref, ref, sem).wait())

        @pl.when(helping == 1)
        def _():
            some = pl.ds(0, WIDE + 2 * STATE)
            for at, ref in enumerate((
                uin.at[HALF], steps.at[1], w_ref.at[pl.ds(1, 1), :, some], b_ref.at[1, :, some],
                ng_ref.at[1, :, pl.ds(0, WIDE)], per_head.at[1],
            )):
                landed(ref, ship_sem.at[at])

        conv_rows(pl.multiple_of(core * tok, tok), tok, True)

        @pl.when(j == 0)
        def _():
            landed(steps.at[0, other], step_sem)

        @pl.when(jnp.logical_and(j == 0, sec == 1))
        def _():
            pl.semaphore_wait(plane_sem, 1)
            for k in range(1, ndp):
                greet(core, 0, lax.rem(dp + k, ndp))

        @pl.when(lax.rem(j, HALF) == 0)
        def _():
            token_terms(helping)

        arrived(xr_sem, theirs, landed)

        conv_rows(pl.multiple_of(other * tok, tok), tok, True)
        conv_rows(tok, 8, False)

        lane = lax.broadcasted_iota(jnp.int32, (seq, 128), 1)
        lane1 = lax.broadcasted_iota(jnp.int32, (1, 128), 1)
        lane16 = lax.broadcasted_iota(jnp.int32, (1, HEADS), 1)
        row = lax.broadcasted_iota(jnp.int32, (seq, seq), 0)
        column = lax.broadcasted_iota(jnp.int32, (seq, seq), 1)
        first = lane < HEAD_DIM

        def pick(at):
            return jnp.sum(
                jnp.where(lane == lane0 + at, token_cols[...], 0.0), axis=1, keepdims=True
            )

        def pick1(ref, h):
            return jnp.sum(jnp.where(lane16 == h, ref[helping], 0.0), axis=1, keepdims=True)

        x = mix[:, 0:WIDE]
        bmap = split(mix[:, WIDE : WIDE + STATE])
        cmap = split(mix[:, WIDE + STATE : MIX])
        h0 = g * REPS
        dt2 = jnp.where(first, pick(h0), pick(h0 + 1))
        skip2 = jnp.where(first[0:1], pick1(sk_ref, h0), pick1(sk_ref, h0 + 1))
        xs = x * dt2
        xs_p = split(xs)
        scores = dot3(cmap, bmap, NT)
        decay, mixed, ys = [], [], []
        for r in range(REPS):
            seg = pick(HEADS + h0 + r) - token_rows[pl.ds(lane0 + HEADS + h0 + r, 1), :]
            w = jnp.exp(jnp.where(row >= column, seg, -jnp.inf))
            a = scores * w
            a_p = split(a)
            decay.append(w)
            mixed.append((a, a_p))
            ys.append(dot3(a_p, xs_p, NN))
        y = jnp.where(first, ys[0], ys[1]) + skip2 * x
        gate = uin[j, :, MIX : MIX + WIDE].astype(F32)
        cot = uin[j, :, MIX + WIDE : MIX + 2 * WIDE].astype(F32)
        gain = ng_ref[helping, :, pl.ds(cols[0], WIDE)]
        s = jax.nn.sigmoid(gate)
        act = gate * s
        gated = y * act
        scale = lax.rsqrt(jnp.mean(gated * gated, axis=1, keepdims=True) + 1e-05)
        normed = gated * scale
        stage_o[j, :, 0:WIDE] = (normed * gain).astype(BF16)
        dn = cot * gain
        dgated = scale * (dn - normed * jnp.mean(dn * normed, axis=1, keepdims=True))
        dy = dgated * act
        stage_o[j, :, WIDE : 2 * WIDE] = (dgated * y * (s * (1.0 + gate * (1.0 - s)))).astype(BF16)

        even = lax.rem(j, 2) == 0
        out_cut = pl.ds(cols[0], WIDE)

        def send_half(base, t, dst, sem, s):
            remote(
                stage_o.at[j, pl.ds(t * tok, tok), pl.ds(base, WIDE)], dst, sem, t, s, dp
            ).start()

        direct = jnp.logical_and(
            ours, jnp.logical_and(sec < nsec - 1, jnp.logical_not(jnp.logical_and(sec == 1, even)))
        )

        @pl.when(direct)
        def _():
            for t in range(2):
                send_half(0, t, nxt.at[:, out_cut], land_sem, sec + 1)

        @pl.when(jnp.logical_and(ours, jnp.logical_and(sec == 1, even)))
        def _():
            slot = core * (HALF // 2) + j // 2
            send_half(0, 0, relay.at[slot], relay_sem, 3)

            @pl.when(core + j > 0)
            def _():
                send_half(0, 1, relay.at[slot], relay_sem, 3)

            @pl.when(core + j == 0)
            def _():
                send_half(0, 1, nxt.at[:, out_cut], land_sem, 2)

        @pl.when(jnp.logical_and(ours, jnp.logical_or(sec == 1, sec == 3)))
        def _():
            for t in range(2):
                send_half(
                    WIDE, t, ggate.at[:, out_cut], land_sem, sec - 1
                )

        @pl.when(jnp.logical_and(ours, sec == 2))
        def _():
            slot = core * HALF + j
            for t in range(2):
                send_half(WIDE, t, relay.at[slot], relay_sem, 0)

        @pl.when(helping == 1)
        def _():
            ggate[:, out_cut] = stage_o[j, tok : 2 * tok, WIDE : 2 * WIDE]
            send_half(WIDE, 0, ggate.at[:, out_cut], land_sem, sec)

        @pl.when(jnp.logical_and(helping == 1, sec < nsec - 2))
        def _():
            for t in range(2):
                send_half(0, t, nxt.at[:, out_cut], land_sem, sec + 2)

        partial[dp, slot_p, 6:8, :] = jnp.zeros((2, MIX), F32)
        partial[dp, slot_p, 5:6, WIDE:MIX] = jnp.zeros((1, MIX - WIDE), F32)
        partial[dp, slot_p, 5:6, 0:WIDE] = jnp.sum(cot * normed, axis=0, keepdims=True)
        dyx = jnp.sum(dy * x, axis=0, keepdims=True)
        dscore = jnp.zeros((seq, seq), F32)
        dy_p = split(dy)
        das = []
        for r in range(REPS):
            own = first if r == 0 else jnp.logical_not(first)
            da = dot3(split(jnp.where(own, dy, 0.0)), xs_p, NT)
            das.append(da)
            dscore = dscore + da * decay[r]
        ds_p = split(dscore)

        def conv_back(off, width, start):
            for part in range(width // 128):
                here = slice(off + part * 128, off + part * 128 + 128)
                col = pl.multiple_of(start + part * 128, 128)
                dz = zpad[0:seq, here]
                du = jnp.zeros((seq, 128), F32)
                for k in range(CONV):
                    du = du + (
                        w_ref[helping, pl.ds(k, 1), pl.ds(col, 128)]
                        * zpad[3 - k : 3 - k + seq, here]
                    )
                    partial[dp, slot_p, pl.ds(k, 1), here] = jnp.sum(
                        dz * upad[5 + k : 5 + k + seq, here], axis=0, keepdims=True
                    )
                partial[dp, slot_p, pl.ds(4, 1), here] = jnp.sum(dz, axis=0, keepdims=True)
                stage_c[j, :, here] = du.astype(BF16)

            @pl.when(helping == 1)
            def _():
                gconv[:, pl.ds(start, width)] = stage_c[j, tok : 2 * tok, off : off + width]
                remote(
                    stage_c.at[j, pl.ds(0, tok), pl.ds(off, width)],
                    gconv.at[:, pl.ds(start, width)],
                    land_sem, 0, sec, dp,
                ).start()

            @pl.when(jnp.logical_and(ours, sec > 0))
            def _():
                for t in range(2):
                    remote(
                        stage_c.at[j, pl.ds(t * tok, tok), pl.ds(off, width)],
                        gconv.at[:, pl.ds(start, width)],
                        land_sem, t, sec - 1, dp,
                    ).start()

        zpad[0:seq, WIDE + STATE : MIX] = dot3(ds_p, bmap, NN) * dsl[:, WIDE + STATE : MIX]
        conv_back(WIDE + STATE, STATE, cols[2])
        zpad[0:seq, WIDE : WIDE + STATE] = dot3(ds_p, cmap, TN) * dsl[:, WIDE : WIDE + STATE]
        conv_back(WIDE, STATE, cols[1])
        dxs = jnp.where(first, dot3(mixed[0][1], dy_p, TN), dot3(mixed[1][1], dy_p, TN))
        zpad[0:seq, 0:WIDE] = (skip2 * dy + dxs * dt2) * dsl[:, 0:WIDE]
        conv_back(0, WIDE, cols[0])
        upper = jnp.where(row <= column, 1.0, 0.0).astype(BF16)
        dxx = dxs * x
        for r in range(REPS):
            own = first if r == 0 else jnp.logical_not(first)
            p = split(das[r] * mixed[r][0])
            later = dot(upper, p[0], NN) + dot(upper, p[1], NN)
            dr = jnp.sum(jnp.where(row > column, later, 0.0), axis=1, keepdims=True)
            drate[...] += jnp.where(lane == lane0 + h0 + r, dr, 0.0)
            total = jnp.sum(jnp.where(own[0:1], dyx, 0.0), axis=1, keepdims=True)
            small[2:3, :] += jnp.where(lane1 == lane0 + h0 + r, total, 0.0)
            dd = jnp.sum(jnp.where(own, dxx, 0.0), axis=1, keepdims=True)
            ddt[...] += jnp.where(lane == lane0 + h0 + r, dd, 0.0)

        @pl.when(jnp.logical_and(j == 0, sec == 0))
        def _():
            pl.semaphore_wait(plane_sem, 1)
            pl.semaphore_wait(barrier, ndp - 1)
            for s in range(1, 4):
                pl.semaphore_signal(
                    world_sem, inc=1, device_id=place(core, s, dp), device_id_type=MESH
                )

        @pl.when(jnp.logical_and(j == 0, sec > 0))
        def _():
            pl.semaphore_wait(world_sem, 1)

        @pl.when(ours)
        def _():
            spread(j)

        @pl.when(helping == 1)
        def _():
            remote(
                partial.at[dp, HALF + 1], partial.at[dp, HALF - 1],
                hand_sem.at[0], core, sec + 1, dp,
            ).start()

        return 0

    def spread(slot):
        for k in range(1, ndp):
            to = lax.rem(dp + k, ndp)
            remote(
                partial.at[dp, slot], partial.at[dp, slot], sum_sem, core, sec, to
            ).start()

    lax.fori_loop(0, own_groups + helper, group, 0)

    def pass_on(slots, groups, out, sem, s):
        landed(relay.at[pl.ds(slots[0], len(slots))], relay_sem)
        for slot, g in zip(slots, groups):
            remote(
                relay.at[slot], out.at[:, pl.ds(g * WIDE, WIDE)], sem, core, s, dp
            ).start()

    @pl.when(sec == 0)
    def _():
        pass_on(range(GROUPS - 1), range(GROUPS - 1), ggate, land_sem, 1)

    for c in range(2):

        @pl.when(jnp.logical_and(sec == 3, core == c))
        def _():
            pass_on(range(c, GROUPS // 2), range(2 * c, GROUPS, 2), nxt, land_sem, 2)

    @pl.when(sec == 0)
    def _():
        nxt[...] = jnp.zeros_like(nxt)

    @pl.when(sec == nsec - 1)
    def _():
        gconv[...] = jnp.zeros_like(gconv)
        ggate[...] = jnp.zeros_like(ggate)
        gstep[...] = jnp.zeros_like(gstep)

    def step_terms(which, into):
        lane0 = which * halves_of
        heads = slice(lane0, lane0 + HEADS)
        dr16 = drate[:, heads]
        gate = token_cols[:, lane0 + 2 * HEADS : lane0 + 3 * HEADS]
        rate = token_cols[:, lane0 + 3 * HEADS : lane0 + 4 * HEADS]
        dstep = (ddt[:, heads] - dr16 * jnp.exp(dl_ref[which])) * gate
        into[0:1, 0:HEADS] = jnp.sum(dstep, axis=0, keepdims=True)
        into[1:2, 0:HEADS] = jnp.sum(dr16 * rate, axis=0, keepdims=True)
        drate[:, heads] = dstep

    step_terms(0, small)

    @pl.when(helper == 1)
    def _():
        step_terms(1, small_out)
        small_out[2:3, 0:HEADS] = small[2:3, halves_of : halves_of + HEADS]
        remote(
            small_out, small_in, hand_sem.at[1], core, sec + 1, dp
        ).start()

    turned = drate[...].T
    for t in range(2):
        for c in range(2):
            stage_s[t, c] = turned[c * 8 : c * 8 + 8, t * tok : (t + 1) * tok].astype(BF16)

    @pl.when(sec > 0)
    def _():
        for t in range(2):
            remote(
                stage_s.at[t, core], step_parts.at[0, core], dstep_sem, t, sec - 1, dp
            ).start()

    @pl.when(helper == 1)
    def _():
        for c in range(2):
            top = halves_of + c * 8
            stage_s[2, c] = turned[top : top + 8, 0:tok].astype(BF16)
            step_parts[1, c] = turned[top : top + 8, tok : 2 * tok].astype(BF16)
        remote(stage_s.at[2], step_parts.at[1], dstep_sem, other, sec, dp).start()

    @pl.when(donor == 1)
    def _():
        landed(partial.at[dp, HALF - 1], hand_sem.at[0])
        landed(small_in, hand_sem.at[1])
        spread(HALF - 1)
        small[...] += small_in[...]

    partial[dp, HALF] = jnp.zeros((8, MIX), F32)
    partial[dp, HALF, :, 0:128] = small[...]
    spread(HALF)
    landed(partial.at[pl.ds(0, ndp - 1), pl.ds(0, HALF + 1)], sum_sem)
    total = partial[0, 0 : HALF + 1]
    for k in range(1, ndp):
        total = total + partial[k, 0 : HALF + 1]
    final[core] = total
    remote(final.at[core], final.at[core], fin_sem, other, sec, dp).start()
    landed(final.at[other], fin_sem)
    for g in range(GROUPS):
        c, j = g // HALF, g % HALF
        table_out[5:6, g * WIDE : (g + 1) * WIDE] = final[c, j, 5:6, 0:WIDE]
        for off, width, col in (
            (0, WIDE, g * WIDE),
            (WIDE, STATE, INNER + g * STATE),
            (WIDE + STATE, STATE, INNER + (GROUPS + g) * STATE),
        ):
            table_out[0:CONV, col : col + width] = final[c, j, 0:CONV, off : off + width]
            table_out[CONV : CONV + 1, col : col + width] = final[c, j, CONV : CONV + 1, off : off + width]
    for at in range(3):
        heads_out[at] = final[0, HALF, at : at + 1, 0:HEADS] + final[1, HALF, at : at + 1, 0:HEADS]

    @pl.when(sec < nsec - 1)
    def _():
        @pl.when(core == 0)
        def _():
            landed(step_parts, dstep_sem)

        @pl.when(core == 1)
        def _():
            landed(step_parts.at[0], dstep_sem)

        for c in range(2):
            both = step_parts[0, c].astype(F32) + step_parts[1, c].astype(F32)
            gstep[c * 8 : c * 8 + 8, :] = both.astype(BF16)

    first = pl.ds(0, HALF - 1)
    half = pl.ds(0, WIDE)
    sent(steps.at[0, 0])
    sent(uin.at[first, pl.ds(0, tok)])
    sent(partial.at[pl.ds(0, ndp - 1), pl.ds(0, HALF + 1)])
    sent(final.at[0])

    @pl.when(other * gives == 0)
    def _():
        sent(uin.at[0, pl.ds(0, tok)])

    @pl.when(sec == 0)
    def _():
        sent(relay.at[pl.ds(0, GROUPS - 1)])

    for c in range(2):

        @pl.when(jnp.logical_and(sec == nsec - 1, core == c))
        def _():
            sent(relay.at[pl.ds(c, GROUPS // 2 - c)])

    @pl.when(sec > 0)
    def _():
        sent(uin.at[HALF, pl.ds(0, tok)])
        sent(steps.at[1, 0])
        sent(stage_c.at[first])
        sent(stage_o.at[first, :, half])
        sent(stage_s.at[0])

    @pl.when(jnp.logical_and(sec > 0, core == 0))
    def _():
        some = pl.ds(0, WIDE + 2 * STATE)
        for ref in (
            w_ref.at[pl.ds(1, 1), :, some], b_ref.at[1, :, some], ng_ref.at[1, :, half],
            per_head.at[1], stage_c.at[HALF - 1], stage_o.at[HALF - 1, :, half],
        ):
            sent(ref)

    @pl.when(sec < nsec - 1)
    def _():
        sent(stage_o.at[first, :, half])

    @pl.when(jnp.logical_and(sec < nsec - 1, donor == 0))
    def _():
        sent(stage_o.at[HALF - 1, :, half])

    @pl.when(helper == 1)
    def _():
        sent(stage_c.at[HALF, pl.ds(0, tok)])
        sent(stage_o.at[HALF, pl.ds(0, tok), half])
        sent(stage_s.at[2])
        sent(partial.at[dp, HALF + 1])
        sent(small_out)

    @pl.when(jnp.logical_and(helper == 1, sec < nsec - 2))
    def _():
        sent(stage_o.at[HALF, :, half])

    whole, less = 6 * INNER, 6 * (INNER - WIDE)

    @pl.when(sec == nsec - 1)
    def _():
        landed(nxt, land_sem)

    for c, columns in ((0, whole), (1, less)):

        @pl.when(jnp.logical_and(sec == 0, core == c))
        def _():
            landed(rows_out.at[:, pl.ds(0, columns)], land_sem)

        @pl.when(jnp.logical_and(sec * (nsec - 1 - sec) > 0, core == c))
        def _():
            landed(rows_out.at[:, pl.ds(0, INNER + columns)], land_sem)


def finish_kernel(
    rows_in, table_in, heads_in, nxt, gconv, ggate, gstep, gtap, gcb, gsb, gdl, gsk, gng, sem
):
    tok = rows_in.shape[0]
    copies = [
        (rows_in.at[:, pl.ds(INNER, 5 * INNER)], gconv.at[0, 0]),
        (rows_in.at[:, pl.ds(0, INNER)], nxt.at[0, 0]),
        (rows_in.at[:, pl.ds(6 * INNER, INNER)], ggate.at[0, 0]),
        (table_in.at[pl.ds(0, CONV)], gtap.at[0]),
        (table_in.at[pl.ds(CONV, 1)], gcb),
        (table_in.at[pl.ds(CONV + 1, 1), pl.ds(0, INNER)], gng),
        (rows_in.at[pl.ds(0, HEADS), pl.ds(7 * INNER, tok)], gstep.at[0, 0]),
        (heads_in.at[0], gsb),
        (heads_in.at[1], gdl),
        (heads_in.at[2], gsk),
    ]
    copies = [pltpu.make_async_copy(a, b, sem.at[at]) for at, (a, b) in enumerate(copies)]
    for copy in copies:
        copy.start()
    for copy in copies:
        copy.wait()


def paired(
    conv_input, gate_input, step_input, cotangent, conv_weight,
    conv_bias, step_bias, decay_log, skip_gain, norm_gain,
):
    tok = conv_input.shape[2]
    seq = 2 * tok
    ndp = lax.axis_size("dp")
    hbm = pl.BlockSpec(memory_space=pl.ANY)
    vmem = pl.BlockSpec(memory_space=pltpu.VMEM)
    scratch = [
        pltpu.VMEM((2,) + conv_weight.shape[1:], F32),
        pltpu.VMEM((2,) + conv_bias.shape, F32),
        pltpu.VMEM((2, 3) + step_bias.shape, F32),
        pltpu.VMEM((2,) + norm_gain.shape, F32),
        pltpu.VMEM((HALF + 1, seq, MIX + 2 * WIDE), BF16),
        pltpu.VMEM((2, 2, HEADS, tok), BF16),
        pltpu.VMEM((128, seq), F32),
        pltpu.VMEM((seq, 128), F32),
        pltpu.VMEM((seq + 8, MIX), F32),
        pltpu.VMEM((seq + 8, MIX), F32),
        pltpu.VMEM((seq, MIX), F32),
        pltpu.VMEM((seq, MIX), F32),
        pltpu.VMEM((seq, 128), F32),
        pltpu.VMEM((seq, 128), F32),
        pltpu.VMEM((8, 128), F32),
        pltpu.VMEM((HALF + 1, seq, MIX), BF16),
        pltpu.VMEM((HALF + 1, seq, 2 * WIDE), BF16),
        pltpu.VMEM((3, 2, HEADS // 2, tok), BF16),
        pltpu.VMEM((2, 2, HEADS // 2, tok), BF16),
        pltpu.VMEM((ndp, HALF + 2, 8, MIX), F32),
        pltpu.VMEM((2, HALF + 1, 8, MIX), F32),
        pltpu.VMEM((GROUPS, tok, WIDE), BF16),
        pltpu.VMEM((8, 128), F32),
        pltpu.VMEM((8, 128), F32),
        pltpu.SemaphoreType.DMA((2,)),
        pltpu.SemaphoreType.DMA((2,)),
    ]
    one = pltpu.SemaphoreType.DMA
    scratch += [one, one, one((5,)), one, one((6,)), one, one, one, one((2,)), one]
    scratch += [pltpu.SemaphoreType.REGULAR] * 4
    turned = jnp.swapaxes(step_input, 2, 3)
    shapes = [
        (gate_input.shape, BF16),
        (conv_input.shape, BF16),
        (gate_input.shape, BF16),
        (turned.shape, BF16),
        (conv_weight.shape, F32),
        (conv_bias.shape, F32),
        (step_bias.shape, F32),
        (decay_log.shape, F32),
        (skip_gain.shape, F32),
        (norm_gain.shape, F32),
    ]
    inputs = [
        pltpu.with_memory_space_constraint(a, pltpu.HBM)
        for a in (
            conv_input, gate_input, turned, cotangent, conv_weight,
            conv_bias, step_bias, decay_log, skip_gain, norm_gain,
        )
    ]
    sent = pl.pallas_call(
        pair_kernel,
        name="mixer_tick",
        in_specs=[hbm] * 10,
        out_specs=[vmem] * 3,
        out_shape=[
            pltpu.VMEM((tok, 7 * INNER + tok), BF16),
            pltpu.VMEM((8, conv_bias.shape[1]), F32),
            pltpu.VMEM((3,) + step_bias.shape, F32),
        ],
        scratch_shapes=scratch,
        compiler_params=pltpu.CompilerParams(
            collective_id=0, has_side_effects=True, vmem_limit_bytes=24 * 1024 * 1024
        ),
    )(*inputs)
    done = pl.pallas_call(
        finish_kernel,
        name="mixer_finish",
        in_specs=[vmem] * 3,
        out_specs=[hbm] * 10,
        out_shape=[jax.ShapeDtypeStruct(shape, kind) for shape, kind in shapes],
        scratch_shapes=[pltpu.SemaphoreType.DMA((10,))],
        compiler_params=pltpu.CompilerParams(vmem_limit_bytes=1024 * 1024),
    )(*sent)
    return tuple(done[:3]) + (jnp.swapaxes(done[3], 2, 3),) + tuple(done[4:])


def solution(mesh):
    in_specs = (
        P("section", "dp", "ctx", None),
        P("section", "dp", "ctx", None),
        P("section", "dp", "ctx", None),
        P("section", "dp", "ctx", None),
        P("section", None, None),
        P("section", None),
        P("section", None),
        P("section", None),
        P("section", None),
        P("section", None),
    )
    out_specs = (
        P("section", "dp", "ctx", None),
        P("section", "dp", "ctx", None),
        P("section", "dp", "ctx", None),
        P("section", "dp", "ctx", None),
        P("section", None, None),
        P("section", None),
        P("section", None),
        P("section", None),
        P("section", None),
        P("section", None),
    )
    body = paired if (mesh.shape["ctx"], mesh.shape["section"]) == (2, 4) else shards
    return jax.shard_map(body, mesh=mesh, in_specs=in_specs, out_specs=out_specs, check_vma=False)
```
